32 devices in a mesh: agent: 4 (over y, x), dp: 8 (over z, core).
Axes of the slice: x: 2, y: 2, z: 4, core: 2. Of those that a mesh axis runs over, the one named last changes fastest.
Arguments:
- learn_obs: bfloat16 [4, 256, 16, 3456], P('agent', 'dp'), may hold values from -6 to 6
- own_obs: bfloat16 [4, 256, 3456], P('agent', 'dp'), may hold values from -6 to 6
- opp_obs: bfloat16 [4, 256, 3456], P('agent', 'dp'), may hold values from -6 to 6
- opponent: int32 [4, 256, 1], P('agent', 'dp'), may hold values from 0 to 3; in each aligned block of 32 rows (0 to 31, 32 to 63, ..., all dimensions but the last counted through in order) at most 32 rows name the same one
- actions: int32 [4, 256, 16], P('agent', 'dp'), may hold values from 0 to 17
- done: int32 [4, 256, 16], P('agent', 'dp'), may hold values 0 or 1
- rewards: float32 [4, 256, 16], P('agent', 'dp'), may hold values from -6 to 6
- behaviour: float32 [4, 256, 16], P('agent', 'dp'), may hold values from -4.5 to -1.5
- core_master: float32 [4, 256, 3712], P('agent', 'dp'), may hold values from -0.109375 to 0.109375
- core_mom: float32 [4, 256, 3712], P('agent', 'dp'), may hold values from -6 to 6
- core_vel: float32 [4, 256, 3712], P('agent', 'dp'), may hold values from 0.1 to 1
- head_master: float32 [4, 19, 256], P('agent'), may hold values from -0.375 to 0.375
- head_mom: float32 [4, 19, 256], P('agent'), may hold values from -6 to 6
- head_vel: float32 [4, 19, 256], P('agent'), may hold values from 0.1 to 1
- rates: float32 [4], P('agent'), may hold values from 0.01 to 0.1
Outputs:
- own_logits: float32 [4, 256, 18], P('agent', 'dp')
- opp_logits: bfloat16 [4, 256, 18], P('agent', 'dp')
- new_core: float32 [4, 256, 3712], P('agent', 'dp')
- new_core_mom: float32 [4, 256, 3712], P('agent', 'dp')
- new_core_vel: float32 [4, 256, 3712], P('agent', 'dp')
- new_head: float32 [4, 19, 256], P('agent')
- new_head_mom: float32 [4, 19, 256], P('agent')
- new_head_vel: float32 [4, 19, 256], P('agent')
The draws below stay inside these ranges and needn't reach their ends.
Inputs may be any that keep to these rules, and one draw needn't show every extreme that they name: Among the 32 environments of one device (aligned blocks of the environment dimension), at most 32 face the same opponent agent, and some device reaches 32 in every draw.
All inputs are finite; a program needn't handle non-finite values. No bound on the sum of `done` on one device may be relied on, other than what follows from the above.
Results may differ from the reference program's by a relative error of at most 0.023.
Values may be sent and summed in bfloat16 or wider, within the bound.
No kernel may reach another device: no remote copies, remote signals or barrier semaphores. Data moves between devices by JAX's collectives and lax.ppermute only.
A program may use at most 64 MiB of HBM per device.

```python
import math
import jax
import jax.numpy as jnp
import numpy as np
from jax import lax

FEAT = 3456
HID = 256
ACTIONS = 18
ENVS_DEV = 32
UNROLL = 16
AGENTS = 4
ENVS = 256
MOST = 32
HEADS = 19


def touch_ends(array, key, least, top_value):
    shape = array.shape
    index_at = [jax.random.randint(jax.random.fold_in(key, axis), (), 0, shape[axis]) for axis in range(len(shape))]
    array = array.at[tuple(index_at)].set(least)
    longest = shape.index(max(shape))
    index_at[longest] = (index_at[longest] + 1) % shape[longest]
    return array.at[tuple(index_at)].set(top_value)


def block_levels(key, dims, cuts, low, top_value):
    loudness, own = 1.0, jax.random.fold_in(key, 6)
    for dim, parts in cuts:
        steps = jnp.exp(jax.random.uniform(jax.random.fold_in(own, dim), (parts,), jnp.float32, low / len(cuts), top_value / len(cuts)))
        loudness = loudness * jnp.repeat(steps, dims[dim] // parts).reshape([-1 if axis == dim else 1 for axis in range(len(dims))])
    return loudness


def assign_block(key, own, number, rows, amount, top, reach, slope):
    order = jax.random.permutation(key, amount)
    packed, common = shares(amount, rows * top, reach, slope, True), shares(amount, rows * top, reach, slope, False)
    places = jnp.arange(amount)

    def named(tallies, offset_by):
        used = int((tallies > 0).sum())
        fixed = max(1, used // 4)
        shifted = fixed + (places - fixed + offset_by * (used - fixed)) % max(1, amount - fixed)
        return jnp.zeros((amount,), jnp.int32).at[order[jnp.where(places < fixed, places, shifted)]].set(jnp.asarray(tallies, jnp.int32))

    tallies = jnp.where(number % 4 == 0, named(packed, number // 4), named(common, number - number // 4 - 1))
    mixed = jax.random.permutation(jax.random.fold_in(own, 3), amount)
    giver, taker = mixed[0:amount // 2 * 2:2], mixed[1:amount // 2 * 2:2]
    margin = jnp.minimum(tallies[giver] - 1, reach - tallies[taker]) // 2
    margin = jnp.where((giver == order[0]) | (taker == order[0]) | (tallies[taker] == 0), 0, jnp.maximum(margin, 0))
    shifted = jax.random.randint(jax.random.fold_in(own, 4), (amount // 2,), 0, 1 << 20) % (margin + 1)
    tallies = tallies.at[giver].add(-shifted).at[taker].add(shifted)
    items = jnp.searchsorted(jnp.cumsum(tallies), jnp.arange(rows * top), side="right").astype(jnp.int32)
    table = items.reshape(top, rows).T
    table = table[jax.random.permutation(jax.random.fold_in(own, 1), rows)]
    offset_by = jax.random.randint(jax.random.fold_in(own, 2), (rows, 1), 0, top)
    return jnp.take_along_axis(table, (jnp.arange(top)[None, :] + offset_by) % top, axis=1)


def shares(number_of, total, most, skew, full):
    weights = [(1 << 20) // math.isqrt(rank ** skew) + 1 for rank in range(1, number_of + 1)]
    largest = most if full else min(most, max(-(-total // number_of), total * weights[0] // sum(weights)))
    least = 1 if total - largest >= number_of - 1 else 0
    holding, rest = [largest] + [least] * (number_of - 1), total - largest - least * (number_of - 1)
    while rest > 0:
        free = [i for i in range(1, number_of) if holding[i] < largest] or [i for i in range(1, number_of) if holding[i] < most]
        whole, remaining = sum([weights[i] for i in free]), rest
        for i in free:
            more = min(most - holding[i], max(1, remaining * weights[i] // whole), rest)
            holding[i] = holding[i] + more
            rest = rest - more
    return np.array(holding)


def gaussian(own_key, dims, scale, most, cuts=(), kind=jnp.bfloat16):
    loudness = block_levels(own_key, dims, cuts, -0.22, 0.18) if cuts else 1.0
    values = jax.random.normal(own_key, dims, jnp.float32) * scale * loudness
    return jnp.minimum(jnp.maximum(values, -most), most).astype(kind)


def setup_inputs(seed: int = 0) -> dict:
    keys = jax.random.split(jax.random.key(seed), 16)
    learn_obs = gaussian(keys[0], (AGENTS, ENVS, UNROLL, FEAT), 1.0, 6.0, ((0, 4), (1, 8)))
    own_obs = gaussian(keys[1], (AGENTS, ENVS, FEAT), 1.0, 6.0, ((0, 4), (1, 8)))
    opp_obs = gaussian(keys[2], (AGENTS, ENVS, FEAT), 1.0, 6.0, ((0, 4), (1, 8)))
    opponent_keys = jax.random.split(jax.random.fold_in(keys[3], 1), AGENTS * ENVS // ENVS_DEV)
    opponent_turns = jax.random.permutation(jax.random.fold_in(keys[3], 3), AGENTS * ENVS // ENVS_DEV)
    opponent = jax.vmap(lambda own, number: assign_block(jax.random.fold_in(keys[3], 2), own, number, ENVS_DEV, AGENTS, 1, MOST, 2))(opponent_keys, opponent_turns).reshape((AGENTS, ENVS, 1))
    actions = touch_ends(jax.random.randint(keys[4], (AGENTS, ENVS, UNROLL), 0, ACTIONS), jax.random.fold_in(keys[4], 1), 0, ACTIONS - 1).astype(jnp.int32)
    done = touch_ends((jax.random.randint(keys[5], (AGENTS, ENVS, UNROLL), 0, 8) < 1).astype(jnp.int32), jax.random.fold_in(keys[5], 1), 0, 1)
    rewards = gaussian(keys[6], (AGENTS, ENVS, UNROLL), 1.0, 6.0, ((0, 4), (1, 8)), jnp.float32)
    behaviour = jnp.clip(-4.5 + 3.0 * jax.random.uniform(keys[7], (AGENTS, ENVS, UNROLL), jnp.float32) ** block_levels(keys[7], (AGENTS, ENVS, UNROLL), ((0, 4), (1, 8)), -0.2, 0.2), -4.5, -1.5)
    core_master = gaussian(keys[8], (AGENTS, HID, FEAT + HID), FEAT ** -0.5, 0.109375, ((0, 4), (1, 8)), jnp.float32)
    core_mom = gaussian(keys[9], (AGENTS, HID, FEAT + HID), 0.5, 6.0, ((0, 4), (1, 8)), jnp.float32)
    core_vel = jnp.clip(jnp.exp(math.log(1.0) - 2.3025851 * jax.random.uniform(keys[10], (AGENTS, HID, FEAT + HID), jnp.float32) ** block_levels(keys[10], (AGENTS, HID, FEAT + HID), ((0, 4), (1, 8)), -0.2, 0.2)), 0.1, 1.0)
    head_master = gaussian(keys[11], (AGENTS, HEADS, HID), HID ** -0.5, 0.375, ((0, 4),), jnp.float32)
    head_mom = gaussian(keys[12], (AGENTS, HEADS, HID), 0.5, 6.0, ((0, 4),), jnp.float32)
    head_vel = jnp.clip(jnp.exp(math.log(1.0) - 2.3025851 * jax.random.uniform(keys[13], (AGENTS, HEADS, HID), jnp.float32) ** block_levels(keys[13], (AGENTS, HEADS, HID), ((0, 4),), -0.2, 0.2)), 0.1, 1.0)
    rates = jnp.clip(jnp.exp(math.log(0.1) - 2.3025851 * jax.random.uniform(keys[14], (AGENTS,), jnp.float32) ** block_levels(keys[14], (AGENTS,), ((0, 4),), -0.2, 0.2)), 0.01, 0.1)
    return dict(learn_obs=learn_obs, own_obs=own_obs, opp_obs=opp_obs, opponent=opponent, actions=actions, done=done, rewards=rewards, behaviour=behaviour, core_master=core_master, core_mom=core_mom, core_vel=core_vel, head_master=head_master, head_mom=head_mom, head_vel=head_vel, rates=rates)


gamma_rate = 0.99
baseline_cost = 0.5
entropy_cost = 0.05
beta_first = 0.9
beta_second = 0.99
adam_eps = 1e-08

def contract(left, right):
    return lax.dot_general(left, right, (((1,), (1,)), ((), ())), preferred_element_type=jnp.float32)

def contract_rows(left, right):
    return lax.dot_general(left, right, (((0,), (0,)), ((), ())), preferred_element_type=jnp.float32)

def forward(inputs, core_bf, head_bf):
    width = inputs.shape[-1]
    pre_one = contract(inputs, core_bf[:, :width])
    first_act = jax.nn.relu(pre_one)
    first_bf = first_act.astype(jnp.bfloat16)
    pre_two = contract(first_bf, core_bf[:, width:])
    second_act = jax.nn.relu(pre_two) + first_act
    second_bf = second_act.astype(jnp.bfloat16)
    network_outputs = contract(second_bf, head_bf)
    return (network_outputs, pre_one, first_bf, pre_two, second_bf)

def importance_trace_gradients(network_outputs, bootstrap_value, actions, done, rewards, behaviour, scale_factor):
    action_count = network_outputs.shape[-1] - 1
    logits = network_outputs[..., :action_count]
    values = network_outputs[..., action_count]
    totals = lax.optimization_barrier(jnp.sum(jnp.exp(logits), -1))
    logp = logits - jnp.log(totals)[..., None]
    probs = jnp.exp(logp)
    chosen = (actions[..., None] == jnp.arange(action_count, dtype=jnp.int32)).astype(jnp.float32)
    logp_act = lax.optimization_barrier(jnp.sum(logp * chosen, -1))
    ratio = jnp.minimum(1.0, jnp.exp(logp_act - behaviour))
    discount = gamma_rate * (1.0 - done.astype(jnp.float32))
    next_values = jnp.concatenate([values[:, 1:], bootstrap_value[:, None]], 1)
    deltas = ratio * (rewards + discount * next_values - values)

    def backstep(carry, item):
        delta, factor = item
        carry = delta + factor * carry
        return (carry, carry)
    start = jnp.zeros((values.shape[0],), jnp.float32)
    final_carry, corrections = lax.scan(backstep, start, (deltas.T, (discount * ratio).T), reverse=True)
    targets = values + corrections.T
    next_targets = jnp.concatenate([targets[:, 1:], bootstrap_value[:, None]], 1)
    advantage = ratio * (rewards + discount * next_targets - values)
    entropy = -lax.optimization_barrier(jnp.sum(probs * logp, -1))
    grad_logits = scale_factor * (-advantage[..., None] * (chosen - probs) + entropy_cost * probs * (logp + entropy[..., None]))
    grad_value = scale_factor * (-baseline_cost * (targets - values))
    return jnp.concatenate([grad_logits, grad_value[..., None]], -1)

def backward(core_bf, head_bf, output_gradient, pre_one, pre_two, second_bf, width):
    grad_bf = output_gradient.astype(jnp.bfloat16)
    head_grad = contract_rows(grad_bf, second_bf)
    grad_second = jnp.dot(grad_bf, head_bf, preferred_element_type=jnp.float32)
    grad_pre_two = jnp.where(pre_two > 0, grad_second, 0.0).astype(jnp.bfloat16)
    grad_first = grad_second + jnp.dot(grad_pre_two, core_bf[:, width:], preferred_element_type=jnp.float32)
    grad_pre_one = jnp.where(pre_one > 0, grad_first, 0.0).astype(jnp.bfloat16)
    return (head_grad, grad_pre_one, grad_pre_two)

def adam_step(master, moment, second, grad, rate):
    moment = beta_first * moment + (1.0 - beta_first) * grad
    second = beta_second * second + (1.0 - beta_second) * grad * grad
    master = master - rate * moment / (jnp.sqrt(second) + adam_eps)
    return (master, moment, second)

def reference(learn_obs, own_obs, opp_obs, opponent, actions, done, rewards, behaviour, core_master, core_mom, core_vel, head_master, head_mom, head_vel, rates):
    agent_count, environment_total, rollout_length, width = learn_obs.shape
    action_count = head_master.shape[1] - 1
    scale_factor = 1.0 / rollout_length
    opp_flat = opp_obs.reshape(agent_count * environment_total, width)
    opp_ids = opponent.reshape(-1).astype(jnp.int32)

    def per_agent(slot_index):
        core_bf = core_master[slot_index].astype(jnp.bfloat16)
        head_bf = head_master[slot_index].astype(jnp.bfloat16)
        own_out = forward(own_obs[slot_index], core_bf, head_bf)[0]
        bootstrap_value = own_out[:, action_count]
        opp_out = forward(opp_flat, core_bf, head_bf)[0][:, :action_count].astype(jnp.bfloat16)
        rows = learn_obs[slot_index].reshape(environment_total * rollout_length, width)
        network_outputs, pre_one, first_bf, pre_two, second_bf = forward(rows, core_bf, head_bf)
        output_gradient = importance_trace_gradients(network_outputs.reshape(environment_total, rollout_length, action_count + 1), bootstrap_value, actions[slot_index], done[slot_index], rewards[slot_index], behaviour[slot_index], scale_factor)
        output_gradient = output_gradient.reshape(environment_total * rollout_length, action_count + 1)
        head_grad, grad_pre_one, grad_pre_two = backward(core_bf, head_bf, output_gradient, pre_one, pre_two, second_bf, width)
        core_grad = jnp.concatenate([contract_rows(grad_pre_one, rows), contract_rows(grad_pre_two, first_bf)], 1)
        rate = rates[slot_index]
        new_core, new_core_mom, new_core_vel = adam_step(core_master[slot_index], core_mom[slot_index], core_vel[slot_index], core_grad, rate)
        new_head, new_head_mom, new_head_vel = adam_step(head_master[slot_index], head_mom[slot_index], head_vel[slot_index], head_grad, rate)
        return (own_out[:, :action_count], opp_out, new_core, new_core_mom, new_core_vel, new_head, new_head_mom, new_head_vel)
    results = lax.map(per_agent, jnp.arange(agent_count, dtype=jnp.int32))
    own_logits = results[0]
    every_opp = results[1]
    picked = every_opp[opp_ids, jnp.arange(agent_count * environment_total, dtype=jnp.int32)]
    opp_logits = picked.reshape(agent_count, environment_total, action_count)
    return (own_logits, opp_logits, results[2], results[3], results[4], results[5], results[6], results[7])
```

```python
import functools

import jax
import jax.numpy as jnp
from jax import lax
from jax.experimental import pallas as pl
from jax.experimental.pallas import tpu as pltpu
from jax.sharding import PartitionSpec as P

gamma_rate = 0.99
baseline_cost = 0.5
entropy_cost = 0.05
beta_first = 0.9
beta_second = 0.99
adam_eps = 1e-08

CORES = 2
SUBLANES = 32

LINE = 4
GATHER_FAR = ((0, 2), (3, 1), (1, 0), (2, 3))
GATHER_NEAR = ((0, 1), (3, 2), (1, 3), (2, 0))
GATHER_MID = ((1, 2), (2, 1))
GATHER_FORWARD = ((2, 3), (1, 0))
FAR_FROM = (1, 3, 0, 2)
NEAR_FROM = (2, 0, 3, 1)
LAST_FROM = (3, 2, 1, 0)
SELF_FROM = (0, 1, 2, 3)
ROLES = (LAST_FROM, NEAR_FROM, FAR_FROM, SELF_FROM)
SCATTER_FORWARD = ((3, 2), (0, 1))
SCATTER_NEAR = tuple((b, a) for a, b in GATHER_NEAR)
SCATTER_MID = ((1, 2), (2, 1))
SCATTER_FAR = tuple((b, a) for a, b in GATHER_FAR)


def dot(left, right, dims, precision=None):
    return lax.dot_general(
        left, right, (dims, ((), ())), preferred_element_type=jnp.float32, precision=precision
    )


NN = ((1,), (0,))
NT = ((1,), (1,))


def table(values, index):
    result = jnp.int32(values[0])
    for place, value in enumerate(values[1:], 1):
        result = jnp.where(index == place, jnp.int32(value), result)
    return result


def trace_gradients(out, boot, aux, action_count, length, scale):
    rows, lanes = out.shape
    row = lax.broadcasted_iota(jnp.int32, (rows, lanes), 0)
    step = lax.rem(lax.broadcasted_iota(jnp.int32, (1, lanes), 1), length)
    last = step == length - 1
    policy = row < action_count
    actions, done, rewards, behaviour = (aux[i : i + 1] for i in range(4))
    values = out[action_count : action_count + 1]
    totals = jnp.sum(jnp.where(policy, jnp.exp(out), 0.0), 0, keepdims=True)
    logp = out - jnp.log(totals)
    probs = jnp.where(policy, jnp.exp(logp), 0.0)
    chosen = (row == actions.astype(jnp.int32)).astype(jnp.float32)
    picked = jnp.sum(logp * chosen, 0, keepdims=True)
    ratio = jnp.minimum(1.0, jnp.exp(picked - behaviour))
    discount = gamma_rate * (1.0 - done)
    following = lambda x, end: jnp.where(last, end, pltpu.roll(x, lanes - 1, 1))
    delta = ratio * (rewards + discount * following(values, boot) - values)
    factor = jnp.where(last, 0.0, discount * ratio)
    reach = 1
    while reach < length:
        delta = delta + factor * pltpu.roll(delta, lanes - reach, 1)
        factor = factor * pltpu.roll(factor, lanes - reach, 1)
        reach *= 2
    targets = values + delta
    advantage = ratio * (rewards + discount * following(targets, boot) - values)
    entropy = -jnp.sum(jnp.where(policy, probs * logp, 0.0), 0, keepdims=True)
    grad_logits = scale * (
        -advantage * (chosen - probs) + entropy_cost * probs * (logp + entropy)
    )
    grad_value = scale * (-baseline_cost * (targets - values))
    return jnp.where(policy, grad_logits, jnp.where(row == action_count, grad_value, 0.0))


def learner_kernel(cfg, *refs):
    frames, pieces, heads = cfg["frames"], cfg["pieces"], cfg["heads"]
    x_refs, refs = refs[: len(frames)], refs[len(frames) :]
    w_refs, refs = refs[: len(pieces)], refs[len(pieces) :]
    aux_ref, head_ref, head_t_ref, grad_ref, ghead_ref, other_ref, xs, ws, gp, gs, sx, sw, sg = refs
    learn, width, units, length = cfg["learn"], cfg["width"], cfg["units"], cfg["length"]
    envs = learn // length
    place = lax.axis_index("dp")
    core, chip = lax.rem(place, CORES), lax.div(place, CORES)

    def frame_copy(i):
        offset, count = frames[i]
        return pltpu.make_async_copy(x_refs[i], xs.at[pl.ds(offset, count)], sx.at[i])

    def piece_copy(i):
        rows, source, same, chips = pieces[i]
        if source is None:
            return pltpu.make_async_copy(w_refs[i], ws, sw.at[i]), None
        owner = core if same else 1 - core
        start = pl.multiple_of((table(source, chip) * CORES + owner) * rows, rows)
        live = None
        if chips is not None:
            live = functools.reduce(jnp.logical_or, [chip == one for one in chips])
        return pltpu.make_async_copy(w_refs[i], ws.at[pl.ds(start, rows)], sw.at[i]), live

    def each_piece(act):
        for i in range(len(pieces)):
            copy, live = piece_copy(i)
            if live is None:
                act(copy)
            else:
                pl.when(live)(functools.partial(act, copy))

    for i in range(len(frames)):
        frame_copy(i).start()
    each_piece(lambda copy: copy.start())
    for i in range(len(frames)):
        frame_copy(i).wait()
    each_piece(lambda copy: copy.wait())

    head = head_ref[...]
    second = ws[:, width:]
    pre_one = dot(ws[:, :width], xs[...], NT)
    first = jnp.maximum(pre_one, 0.0)
    first_bf = first.astype(jnp.bfloat16)
    pre_two = dot(second, first_bf, NN)
    second_bf = (jnp.maximum(pre_two, 0.0) + first).astype(jnp.bfloat16)
    out = dot(head, second_bf, NN)
    other_ref[...] = out[:, learn:]
    values = out[:, learn : learn + envs]
    spread = lax.broadcasted_iota(jnp.int32, (envs, learn), 1) // length
    spread = (spread == lax.broadcasted_iota(jnp.int32, (envs, learn), 0)).astype(jnp.float32)
    boot = dot(values, spread, NN, lax.Precision.HIGHEST)[heads - 1 : heads]
    grad = trace_gradients(
        out[:, :learn], boot, aux_ref[...], heads - 1, length, 1.0 / length
    ).astype(jnp.bfloat16)
    ghead_ref[...] = dot(grad, second_bf[:, :learn], NT)
    grad_second = dot(head_t_ref[...], grad, NN)
    grad_two = jnp.where(pre_two[:, :learn] > 0, grad_second, 0.0).astype(jnp.bfloat16)
    grad_first = grad_second + dot(second.T, grad_two, NN)
    grad_one = jnp.where(pre_one[:, :learn] > 0, grad_first, 0.0).astype(jnp.bfloat16)

    roles = cfg["roles"]
    if roles is None:
        grad_one_s, grad_two_s = grad_one, grad_two
    else:
        gp[:, :learn] = grad_one
        gp[:, learn:] = grad_two
        rows = units // (len(roles) * CORES)
        order = []
        for same in (False, True):
            owner = core if same else 1 - core
            for role in roles:
                start = pl.multiple_of((table(role, chip) * CORES + owner) * rows, rows)
                order.append(gp[pl.ds(start, rows), :])
        ordered = jnp.concatenate(order, 0)
        grad_one_s, grad_two_s = ordered[:, :learn], ordered[:, learn:]

    def out_copy(i, start, count):
        part = pl.ds(start, count)
        return pltpu.make_async_copy(gs.at[:, part], grad_ref.at[:, part], sg.at[i])

    chunk = cfg["chunk"]
    starts = list(range(0, width, chunk))
    for i, start in enumerate(starts):
        gs[:, start : start + chunk] = dot(
            grad_one_s, xs[:learn, start : start + chunk], NN
        ).astype(jnp.bfloat16)
        out_copy(i, start, chunk).start()
    gs[:, width:] = dot(grad_two_s, first_bf[:, :learn], NT).astype(jnp.bfloat16)
    out_copy(len(starts), width, units).start()
    for i, start in enumerate(starts):
        out_copy(i, start, chunk).wait()
    out_copy(len(starts), width, units).wait()


def column_chunk(width):
    return max(c for c in range(128, 1153, 128) if width % c == 0)


def learner(frame_list, piece_list, aux, head, head_t, cfg):
    total = sum(f.shape[0] for f in frame_list)
    units, width = cfg["units"], cfg["width"]
    padded = head.shape[0]
    offsets, at = [], 0
    for f in frame_list:
        offsets.append((at, f.shape[0]))
        at += f.shape[0]
    learn = frame_list[0].shape[0]
    chunk = column_chunk(width)
    cfg = dict(cfg, frames=offsets, learn=learn, chunk=chunk)
    copies = width // chunk + 1
    anywhere = pl.BlockSpec(memory_space=pl.ANY)
    local = pl.BlockSpec(memory_space=pltpu.VMEM)
    return pl.pallas_call(
        functools.partial(learner_kernel, cfg),
        out_shape=(
            jax.ShapeDtypeStruct((units, width + units), jnp.bfloat16),
            jax.ShapeDtypeStruct((padded, units), jnp.float32),
            jax.ShapeDtypeStruct((padded, total - learn), jnp.float32),
        ),
        in_specs=[anywhere] * (len(frame_list) + len(piece_list)) + [local] * 3,
        out_specs=(anywhere, local, local),
        scratch_shapes=[
            pltpu.VMEM((total, width), jnp.bfloat16),
            pltpu.VMEM((units, width + units), jnp.bfloat16),
            pltpu.VMEM((units, 2 * learn), jnp.bfloat16),
            pltpu.VMEM((units, width + units), jnp.bfloat16),
            pltpu.SemaphoreType.DMA((len(frame_list),)),
            pltpu.SemaphoreType.DMA((len(piece_list),)),
            pltpu.SemaphoreType.DMA((copies,)),
        ],
        compiler_params=pltpu.CompilerParams(vmem_limit_bytes=40 << 20),
        cost_estimate=pl.CostEstimate(
            flops=4 * units * total * width, bytes_accessed=4 * total * width, transcendentals=0
        ),
        name="learner",
    )(*frame_list, *piece_list, aux, head, head_t)


def adam_step(master, moment, second, grad, rate):
    moment = beta_first * moment + (1.0 - beta_first) * grad
    second = beta_second * second + (1.0 - beta_second) * grad * grad
    master = master - rate * moment / (jnp.sqrt(second) + adam_eps)
    return (master, moment, second)


def per_device(
    learn_obs,
    own_obs,
    opp_obs,
    opponent,
    actions,
    done,
    rewards,
    behaviour,
    core_master,
    core_mom,
    core_vel,
    head_master,
    head_mom,
    head_vel,
    rates,
):
    envs, length, width = learn_obs.shape[1:]
    heads, units = head_master.shape[1:]
    action_count = heads - 1
    agents, members = lax.axis_size("agent"), lax.axis_size("dp")
    rows = core_master.shape[1]
    chips = members // CORES
    line = chips == LINE and members == LINE * CORES and units == members * rows
    wide = jnp.float32

    def along(x, pairs):
        return lax.ppermute(
            x, "dp", [(a * CORES + c, b * CORES + c) for a, b in pairs for c in range(CORES)]
        )

    def sibling(x):
        return lax.ppermute(x, "dp", [(i, i ^ 1) for i in range(members)])

    def shift(x, by):
        return lax.ppermute(x, "agent", [(i, (i + by) % agents) for i in range(agents)])

    mine = core_master[0].astype(jnp.bfloat16)
    if line:
        far = along(mine, GATHER_FAR)
        near = along(mine, GATHER_NEAR)
        mid = along(mine, GATHER_MID)
        forward = along(far, GATHER_FORWARD)
        got = ((mine, SELF_FROM, None), (far, FAR_FROM, None), (near, NEAR_FROM, None),
               (mid, LAST_FROM, (1, 2)), (forward, LAST_FROM, (0, 3)))
        piece_list = [g[0] for g in got] + [sibling(g[0]) for g in got]
        pieces = [(rows, g[1], True, g[2]) for g in got] + [(rows, g[1], False, g[2]) for g in got]
        roles = ROLES
    else:
        piece_list = [lax.all_gather(mine, "dp", axis=0, tiled=True)]
        pieces = [(units, None, True, None)]
        roles = None

    frames = [opp_obs[0]] + [shift(opp_obs[0], by) for by in range(1, agents)]

    aux = jnp.stack(
        [actions[0].astype(wide), done[0].astype(wide), rewards[0], behaviour[0]]
    ).reshape(4, envs * length)
    padded = -(-heads // SUBLANES) * SUBLANES
    head = jnp.pad(head_master[0].astype(jnp.bfloat16), ((0, padded - heads), (0, 0)))
    cfg = dict(pieces=pieces, heads=heads, width=width, units=units, length=length, roles=roles)
    grads, ghead, other = learner(
        [learn_obs[0].reshape(envs * length, width), own_obs[0]] + frames,
        piece_list, aux, head, head.T, cfg,
    )

    own_logits = other[:action_count, :envs].T
    played = other[:action_count, envs:].astype(jnp.bfloat16).reshape(action_count, agents, envs)
    me = lax.axis_index("agent")
    ids = opponent[0, :, 0][None]
    opp_logits = jnp.zeros((action_count, envs), jnp.bfloat16)
    for by in range(agents):
        answer = played[:, by]
        if by:
            answer = shift(answer, agents - by)
        opp_logits = jnp.where(ids == (me + by) % agents, answer, opp_logits)

    rate = rates[0]
    if line:
        grads = grads.reshape(CORES, len(roles), rows, width + units)
        keep = [grads[1, i].astype(wide) for i in range(len(roles))]
        came = [sibling(grads[0, i]).astype(wide) for i in range(len(roles))]
        last, toward = [(k + c).astype(jnp.bfloat16) for k, c in zip(keep[:2], came[:2])]
        through = along(last, SCATTER_FORWARD).astype(wide)
        part_near = along(toward, SCATTER_NEAR).astype(wide)
        part_mid = along(last, SCATTER_MID).astype(wide)
        part_far = along((keep[2] + came[2] + through).astype(jnp.bfloat16), SCATTER_FAR).astype(wide)
        core_grad = keep[3] + came[3] + part_near + part_mid + part_far
        head_total = ghead[:heads]
        head_total = head_total + sibling(head_total)
        head_total = head_total + along(head_total, ((0, 1), (1, 0), (2, 3), (3, 2)))
        head_total = head_total + along(head_total, ((0, 2), (2, 0), (1, 3), (3, 1)))
    else:
        core_grad = lax.psum_scatter(grads, "dp", scatter_dimension=0, tiled=True).astype(wide)
        head_total = lax.psum(ghead[:heads], "dp")
    new_core, new_core_mom, new_core_vel = adam_step(
        core_master[0], core_mom[0], core_vel[0], core_grad, rate
    )
    new_head, new_head_mom, new_head_vel = adam_step(
        head_master[0], head_mom[0], head_vel[0], head_total, rate
    )
    return (
        own_logits[None],
        opp_logits.T[None],
        new_core[None],
        new_core_mom[None],
        new_core_vel[None],
        new_head[None],
        new_head_mom[None],
        new_head_vel[None],
    )


def solution(mesh):
    sharded, whole = P("agent", "dp", None), P("agent", None, None)
    return jax.shard_map(
        per_device,
        mesh=mesh,
        in_specs=(P("agent", "dp", None, None),) + (sharded,) * 10 + (whole,) * 3 + (P("agent"),),
        out_specs=(sharded,) * 5 + (whole,) * 3,
        check_vma=False,
    )
```

```python
import functools

import jax
import jax.numpy as jnp
from jax import lax
from jax.experimental import pallas as pl
from jax.experimental.pallas import tpu as pltpu
from jax.sharding import PartitionSpec as P


gamma_rate = 0.99
baseline_cost = 0.5
entropy_cost = 0.05
beta_first = 0.9
beta_second = 0.99
adam_eps = 1e-08

CORES = 2
SUBLANES = 32

LINE = 4
GATHER_FAR = ((0, 2), (3, 1), (1, 0), (2, 3))
GATHER_NEAR = ((0, 1), (3, 2), (1, 3), (2, 0))
GATHER_MID = ((1, 2), (2, 1))
GATHER_FORWARD = ((2, 3), (1, 0))
FAR_FROM = (1, 3, 0, 2)
NEAR_FROM = (2, 0, 3, 1)
LAST_FROM = (3, 2, 1, 0)
SELF_FROM = (0, 1, 2, 3)
ROLES = (LAST_FROM, NEAR_FROM, FAR_FROM, SELF_FROM)
SCATTER_FORWARD = ((3, 2), (0, 1))
SCATTER_NEAR = tuple((b, a) for a, b in GATHER_NEAR)
SCATTER_MID = ((1, 2), (2, 1))
SCATTER_FAR = tuple((b, a) for a, b in GATHER_FAR)


def dot(left, right, dims, precision=None):
    return lax.dot_general(
        left, right, (dims, ((), ())), preferred_element_type=jnp.float32, precision=precision
    )


NN = ((1,), (0,))
NT = ((1,), (1,))


def table(values, index):
    result = jnp.int32(values[0])
    for place, value in enumerate(values[1:], 1):
        result = jnp.where(index == place, jnp.int32(value), result)
    return result


def trace_gradients(out, boot, aux, action_count, length, scale):
    rows, lanes = out.shape
    row = lax.broadcasted_iota(jnp.int32, (rows, lanes), 0)
    step = lax.rem(lax.broadcasted_iota(jnp.int32, (1, lanes), 1), length)
    last = step == length - 1
    policy = row < action_count
    actions, done, rewards, behaviour = (aux[i : i + 1] for i in range(4))
    values = out[action_count : action_count + 1]
    totals = jnp.sum(jnp.where(policy, jnp.exp(out), 0.0), 0, keepdims=True)
    logp = out - jnp.log(totals)
    probs = jnp.where(policy, jnp.exp(logp), 0.0)
    chosen = (row == actions.astype(jnp.int32)).astype(jnp.float32)
    picked = jnp.sum(logp * chosen, 0, keepdims=True)
    ratio = jnp.minimum(1.0, jnp.exp(picked - behaviour))
    discount = gamma_rate * (1.0 - done)
    following = lambda x, end: jnp.where(last, end, pltpu.roll(x, lanes - 1, 1))
    delta = ratio * (rewards + discount * following(values, boot) - values)
    factor = jnp.where(last, 0.0, discount * ratio)
    reach = 1
    while reach < length:
        delta = delta + factor * pltpu.roll(delta, lanes - reach, 1)
        factor = factor * pltpu.roll(factor, lanes - reach, 1)
        reach *= 2
    targets = values + delta
    advantage = ratio * (rewards + discount * following(targets, boot) - values)
    entropy = -jnp.sum(jnp.where(policy, probs * logp, 0.0), 0, keepdims=True)
    grad_logits = scale * (
        -advantage * (chosen - probs) + entropy_cost * probs * (logp + entropy)
    )
    grad_value = scale * (-baseline_cost * (targets - values))
    return jnp.where(policy, grad_logits, jnp.where(row == action_count, grad_value, 0.0))


ANYWHERE = pl.BlockSpec(memory_space=pl.ANY)
LOCAL = pl.BlockSpec(memory_space=pltpu.VMEM)


def in_hbm(arrays):
    return [pltpu.with_memory_space_constraint(x, pltpu.HBM) for x in arrays]


def stage_kernel(*refs):
    count = (len(refs) - 2) // 1
    sources, staged, sems = refs[:count], refs[count], refs[count + 1]
    copies, at = [], 0
    for i, source in enumerate(sources):
        rows = source.shape[0]
        copies.append(pltpu.make_async_copy(source, staged.at[pl.ds(at, rows)], sems.at[i]))
        at += rows
    for copy in copies:
        copy.start()
    for copy in copies:
        copy.wait()


def stage(arrays):
    rows, width = sum(x.shape[0] for x in arrays), arrays[0].shape[1]
    return pl.pallas_call(
        stage_kernel,
        out_shape=jax.ShapeDtypeStruct((rows, width), arrays[0].dtype),
        in_specs=[ANYWHERE] * len(arrays),
        out_specs=LOCAL,
        scratch_shapes=[pltpu.SemaphoreType.DMA((len(arrays),))],
        compiler_params=pltpu.CompilerParams(vmem_limit_bytes=8 << 20),
        cost_estimate=pl.CostEstimate(
            flops=0, bytes_accessed=4 * rows * width, transcendentals=0
        ),
    )(*in_hbm(arrays))


def forward(frames, weights, head, width):
    pre_one = dot(weights[:, :width], frames, NT)
    first = jnp.maximum(pre_one, 0.0)
    first_bf = first.astype(jnp.bfloat16)
    pre_two = dot(weights[:, width:], first_bf, NN)
    second_bf = (jnp.maximum(pre_two, 0.0) + first).astype(jnp.bfloat16)
    return dot(head, second_bf, NN), pre_one, first_bf, pre_two, second_bf


def learner_kernel(cfg, *refs):
    pieces, heads, roles = cfg["pieces"], cfg["heads"], cfg["roles"]
    xs, refs = refs[0], refs[1:]
    w_refs, refs = refs[: len(pieces)], refs[len(pieces) :]
    aux_ref, head_ref, ws, ghead_ref, own_ref, order_ref, first_ref, refs = *refs[:7], refs[7:]
    lead, (gp, sw) = refs[:-2], refs[-2:]
    learn, width, units, length = cfg["learn"], cfg["width"], cfg["units"], cfg["length"]
    envs = learn // length
    place = lax.axis_index("dp")
    core, chip = lax.rem(place, CORES), lax.div(place, CORES)

    def piece_copy(i):
        rows, source, same, chips = pieces[i]
        if source is None:
            return pltpu.make_async_copy(w_refs[i], ws, sw.at[i]), None
        owner = core if same else 1 - core
        start = pl.multiple_of((table(source, chip) * CORES + owner) * rows, rows)
        live = None
        if chips is not None:
            live = functools.reduce(jnp.logical_or, [chip == one for one in chips])
        return pltpu.make_async_copy(w_refs[i], ws.at[pl.ds(start, rows)], sw.at[i]), live

    def each_piece(act):
        for i in range(len(pieces)):
            copy, live = piece_copy(i)
            if live is None:
                act(copy)
            else:
                pl.when(live)(functools.partial(act, copy))

    each_piece(lambda copy: copy.start())
    each_piece(lambda copy: copy.wait())

    out, pre_one, first_bf, pre_two, second_bf = forward(xs[...], ws[...], head_ref[...], width)
    own_ref[...] = out[: heads - 1, learn:].reshape(heads - 1, 1, envs)
    spread = lax.broadcasted_iota(jnp.int32, (envs, learn), 1) // length
    spread = (spread == lax.broadcasted_iota(jnp.int32, (envs, learn), 0)).astype(jnp.float32)
    boot = dot(out[:, learn:], spread, NN, lax.Precision.HIGHEST)[heads - 1 : heads]
    grad = trace_gradients(
        out[:, :learn], boot, aux_ref[...], heads - 1, length, 1.0 / length
    ).astype(jnp.bfloat16)
    ghead_ref[...] = dot(grad, second_bf[:, :learn], NT)
    grad_second = dot(head_ref[...].T, grad, NN)
    grad_two = jnp.where(pre_two[:, :learn] > 0, grad_second, 0.0).astype(jnp.bfloat16)
    grad_first = grad_second + dot(ws[:, width:].T, grad_two, NN)
    grad_one = jnp.where(pre_one[:, :learn] > 0, grad_first, 0.0).astype(jnp.bfloat16)
    first_ref[...] = first_bf[:, :learn]

    if roles is None:
        order_ref[:, :learn] = grad_one
        order_ref[:, learn:] = grad_two
        return
    gp[:, :learn] = grad_one
    gp[:, learn:] = grad_two
    rows = units // (len(roles) * CORES)
    order = []
    for role in roles:
        for same in (False, True):
            owner = core if same else 1 - core
            start = pl.multiple_of((table(role, chip) * CORES + owner) * rows, rows)
            order.append(gp[pl.ds(start, rows), :])
    order_ref[...] = jnp.concatenate(order[CORES:], 0)
    gradient_rows(jnp.concatenate(order[:CORES], 0), xs, first_ref, lead, learn, width, cfg["chunk"])


def gradient_rows(order, xs, first_ref, outs, learn, width, chunk):
    rows = outs[0].shape[0]

    def put(columns, value):
        value = value.astype(jnp.bfloat16)
        for i, out in enumerate(outs):
            out[:, columns] = value[i * rows : (i + 1) * rows]

    for start in range(0, width, chunk):
        columns = slice(start, start + chunk)
        put(columns, dot(order[:, :learn], xs[:learn, columns], NN))
    put(slice(width, None), dot(order[:, learn:], first_ref[...], NT))


def rest_kernel(cfg, xs, order_ref, first_ref, *outs):
    gradient_rows(order_ref[...], xs, first_ref, outs, cfg["learn"], cfg["width"], cfg["chunk"])


def column_chunk(width):
    return max(c for c in range(128, 1153, 128) if width % c == 0)


def learner(staged, piece_list, aux, head, cfg):
    total, width, units, learn = staged.shape[0], cfg["width"], cfg["units"], cfg["learn"]
    padded = head.shape[0]
    cfg = dict(cfg, chunk=column_chunk(width))
    roles = cfg["roles"]
    block = lambda rows: jax.ShapeDtypeStruct((rows, width + units), jnp.bfloat16)
    if roles is None:
        lead, rest, later = [], [block(units)], units
    else:
        rows = units // (len(roles) * CORES)
        lead, rest = [block(rows)] * CORES, [block(rows)] * (CORES * (len(roles) - 1))
        later = units - CORES * rows
    weights, ghead, own, order, first, *first_outs = pl.pallas_call(
        functools.partial(learner_kernel, cfg),
        out_shape=(
            block(units),
            jax.ShapeDtypeStruct((padded, units), jnp.float32),
            jax.ShapeDtypeStruct((cfg["heads"] - 1, 1, total - learn), jnp.float32),
            jax.ShapeDtypeStruct((later, 2 * learn), jnp.bfloat16),
            jax.ShapeDtypeStruct((units, learn), jnp.bfloat16),
            *lead,
        ),
        in_specs=[LOCAL] + [ANYWHERE] * len(piece_list) + [LOCAL] * 2,
        out_specs=(LOCAL,) * (5 + len(lead)),
        scratch_shapes=[
            pltpu.VMEM((units, 2 * learn), jnp.bfloat16),
            pltpu.SemaphoreType.DMA((len(piece_list),)),
        ],
        compiler_params=pltpu.CompilerParams(vmem_limit_bytes=32 << 20),
        cost_estimate=pl.CostEstimate(
            flops=4 * units * total * width, bytes_accessed=4 * total * width, transcendentals=0
        ),
        name="learner",
    )(staged, *piece_list, aux, head)
    rest_outs = pl.pallas_call(
        functools.partial(rest_kernel, cfg),
        out_shape=tuple(rest),
        in_specs=[LOCAL] * 3,
        out_specs=(LOCAL,) * len(rest),
        compiler_params=pltpu.CompilerParams(vmem_limit_bytes=32 << 20),
        cost_estimate=pl.CostEstimate(
            flops=2 * later * learn * width, bytes_accessed=2 * learn * width, transcendentals=0
        ),
        name="rest",
    )(staged, order, first)
    return weights, ghead, own, first_outs, list(rest_outs)


def opponent_kernel(cfg, count, *refs):
    frames, (weights, head, out, xs, sems) = refs[:count], refs[count:]
    envs = frames[0].shape[0]
    copies = [
        pltpu.make_async_copy(f, xs.at[pl.ds(i * envs, envs)], sems.at[i])
        for i, f in enumerate(frames)
    ]
    for copy in copies:
        copy.start()
    for copy in copies:
        copy.wait()
    result = forward(xs[...], weights[...], head[...], cfg["width"])[0].astype(jnp.bfloat16)
    for i in range(count):
        out[i] = result[:, i * envs : (i + 1) * envs]


def opponents(frames, weights, head, cfg):
    count, (envs, width) = len(frames), frames[0].shape
    return pl.pallas_call(
        functools.partial(opponent_kernel, cfg, count),
        out_shape=jax.ShapeDtypeStruct((count, head.shape[0], envs), jnp.bfloat16),
        in_specs=[ANYWHERE] * count + [LOCAL] * 2,
        out_specs=LOCAL,
        scratch_shapes=[
            pltpu.VMEM((count * envs, width), jnp.bfloat16),
            pltpu.SemaphoreType.DMA((count,)),
        ],
        compiler_params=pltpu.CompilerParams(vmem_limit_bytes=24 << 20),
        cost_estimate=pl.CostEstimate(
            flops=2 * cfg["units"] * count * envs * width,
            bytes_accessed=2 * count * envs * width,
            transcendentals=0,
        ),
        name="opponents",
    )(*frames, weights, head)


def adam_step(master, moment, second, grad, rate):
    moment = beta_first * moment + (1.0 - beta_first) * grad
    second = beta_second * second + (1.0 - beta_second) * grad * grad
    master = master - rate * moment / (jnp.sqrt(second) + adam_eps)
    return (master, moment, second)


def adam_kernel(parts, head_parts, cuts, *refs):
    rate = refs[0][0]
    parts, refs = refs[1 : 1 + parts], refs[1 + parts :]
    head_parts, refs = refs[:head_parts], refs[head_parts:]
    core, head, core_out, head_out = refs[:3], refs[3:6], refs[6:9], refs[9:12]
    stages, sems = refs[12:15], refs[15]
    copies = []
    for n, (start, stop) in enumerate(cuts):
        columns = slice(start, stop)
        grad = sum(part[:, columns].astype(jnp.float32) for part in parts)
        for i, value in enumerate(adam_step(*(x[:, columns] for x in core), grad, rate)):
            stages[i][:, columns] = value
            copies.append(
                pltpu.make_async_copy(
                    stages[i].at[:, columns], core_out[i].at[:, columns], sems.at[n, i]
                )
            )
            copies[-1].start()
    count = head[0].shape[0]
    sums = [part[:count] for part in head_parts]
    while len(sums) > 1:
        sums = [a + b for a, b in zip(sums[::2], sums[1::2])]
    grad = sums[0].reshape(head[0].shape)
    for out, value in zip(head_out, adam_step(*(x[...] for x in head), grad, rate)):
        out[...] = value
    for copy in copies:
        copy.wait()


def adam(rates, parts, head_parts, core, head):
    rows, width = core[0].shape
    tiles = width // 128
    cuts = [(128 * (tiles * n // 3), 128 * (tiles * (n + 1) // 3)) for n in range(3)]
    cuts[-1] = (cuts[-1][0], width)
    one = jax.ShapeDtypeStruct((rows, width), jnp.float32)
    small = jax.ShapeDtypeStruct(head[0].shape, jnp.float32)
    smem = pl.BlockSpec(memory_space=pltpu.SMEM)
    return pl.pallas_call(
        functools.partial(adam_kernel, len(parts), len(head_parts), cuts),
        out_shape=(one,) * 3 + (small,) * 3,
        in_specs=[smem] + [LOCAL] * (len(parts) + len(head_parts) + 6),
        out_specs=(ANYWHERE,) * 3 + (LOCAL,) * 3,
        scratch_shapes=[pltpu.VMEM((rows, width), jnp.float32)] * 3
        + [pltpu.SemaphoreType.DMA((len(cuts), 3))],
        compiler_params=pltpu.CompilerParams(vmem_limit_bytes=16 << 20),
        cost_estimate=pl.CostEstimate(
            flops=20 * rows * width, bytes_accessed=32 * rows * width, transcendentals=0
        ),
        name="adam",
    )(rates, *parts, *head_parts, *core, *head)


def per_device(
    learn_obs,
    own_obs,
    opp_obs,
    opponent,
    actions,
    done,
    rewards,
    behaviour,
    core_master,
    core_mom,
    core_vel,
    head_master,
    head_mom,
    head_vel,
    rates,
):
    envs, length, width = learn_obs.shape[1:]
    heads, units = head_master.shape[1:]
    action_count = heads - 1
    agents, members = lax.axis_size("agent"), lax.axis_size("dp")
    rows = core_master.shape[1]
    chips = members // CORES
    line = chips == LINE and members == LINE * CORES and units == members * rows
    wide = jnp.float32

    def along(x, pairs):
        return lax.ppermute(
            x, "dp", [(a * CORES + c, b * CORES + c) for a, b in pairs for c in range(CORES)]
        )

    def sibling(x):
        return lax.ppermute(x, "dp", [(i, i ^ 1) for i in range(members)])

    paired = agents & (agents - 1) == 0

    def other_agent(i, by):
        return i ^ by if paired else (i + by) % agents

    def swap(x, by):
        return lax.ppermute(x, "agent", [(i, other_agent(i, by)) for i in range(agents)])

    mine = core_master[0].astype(jnp.bfloat16)
    if line:
        far = along(mine, GATHER_FAR)
        near = along(mine, GATHER_NEAR)
        mid = along(mine, GATHER_MID)
        onward = along(far, GATHER_FORWARD)
        got = (("mine", mine, SELF_FROM, None), ("far", far, FAR_FROM, None),
               ("near", near, NEAR_FROM, None), ("mid", mid, LAST_FROM, (1, 2)),
               ("onward", onward, LAST_FROM, (0, 3)))
        piece_list = [g[1] for g in got] + [sibling(g[1]) for g in got]
        pieces = [(rows, g[2], True, g[3]) for g in got] + [(rows, g[2], False, g[3]) for g in got]
        roles = ROLES
    else:
        piece_list = [lax.all_gather(mine, "dp", axis=0, tiled=True)]
        pieces = [(units, None, True, None)]
        roles = None

    frames = [opp_obs[0]] + [swap(opp_obs[0], by) for by in range(1, agents)]

    aux = jnp.stack(
        [actions[0].astype(wide), done[0].astype(wide), rewards[0], behaviour[0]]
    ).reshape(4, envs * length)
    padded = -(-heads // SUBLANES) * SUBLANES
    head = jnp.pad(head_master[0].astype(jnp.bfloat16), ((0, padded - heads), (0, 0)))
    cfg = dict(pieces=pieces, heads=heads, width=width, units=units, length=length, roles=roles,
               learn=envs * length)
    me = lax.axis_index("agent")
    chosen = [
        opponent[0, :, 0][None] == other_agent(me, by if paired else agents - by)
        for by in range(agents)
    ]
    learn_rows, own_rows, aux, head, chosen = lax.optimization_barrier(
        (learn_obs[0].reshape(envs * length, width), own_obs[0], aux, head, chosen)
    )
    staged = stage([learn_rows, own_rows])
    weights, ghead, own, lead, rest = learner(staged, piece_list, aux, head, cfg)
    played = opponents(frames, weights, head, cfg)

    own_logits = jnp.transpose(own, (1, 2, 0))
    opp_logits = jnp.zeros((action_count, envs), jnp.bfloat16)
    for by in range(agents):
        answer = played[by]
        if by:
            back = by if paired else agents - by
            answer = swap(answer, back)
        opp_logits = jnp.where(chosen[by], answer[:action_count], opp_logits)

    if line:
        blocks = lead + rest
        send, keep = blocks[::CORES], [b.astype(wide) for b in blocks[1::CORES]]
        came = [sibling(b) for b in send]
        last, toward = [
            (k + c.astype(wide)).astype(jnp.bfloat16) for k, c in zip(keep[:2], came[:2])
        ]
        through = along(last, SCATTER_FORWARD).astype(wide)
        part_mid = along(last, SCATTER_MID)
        part_near = along(toward, SCATTER_NEAR)
        onward = (keep[2] + came[2].astype(wide) + through).astype(jnp.bfloat16)
        part_far = along(onward, SCATTER_FAR)
        core_parts = (blocks[-1], came[3], part_near, part_mid, part_far)
        ghead = ghead + sibling(ghead)
        one = along(ghead, ((0, 1), (1, 0), (2, 3), (3, 2)))
        two = along(ghead, ((0, 2), (2, 0), (1, 3), (3, 1)))
        three = along(ghead, ((0, 3), (3, 0), (1, 2), (2, 1)))
        head_parts = (ghead, one, two, three)
    else:
        core_parts = (lax.psum_scatter(rest[0], "dp", scatter_dimension=0, tiled=True),)
        head_parts = (lax.psum(ghead, "dp"),)
    by_row = lambda x: jnp.transpose(x, (1, 0, 2))
    new = adam(
        rates,
        core_parts,
        head_parts,
        (core_master[0], core_mom[0], core_vel[0]),
        (by_row(head_master), by_row(head_mom), by_row(head_vel)),
    )
    return (own_logits, opp_logits.T[None], *[x[None] for x in new[:3]], *map(by_row, new[3:]))


def solution(mesh):
    sharded, whole = P("agent", "dp", None), P("agent", None, None)

    return jax.shard_map(
        per_device,
        mesh=mesh,
        in_specs=(P("agent", "dp", None, None),) + (sharded,) * 10 + (whole,) * 3 + (P("agent"),),
        out_specs=(sharded,) * 5 + (whole,) * 3,
        check_vma=False,
    )
```

```python
import functools

import jax
import jax.numpy as jnp
from jax import lax
from jax.experimental import pallas as pl
from jax.experimental.pallas import tpu as pltpu
from jax.sharding import PartitionSpec as P


gamma_rate = 0.99
baseline_cost = 0.5
entropy_cost = 0.05
beta_first = 0.9
beta_second = 0.99
adam_eps = 1e-08

CORES = 2
SUBLANES = 32

LINE = 4
GATHER_FAR = ((0, 2), (3, 1), (1, 0), (2, 3))
GATHER_NEAR = ((0, 1), (3, 2), (1, 3), (2, 0))
GATHER_MID = ((1, 2), (2, 1))
GATHER_FORWARD = ((2, 3), (1, 0))
FAR_FROM = (1, 3, 0, 2)
NEAR_FROM = (2, 0, 3, 1)
LAST_FROM = (3, 2, 1, 0)
SELF_FROM = (0, 1, 2, 3)
ROLES = (LAST_FROM, NEAR_FROM, FAR_FROM, SELF_FROM)
SCATTER_FORWARD = ((3, 2), (0, 1))
SCATTER_NEAR = tuple((b, a) for a, b in GATHER_NEAR)
SCATTER_MID = ((1, 2), (2, 1))
SCATTER_FAR = tuple((b, a) for a, b in GATHER_FAR)


def dot(left, right, dims, precision=None):
    return lax.dot_general(
        left, right, (dims, ((), ())), preferred_element_type=jnp.float32, precision=precision
    )


NN = ((1,), (0,))
NT = ((1,), (1,))


def table(values, index):
    result = jnp.int32(values[0])
    for place, value in enumerate(values[1:], 1):
        result = jnp.where(index == place, jnp.int32(value), result)
    return result


def trace_gradients(out, boot, aux, action_count, length, scale):
    rows, lanes = out.shape
    row = lax.broadcasted_iota(jnp.int32, (rows, lanes), 0)
    step = lax.rem(lax.broadcasted_iota(jnp.int32, (1, lanes), 1), length)
    last = step == length - 1
    policy = row < action_count
    actions, done, rewards, behaviour = (aux[i : i + 1] for i in range(4))
    values = out[action_count : action_count + 1]
    totals = jnp.sum(jnp.where(policy, jnp.exp(out), 0.0), 0, keepdims=True)
    logp = out - jnp.log(totals)
    probs = jnp.where(policy, jnp.exp(logp), 0.0)
    chosen = (row == actions.astype(jnp.int32)).astype(jnp.float32)
    picked = jnp.sum(logp * chosen, 0, keepdims=True)
    ratio = jnp.minimum(1.0, jnp.exp(picked - behaviour))
    discount = gamma_rate * (1.0 - done)
    following = lambda x, end: jnp.where(last, end, pltpu.roll(x, lanes - 1, 1))
    delta = ratio * (rewards + discount * following(values, boot) - values)
    factor = jnp.where(last, 0.0, discount * ratio)
    reach = 1
    while reach < length:
        delta = delta + factor * pltpu.roll(delta, lanes - reach, 1)
        factor = factor * pltpu.roll(factor, lanes - reach, 1)
        reach *= 2
    targets = values + delta
    advantage = ratio * (rewards + discount * following(targets, boot) - values)
    entropy = -jnp.sum(jnp.where(policy, probs * logp, 0.0), 0, keepdims=True)
    grad_logits = scale * (
        -advantage * (chosen - probs) + entropy_cost * probs * (logp + entropy)
    )
    grad_value = scale * (-baseline_cost * (targets - values))
    return jnp.where(policy, grad_logits, jnp.where(row == action_count, grad_value, 0.0))


ANYWHERE = pl.BlockSpec(memory_space=pl.ANY)
LOCAL = pl.BlockSpec(memory_space=pltpu.VMEM)


def in_hbm(arrays):
    return [pltpu.with_memory_space_constraint(x, pltpu.HBM) for x in arrays]


def stage_kernel(learn_ref, own_ref, *refs):
    small, (staged, aux, head_out), local, sems = refs[:5], refs[5:8], refs[8:13], refs[13]
    per_step, head_ref = local[:4], local[4]
    rows = learn_ref.shape[0]
    small_copies = [
        pltpu.make_async_copy(a, b, sems.at[2 + i]) for i, (a, b) in enumerate(zip(small, local))
    ]
    for copy in small_copies:
        copy.start()
    copies = (
        pltpu.make_async_copy(learn_ref, staged.at[pl.ds(0, rows)], sems.at[0]),
        pltpu.make_async_copy(own_ref, staged.at[pl.ds(rows, own_ref.shape[0])], sems.at[1]),
    )
    for copy in copies:
        copy.start()
    length, envs = per_step[0].shape
    lane = lax.broadcasted_iota(jnp.int32, (envs, rows), 1)
    spread = (lane // length == lax.broadcasted_iota(jnp.int32, (envs, rows), 0)).astype(
        jnp.float32
    )
    mask = lax.rem(lax.broadcasted_iota(jnp.int32, (length, rows), 1), length)
    mask = mask == lax.broadcasted_iota(jnp.int32, (length, rows), 0)
    for copy in small_copies:
        copy.wait()
    for i, ref in enumerate(per_step):
        wide = dot(ref[...].astype(jnp.float32), spread, NN, lax.Precision.HIGHEST)
        aux[i : i + 1] = jnp.sum(jnp.where(mask, wide, 0.0), 0, keepdims=True)
    heads, _, units = head_ref.shape
    head_out[...] = jnp.zeros_like(head_out)
    head_out[:heads] = head_ref[...].reshape(heads, units).astype(jnp.bfloat16)
    for copy in copies:
        copy.wait()


def stage(learn_rows, own_rows, per_step, head):
    rows, width = learn_rows.shape
    total = rows + own_rows.shape[0]
    heads, _, units = head.shape
    padded = -(-heads // SUBLANES) * SUBLANES
    return pl.pallas_call(
        stage_kernel,
        out_shape=(
            jax.ShapeDtypeStruct((total, width), jnp.bfloat16),
            jax.ShapeDtypeStruct((len(per_step), rows), jnp.float32),
            jax.ShapeDtypeStruct((padded, units), jnp.bfloat16),
        ),
        in_specs=[ANYWHERE] * 7,
        out_specs=(LOCAL,) * 3,
        scratch_shapes=[pltpu.VMEM(x.shape, x.dtype) for x in (*per_step, head)]
        + [pltpu.SemaphoreType.DMA((7,))],
        compiler_params=pltpu.CompilerParams(vmem_limit_bytes=8 << 20),
        cost_estimate=pl.CostEstimate(
            flops=0, bytes_accessed=4 * total * width, transcendentals=0
        ),
        name="stage",
    )(*in_hbm((learn_rows, own_rows, *per_step, head)))


def place_pieces(pieces, w_refs, ws, sems):
    place = lax.axis_index("dp")
    core, chip = lax.rem(place, CORES), lax.div(place, CORES)

    def piece_copy(i):
        rows, source, same, chips = pieces[i]
        if source is None:
            return pltpu.make_async_copy(w_refs[i], ws, sems.at[i]), None
        owner = core if same else 1 - core
        start = pl.multiple_of((table(source, chip) * CORES + owner) * rows, rows)
        live = None
        if chips is not None:
            live = functools.reduce(jnp.logical_or, [chip == one for one in chips])
        return pltpu.make_async_copy(w_refs[i], ws.at[pl.ds(start, rows)], sems.at[i]), live

    def each_piece(act):
        for i in range(len(pieces)):
            copy, live = piece_copy(i)
            if live is None:
                act(copy)
            else:
                pl.when(live)(functools.partial(act, copy))

    each_piece(lambda copy: copy.start())
    each_piece(lambda copy: copy.wait())


def last_rows(pieces):
    rows = CORES * pieces[0][0]
    chip = lax.div(lax.axis_index("dp"), CORES)
    return pl.ds(pl.multiple_of(table(LAST_FROM, chip) * rows, rows), rows)


def early_kernel(pieces, width, xs, *refs):
    w_refs, (ws, pre, sems) = refs[: len(pieces)], refs[len(pieces) :]
    ws[last_rows(pieces), :] = jnp.zeros((CORES * pieces[0][0], ws.shape[1]), ws.dtype)
    place_pieces(pieces, w_refs, ws, sems)
    pre[...] = dot(ws[:, :width], xs[...], NT)


def early(staged, pieces, piece_list, units):
    total, width = staged.shape
    return pl.pallas_call(
        functools.partial(early_kernel, pieces, width),
        out_shape=(
            jax.ShapeDtypeStruct((units, width + units), jnp.bfloat16),
            jax.ShapeDtypeStruct((units, total), jnp.float32),
        ),
        in_specs=[LOCAL] + [ANYWHERE] * len(pieces),
        out_specs=(LOCAL,) * 2,
        scratch_shapes=[pltpu.SemaphoreType.DMA((len(pieces),))],
        compiler_params=pltpu.CompilerParams(vmem_limit_bytes=24 << 20),
        cost_estimate=pl.CostEstimate(
            flops=2 * units * total * width, bytes_accessed=4 * units * width, transcendentals=0
        ),
        name="early",
    )(staged, *piece_list)


def forward(pre_one, weights, head, width):
    first = jnp.maximum(pre_one, 0.0)
    first_bf = first.astype(jnp.bfloat16)
    pre_two = dot(weights[:, width:], first_bf, NN)
    second_bf = (jnp.maximum(pre_two, 0.0) + first).astype(jnp.bfloat16)
    return dot(head, second_bf, NN), pre_one, first_bf, pre_two, second_bf


def learner_kernel(cfg, *refs):
    pieces, heads, roles = cfg["pieces"], cfg["heads"], cfg["roles"]
    xs, refs = refs[0], refs[1:]
    w_refs, refs = refs[: len(pieces)], refs[len(pieces) :]
    aux_ref, head_ref, refs = refs[0], refs[1], refs[2:]
    if roles is not None:
        refs = refs[2:]
    ws, pre, ghead_ref, own_ref, order_ref, first_ref, refs = *refs[:6], refs[6:]
    lead, (gp, sw) = refs[:-2], refs[-2:]
    learn, width, units, length = cfg["learn"], cfg["width"], cfg["units"], cfg["length"]
    envs = learn // length
    place = lax.axis_index("dp")
    core, chip = lax.rem(place, CORES), lax.div(place, CORES)

    place_pieces(pieces, w_refs, ws, sw)
    if roles is None:
        pre[...] = dot(ws[:, :width], xs[...], NT)
    else:
        late = last_rows(pieces)
        pre[late, :] = dot(ws[late, :width], xs[...], NT)
    pre_one = pre[...]
    out, pre_one, first_bf, pre_two, second_bf = forward(pre_one, ws[...], head_ref[...], width)
    own_ref[...] = out[: heads - 1, learn:].reshape(heads - 1, 1, envs)
    spread = lax.broadcasted_iota(jnp.int32, (envs, learn), 1) // length
    spread = (spread == lax.broadcasted_iota(jnp.int32, (envs, learn), 0)).astype(jnp.float32)
    boot = dot(out[:, learn:], spread, NN, lax.Precision.HIGHEST)[heads - 1 : heads]
    grad = trace_gradients(
        out[:, :learn], boot, aux_ref[...], heads - 1, length, 1.0 / length
    ).astype(jnp.bfloat16)
    ghead_ref[...] = dot(grad, second_bf[:, :learn], NT)
    grad_second = dot(head_ref[...].T, grad, NN)
    grad_two = jnp.where(pre_two[:, :learn] > 0, grad_second, 0.0).astype(jnp.bfloat16)
    grad_first = grad_second + dot(ws[:, width:].T, grad_two, NN)
    grad_one = jnp.where(pre_one[:, :learn] > 0, grad_first, 0.0).astype(jnp.bfloat16)
    first_ref[...] = first_bf[:, :learn]

    if roles is None:
        order_ref[:, :learn] = grad_one
        order_ref[:, learn:] = grad_two
        return
    gp[:, :learn] = grad_one
    gp[:, learn:] = grad_two
    rows = units // (len(roles) * CORES)
    order = []
    for role in roles:
        for same in (False, True):
            owner = core if same else 1 - core
            start = pl.multiple_of((table(role, chip) * CORES + owner) * rows, rows)
            order.append(gp[pl.ds(start, rows), :])
    order_ref[...] = jnp.concatenate(order[CORES:], 0)
    gradient_rows(jnp.concatenate(order[:CORES], 0), xs, first_ref, lead, learn, width, cfg["chunk"])


def gradient_rows(order, xs, first_ref, outs, learn, width, chunk):
    rows = outs[0].shape[0]

    def put(columns, value):
        value = value.astype(jnp.bfloat16)
        for i, out in enumerate(outs):
            out[:, columns] = value[i * rows : (i + 1) * rows]

    for start in range(0, width, chunk):
        columns = slice(start, start + chunk)
        put(columns, dot(order[:, :learn], xs[:learn, columns], NN))
    put(slice(width, None), dot(order[:, learn:], first_ref[...], NT))


def rest_kernel(cfg, xs, order_ref, first_ref, *outs):
    gradient_rows(order_ref[...], xs, first_ref, outs, cfg["learn"], cfg["width"], cfg["chunk"])


def column_chunk(width):
    return max(c for c in range(128, 1153, 128) if width % c == 0)


def learner(staged, piece_list, aux, head, before, cfg):
    total, width, units, learn = staged.shape[0], cfg["width"], cfg["units"], cfg["learn"]
    padded = head.shape[0]
    cfg = dict(cfg, chunk=column_chunk(width))
    roles = cfg["roles"]
    block = lambda rows: jax.ShapeDtypeStruct((rows, width + units), jnp.bfloat16)
    inputs = 3 + len(piece_list)
    if roles is None:
        lead, rest, later, aliases = [], [block(units)], units, {}
    else:
        rows = units // (len(roles) * CORES)
        lead, rest = [block(rows)] * CORES, [block(rows)] * (CORES * (len(roles) - 1))
        later = units - CORES * rows
        aliases = {inputs: 0, inputs + 1: 1}
    weights, _, ghead, own, order, first, *first_outs = pl.pallas_call(
        functools.partial(learner_kernel, cfg),
        out_shape=(
            block(units),
            jax.ShapeDtypeStruct((units, total), jnp.float32),
            jax.ShapeDtypeStruct((padded, units), jnp.float32),
            jax.ShapeDtypeStruct((cfg["heads"] - 1, 1, total - learn), jnp.float32),
            jax.ShapeDtypeStruct((later, 2 * learn), jnp.bfloat16),
            jax.ShapeDtypeStruct((units, learn), jnp.bfloat16),
            *lead,
        ),
        in_specs=[LOCAL] + [ANYWHERE] * len(piece_list) + [LOCAL] * (2 + len(before)),
        out_specs=(LOCAL,) * (6 + len(lead)),
        input_output_aliases=aliases,
        scratch_shapes=[
            pltpu.VMEM((units, 2 * learn), jnp.bfloat16),
            pltpu.SemaphoreType.DMA((len(piece_list),)),
        ],
        compiler_params=pltpu.CompilerParams(vmem_limit_bytes=32 << 20),
        cost_estimate=pl.CostEstimate(
            flops=4 * units * total * width, bytes_accessed=4 * total * width, transcendentals=0
        ),
        name="learner",
    )(staged, *piece_list, aux, head, *before)
    rest_outs = pl.pallas_call(
        functools.partial(rest_kernel, cfg),
        out_shape=tuple(rest),
        in_specs=[LOCAL] * 3,
        out_specs=(LOCAL,) * len(rest),
        compiler_params=pltpu.CompilerParams(vmem_limit_bytes=32 << 20),
        cost_estimate=pl.CostEstimate(
            flops=2 * later * learn * width, bytes_accessed=2 * learn * width, transcendentals=0
        ),
        name="rest",
    )(staged, order, first)
    return weights, ghead, own, first_outs, list(rest_outs)


def opponent_kernel(cfg, count, *refs):
    frames, (weights, head), refs = refs[:count], refs[count : count + 2], refs[count + 2 :]
    outs, (xs, sems) = refs[:count], refs[count:]
    envs = frames[0].shape[0]
    copies = [
        pltpu.make_async_copy(f, xs.at[pl.ds(i * envs, envs)], sems.at[i])
        for i, f in enumerate(frames)
    ]
    for copy in copies:
        copy.start()
    for copy in copies:
        copy.wait()
    width = cfg["width"]
    pre_one = dot(weights[:, :width], xs[...], NT)
    result = forward(pre_one, weights[...], head[...], width)[0].astype(jnp.bfloat16)
    for i, out in enumerate(outs):
        out[...] = result[:, i * envs : (i + 1) * envs]


def opponents(frames, weights, head, cfg):
    count, (envs, width) = len(frames), frames[0].shape
    return pl.pallas_call(
        functools.partial(opponent_kernel, cfg, count),
        out_shape=(jax.ShapeDtypeStruct((head.shape[0], envs), jnp.bfloat16),) * count,
        in_specs=[ANYWHERE] * count + [LOCAL] * 2,
        out_specs=(LOCAL,) * count,
        scratch_shapes=[
            pltpu.VMEM((count * envs, width), jnp.bfloat16),
            pltpu.SemaphoreType.DMA((count,)),
        ],
        compiler_params=pltpu.CompilerParams(vmem_limit_bytes=24 << 20),
        cost_estimate=pl.CostEstimate(
            flops=2 * cfg["units"] * count * envs * width,
            bytes_accessed=2 * count * envs * width,
            transcendentals=0,
        ),
        name="opponents",
    )(*frames, weights, head)


def other_agent(i, by, agents):
    return i ^ by if agents & (agents - 1) == 0 else (i + by) % agents


def choose_kernel(*refs):
    answers, ids, out = refs[:-2], refs[-2], refs[-1]
    agents, me = len(answers), lax.axis_index("agent")
    result = jnp.zeros(out.shape, jnp.float32)
    for by, answer in enumerate(answers):
        player = other_agent(me, by, agents)
        result = jnp.where(ids[...] == player, answer[: out.shape[0]].astype(jnp.float32), result)
    out[...] = result.astype(out.dtype)


def choose(answers, ids, count):
    return pl.pallas_call(
        choose_kernel,
        out_shape=jax.ShapeDtypeStruct((count, ids.shape[1]), jnp.bfloat16),
        in_specs=[LOCAL] * (len(answers) + 1),
        out_specs=LOCAL,
        compiler_params=pltpu.CompilerParams(vmem_limit_bytes=2 << 20),
        name="choose",
    )(*answers, ids)


def add_kernel(*refs):
    refs[-1][...] = sum(x[...].astype(jnp.float32) for x in refs[:-1]).astype(refs[-1].dtype)


def add(*arrays):
    return pl.pallas_call(
        add_kernel,
        out_shape=jax.ShapeDtypeStruct(arrays[0].shape, arrays[0].dtype),
        in_specs=[LOCAL] * len(arrays),
        out_specs=LOCAL,
        compiler_params=pltpu.CompilerParams(vmem_limit_bytes=4 << 20),
        cost_estimate=pl.CostEstimate(
            flops=arrays[0].size, bytes_accessed=2 * len(arrays) * arrays[0].size, transcendentals=0
        ),
        name="add",
    )(*arrays)


def adam_step(master, moment, second, grad, rate):
    moment = beta_first * moment + (1.0 - beta_first) * grad
    second = beta_second * second + (1.0 - beta_second) * grad * grad
    master = master - rate * moment / (jnp.sqrt(second) + adam_eps)
    return (master, moment, second)


def adam_kernel(parts, head_parts, cuts, *refs):
    rate = refs[0][...]
    parts, refs = refs[1 : 1 + parts], refs[1 + parts :]
    head_parts, refs = refs[:head_parts], refs[head_parts:]
    core, head, core_out, head_out = refs[:3], refs[3:6], refs[6:9], refs[9:12]
    stages, sems = refs[12:15], refs[15]
    copies = []
    for n, (start, stop) in enumerate(cuts):
        columns = slice(start, stop)
        grad = sum(part[:, columns].astype(jnp.float32) for part in parts)
        for i, value in enumerate(adam_step(*(x[:, columns] for x in core), grad, rate)):
            stages[i][:, columns] = value
            copies.append(
                pltpu.make_async_copy(
                    stages[i].at[:, columns], core_out[i].at[:, columns], sems.at[n, i]
                )
            )
            copies[-1].start()
    count = head[0].shape[0]
    sums = [part[:count] for part in head_parts]
    while len(sums) > 1:
        sums = [a + b for a, b in zip(sums[::2], sums[1::2])]
    grad = sums[0].reshape(head[0].shape)
    for out, value in zip(head_out, adam_step(*(x[...] for x in head), grad, rate)):
        out[...] = value
    for copy in copies:
        copy.wait()


def adam(rates, parts, head_parts, core, head):
    rows, width = core[0].shape
    tiles = width // 128
    cuts = [(128 * (tiles * n // 3), 128 * (tiles * (n + 1) // 3)) for n in range(3)]
    cuts[-1] = (cuts[-1][0], width)
    one = jax.ShapeDtypeStruct((rows, width), jnp.float32)
    small = jax.ShapeDtypeStruct(head[0].shape, jnp.float32)
    return pl.pallas_call(
        functools.partial(adam_kernel, len(parts), len(head_parts), cuts),
        out_shape=(one,) * 3 + (small,) * 3,
        in_specs=[LOCAL] * (len(parts) + len(head_parts) + 7),
        out_specs=(ANYWHERE,) * 3 + (LOCAL,) * 3,
        scratch_shapes=[pltpu.VMEM((rows, width), jnp.float32)] * 3
        + [pltpu.SemaphoreType.DMA((len(cuts), 3))],
        compiler_params=pltpu.CompilerParams(vmem_limit_bytes=16 << 20),
        cost_estimate=pl.CostEstimate(
            flops=20 * rows * width, bytes_accessed=32 * rows * width, transcendentals=0
        ),
        name="adam",
    )(rates.reshape(1, 1), *parts, *head_parts, *core, *head)


def per_device(
    learn_obs,
    own_obs,
    opp_obs,
    opponent,
    actions,
    done,
    rewards,
    behaviour,
    core_master,
    core_mom,
    core_vel,
    head_master,
    head_mom,
    head_vel,
    rates,
):
    envs, length, width = learn_obs.shape[1:]
    heads, units = head_master.shape[1:]
    action_count = heads - 1
    agents, members = lax.axis_size("agent"), lax.axis_size("dp")
    rows = core_master.shape[1]
    chips = members // CORES
    line = chips == LINE and members == LINE * CORES and units == members * rows

    def along(x, pairs):
        return lax.ppermute(
            x, "dp", [(a * CORES + c, b * CORES + c) for a, b in pairs for c in range(CORES)]
        )

    def sibling(x):
        return lax.ppermute(x, "dp", [(i, i ^ 1) for i in range(members)])

    def swap(x, by):
        return lax.ppermute(x, "agent", [(i, other_agent(i, by, agents)) for i in range(agents)])

    mine = core_master[0].astype(jnp.bfloat16)
    if line:
        far = along(mine, GATHER_FAR)
        near = along(mine, GATHER_NEAR)
        mid = along(mine, GATHER_MID)
        onward = along(far, GATHER_FORWARD)
        first = (("mine", mine, SELF_FROM, None), ("far", far, FAR_FROM, None),
                 ("near", near, NEAR_FROM, None))
        final = (("mid", mid, LAST_FROM, (1, 2)), ("onward", onward, LAST_FROM, (0, 3)))

        def with_siblings(group):
            arrays = [g[1] for g in group] + [sibling(g[1]) for g in group]
            places = [(rows, g[2], same, g[3]) for same in (True, False) for g in group]
            return arrays, places

        (first_list, first_pieces), (piece_list, pieces) = with_siblings(first), with_siblings(final)
        roles = ROLES
    else:
        piece_list = [lax.all_gather(mine, "dp", axis=0, tiled=True)]
        pieces = [(units, None, True, None)]
        roles = None

    frames = [opp_obs[0]] + [swap(opp_obs[0], by) for by in range(1, agents)]

    by_row = lambda x: jnp.transpose(x, (1, 0, 2))
    cfg = dict(pieces=pieces, heads=heads, width=width, units=units, length=length, roles=roles,
               learn=envs * length)
    staged, aux, head = stage(
        learn_obs[0].reshape(envs * length, width),
        own_obs[0],
        [x[0].T for x in (actions, done, rewards, behaviour)],
        by_row(head_master),
    )
    before = ()
    if line:
        before = early(staged, first_pieces, first_list, units)
    weights, ghead, own, lead, rest = learner(staged, piece_list, aux, head, before, cfg)
    played = opponents(frames, weights, head, cfg)
    own_logits = jnp.transpose(own, (1, 2, 0))

    def undo(by):
        there = other_agent(0, by, agents)
        return next(b for b in range(agents) if other_agent(there, b, agents) == 0)

    answers = [played[0]] + [swap(played[by], undo(by)) for by in range(1, agents)]
    opp_logits = choose(answers, opponent[0].T, action_count)

    if line:
        blocks = lead + rest
        send, keep = blocks[::CORES], blocks[1::CORES]
        came = [sibling(b) for b in send]
        last, toward = add(keep[0], came[0]), add(keep[1], came[1])
        through = along(last, SCATTER_FORWARD)
        part_mid = along(last, SCATTER_MID)
        part_near = along(toward, SCATTER_NEAR)
        part_far = along(add(keep[2], came[2], through), SCATTER_FAR)
        core_parts = (keep[3], came[3], part_near, part_mid, part_far)
        ghead = add(ghead, sibling(ghead))
        one = along(ghead, ((0, 1), (1, 0), (2, 3), (3, 2)))
        two = along(ghead, ((0, 2), (2, 0), (1, 3), (3, 1)))
        three = along(ghead, ((0, 3), (3, 0), (1, 2), (2, 1)))
        head_parts = (ghead, one, two, three)
    else:
        core_parts = (lax.psum_scatter(rest[0], "dp", scatter_dimension=0, tiled=True),)
        head_parts = (lax.psum(ghead, "dp"),)
    new = adam(
        rates,
        core_parts,
        head_parts,
        (core_master[0], core_mom[0], core_vel[0]),
        (by_row(head_master), by_row(head_mom), by_row(head_vel)),
    )
    return (own_logits, opp_logits.T[None], *[x[None] for x in new[:3]], *map(by_row, new[3:]))


def solution(mesh):
    sharded, whole = P("agent", "dp", None), P("agent", None, None)

    return jax.shard_map(
        per_device,
        mesh=mesh,
        in_specs=(P("agent", "dp", None, None),) + (sharded,) * 10 + (whole,) * 3 + (P("agent"),),
        out_specs=(sharded,) * 5 + (whole,) * 3,
        check_vma=False,
    )
```

```python
import functools

import jax
import jax.numpy as jnp
from jax import lax
from jax.experimental import pallas as pl
from jax.experimental.pallas import tpu as pltpu
from jax.sharding import PartitionSpec as P


gamma_rate = 0.99
baseline_cost = 0.5
entropy_cost = 0.05
beta_first = 0.9
beta_second = 0.99
adam_eps = 1e-08

CORES = 2
SUBLANES = 32

LINE = 4
GATHER_FAR = ((0, 2), (3, 1), (1, 0), (2, 3))
GATHER_NEAR = ((0, 1), (3, 2), (1, 3), (2, 0))
GATHER_MID = ((1, 2), (2, 1))
GATHER_FORWARD = ((2, 3), (1, 0))
FAR_FROM = (1, 3, 0, 2)
NEAR_FROM = (2, 0, 3, 1)
LAST_FROM = (3, 2, 1, 0)
SELF_FROM = (0, 1, 2, 3)
ROLES = (LAST_FROM, NEAR_FROM, FAR_FROM, SELF_FROM)
SCATTER_FORWARD = ((3, 2), (0, 1))
SCATTER_NEAR = tuple((b, a) for a, b in GATHER_NEAR)
SCATTER_MID = ((1, 2), (2, 1))
SCATTER_FAR = tuple((b, a) for a, b in GATHER_FAR)


def dot(left, right, dims, precision=None):
    return lax.dot_general(
        left, right, (dims, ((), ())), preferred_element_type=jnp.float32, precision=precision
    )


NN = ((1,), (0,))
NT = ((1,), (1,))


def table(values, index):
    result = jnp.int32(values[0])
    for place, value in enumerate(values[1:], 1):
        result = jnp.where(index == place, jnp.int32(value), result)
    return result


def trace_gradients(out, boot, aux, action_count, length, scale):
    rows, lanes = out.shape
    row = lax.broadcasted_iota(jnp.int32, (rows, lanes), 0)
    step = lax.rem(lax.broadcasted_iota(jnp.int32, (1, lanes), 1), length)
    last = step == length - 1
    policy = row < action_count
    actions, done, rewards, behaviour = (aux[i : i + 1] for i in range(4))
    values = out[action_count : action_count + 1]
    totals = jnp.sum(jnp.where(policy, jnp.exp(out), 0.0), 0, keepdims=True)
    logp = out - jnp.log(totals)
    probs = jnp.where(policy, jnp.exp(logp), 0.0)
    chosen = (row == actions.astype(jnp.int32)).astype(jnp.float32)
    picked = jnp.sum(logp * chosen, 0, keepdims=True)
    ratio = jnp.minimum(1.0, jnp.exp(picked - behaviour))
    discount = gamma_rate * (1.0 - done)
    following = lambda x, end: jnp.where(last, end, pltpu.roll(x, lanes - 1, 1))
    delta = ratio * (rewards + discount * following(values, boot) - values)
    factor = jnp.where(last, 0.0, discount * ratio)
    reach = 1
    while reach < length:
        delta = delta + factor * pltpu.roll(delta, lanes - reach, 1)
        factor = factor * pltpu.roll(factor, lanes - reach, 1)
        reach *= 2
    targets = values + delta
    advantage = ratio * (rewards + discount * following(targets, boot) - values)
    entropy = -jnp.sum(jnp.where(policy, probs * logp, 0.0), 0, keepdims=True)
    grad_logits = scale * (
        -advantage * (chosen - probs) + entropy_cost * probs * (logp + entropy)
    )
    grad_value = scale * (-baseline_cost * (targets - values))
    return jnp.where(policy, grad_logits, jnp.where(row == action_count, grad_value, 0.0))


ANYWHERE = pl.BlockSpec(memory_space=pl.ANY)
LOCAL = pl.BlockSpec(memory_space=pltpu.VMEM)


def in_hbm(arrays):
    return [pltpu.with_memory_space_constraint(x, pltpu.HBM) for x in arrays]


def stage_kernel(learn_ref, own_ref, *refs):
    small, (staged, aux, head_out), local, sems = refs[:5], refs[5:8], refs[8:13], refs[13]
    per_step, head_ref = local[:4], local[4]
    rows = learn_ref.shape[0]
    small_copies = [
        pltpu.make_async_copy(a, b, sems.at[2 + i]) for i, (a, b) in enumerate(zip(small, local))
    ]
    for copy in small_copies:
        copy.start()
    copies = (
        pltpu.make_async_copy(learn_ref, staged.at[pl.ds(0, rows)], sems.at[0]),
        pltpu.make_async_copy(own_ref, staged.at[pl.ds(rows, own_ref.shape[0])], sems.at[1]),
    )
    for copy in copies:
        copy.start()
    length, envs = per_step[0].shape
    lane = lax.broadcasted_iota(jnp.int32, (envs, rows), 1)
    spread = (lane // length == lax.broadcasted_iota(jnp.int32, (envs, rows), 0)).astype(
        jnp.float32
    )
    mask = lax.rem(lax.broadcasted_iota(jnp.int32, (length, rows), 1), length)
    mask = mask == lax.broadcasted_iota(jnp.int32, (length, rows), 0)
    for copy in small_copies:
        copy.wait()
    for i, ref in enumerate(per_step):
        wide = dot(ref[...].astype(jnp.float32), spread, NN, lax.Precision.HIGHEST)
        aux[i : i + 1] = jnp.sum(jnp.where(mask, wide, 0.0), 0, keepdims=True)
    heads, _, units = head_ref.shape
    head_out[...] = jnp.zeros_like(head_out)
    head_out[:heads] = head_ref[...].reshape(heads, units).astype(jnp.bfloat16)
    for copy in copies:
        copy.wait()


def stage(learn_rows, own_rows, per_step, head):
    rows, width = learn_rows.shape
    total = rows + own_rows.shape[0]
    heads, _, units = head.shape
    padded = -(-heads // SUBLANES) * SUBLANES
    return pl.pallas_call(
        stage_kernel,
        out_shape=(
            jax.ShapeDtypeStruct((total, width), jnp.bfloat16),
            jax.ShapeDtypeStruct((len(per_step), rows), jnp.float32),
            jax.ShapeDtypeStruct((padded, units), jnp.bfloat16),
        ),
        in_specs=[ANYWHERE] * 7,
        out_specs=(LOCAL,) * 3,
        scratch_shapes=[pltpu.VMEM(x.shape, x.dtype) for x in (*per_step, head)]
        + [pltpu.SemaphoreType.DMA((7,))],
        compiler_params=pltpu.CompilerParams(vmem_limit_bytes=8 << 20),
        cost_estimate=pl.CostEstimate(
            flops=0, bytes_accessed=4 * total * width, transcendentals=0
        ),
        name="stage",
    )(*in_hbm((learn_rows, own_rows, *per_step, head)))


def where_am_i():
    place = lax.axis_index("dp")
    return lax.rem(place, CORES), lax.div(place, CORES)


def piece_rows(piece):
    rows, source, same, _ = piece
    core, chip = where_am_i()
    owner = core if same else 1 - core
    return pl.ds(pl.multiple_of((table(source, chip) * CORES + owner) * rows, rows), rows)


def piece_live(piece):
    _, chip = where_am_i()
    return functools.reduce(jnp.logical_or, [chip == one for one in piece[3]])


def each_piece(pieces, w_refs, ws, sems, act):
    for i, piece in enumerate(pieces):
        copy = pltpu.make_async_copy(w_refs[i], ws.at[piece_rows(piece)], sems.at[i])
        if piece[3] is None:
            act(copy)
        else:
            pl.when(piece_live(piece))(functools.partial(act, copy))


def multiply_pieces(pieces, w_refs, xs, width, pre):
    blocks, places = [], []
    for piece, ref in zip(pieces, w_refs):
        value = ref[:, :width]
        twin = [n for n, other in enumerate(places) if other[1:3] == piece[1:3]]
        if twin:
            blocks[twin[0]] = jnp.where(piece_live(piece), value, blocks[twin[0]])
        else:
            blocks.append(value)
            places.append(piece)
    result = dot(jnp.concatenate(blocks, 0), xs[...], NT)
    at = 0
    for piece in places:
        pre[piece_rows(piece), :] = result[at : at + piece[0]]
        at += piece[0]


def early_kernel(pieces, width, xs, *refs):
    w_refs, (ws, pre, sems) = refs[: len(pieces)], refs[len(pieces) :]
    each_piece(pieces, w_refs, ws, sems, lambda copy: copy.start())
    multiply_pieces(pieces, w_refs, xs, width, pre)
    each_piece(pieces, w_refs, ws, sems, lambda copy: copy.wait())


def early(staged, pieces, piece_list, units):
    total, width = staged.shape
    return pl.pallas_call(
        functools.partial(early_kernel, pieces, width),
        out_shape=(
            jax.ShapeDtypeStruct((units, width + units), jnp.bfloat16),
            jax.ShapeDtypeStruct((units, total), jnp.float32),
        ),
        in_specs=[LOCAL] * (1 + len(pieces)),
        out_specs=(LOCAL,) * 2,
        scratch_shapes=[pltpu.SemaphoreType.DMA((len(pieces),))],
        compiler_params=pltpu.CompilerParams(vmem_limit_bytes=24 << 20),
        cost_estimate=pl.CostEstimate(
            flops=2 * units * total * width, bytes_accessed=4 * units * width, transcendentals=0
        ),
        name="early",
    )(staged, *piece_list)


def forward(pre_one, weights, head, width):
    first = jnp.maximum(pre_one, 0.0)
    first_bf = first.astype(jnp.bfloat16)
    pre_two = dot(weights[:, width:], first_bf, NN)
    second_bf = (jnp.maximum(pre_two, 0.0) + first).astype(jnp.bfloat16)
    return dot(head, second_bf, NN), pre_one, first_bf, pre_two, second_bf


def learner_kernel(cfg, *refs):
    pieces, heads, roles = cfg["pieces"], cfg["heads"], cfg["roles"]
    xs, refs = refs[0], refs[1:]
    w_refs, refs = refs[: len(pieces)], refs[len(pieces) :]
    aux_ref, head_ref, refs = refs[0], refs[1], refs[2:]
    if roles is not None:
        refs = refs[2:]
    ws, pre, ghead_ref, own_ref, order_ref, first_ref, refs = *refs[:6], refs[6:]
    lead, (gp, sw) = refs[:-2], refs[-2:]
    learn, width, units, length = cfg["learn"], cfg["width"], cfg["units"], cfg["length"]
    envs = learn // length
    core, chip = where_am_i()

    if roles is None:
        pltpu.sync_copy(w_refs[0], ws)
        pre[...] = dot(ws[:, :width], xs[...], NT)
    else:
        each_piece(pieces, w_refs, ws, sw, lambda copy: copy.start())
        multiply_pieces(pieces, w_refs, xs, width, pre)
        each_piece(pieces, w_refs, ws, sw, lambda copy: copy.wait())
    pre_one = pre[...]
    out, pre_one, first_bf, pre_two, second_bf = forward(pre_one, ws[...], head_ref[...], width)
    own_ref[...] = out[: heads - 1, learn:].reshape(heads - 1, 1, envs)
    spread = lax.broadcasted_iota(jnp.int32, (envs, learn), 1) // length
    spread = (spread == lax.broadcasted_iota(jnp.int32, (envs, learn), 0)).astype(jnp.float32)
    boot = dot(out[:, learn:], spread, NN, lax.Precision.HIGHEST)[heads - 1 : heads]
    grad = trace_gradients(
        out[:, :learn], boot, aux_ref[...], heads - 1, length, 1.0 / length
    ).astype(jnp.bfloat16)
    ghead = dot(grad, second_bf[:, :learn], NT)
    ghead_ref[...] = ghead
    grad_second = dot(head_ref[...].T, grad, NN)
    grad_two = jnp.where(pre_two[:, :learn] > 0, grad_second, 0.0).astype(jnp.bfloat16)
    grad_first = grad_second + dot(ws[:, width:].T, grad_two, NN)
    grad_one = jnp.where(pre_one[:, :learn] > 0, grad_first, 0.0).astype(jnp.bfloat16)
    first_ref[...] = first_bf[:, :learn]

    if roles is None:
        order_ref[:, :learn] = grad_one
        order_ref[:, learn:] = grad_two
        return
    gp[:, :learn] = grad_one
    gp[:, learn:] = grad_two
    rows = units // (len(roles) * CORES)
    order = []
    for role in roles:
        for same in (False, True):
            owner = core if same else 1 - core
            start = pl.multiple_of((table(role, chip) * CORES + owner) * rows, rows)
            order.append(gp[pl.ds(start, rows), :])
    order_ref[...] = jnp.concatenate(order[CORES:], 0)
    for out in lead:
        out[:, width + units :] = ghead[:rows].astype(jnp.bfloat16)
    gradient_rows(jnp.concatenate(order[:CORES], 0), xs, first_ref, lead, learn, width, cfg["chunk"])


def gradient_rows(order, xs, first_ref, outs, learn, width, chunk):
    rows = outs[0].shape[0]

    def put(columns, value):
        value = value.astype(jnp.bfloat16)
        for i, out in enumerate(outs):
            out[:, columns] = value[i * rows : (i + 1) * rows]

    for start in range(0, width, chunk):
        columns = slice(start, start + chunk)
        put(columns, dot(order[:, :learn], xs[:learn, columns], NN))
    put(slice(width, width + first_ref.shape[0]), dot(order[:, learn:], first_ref[...], NT))


def rest_kernel(cfg, xs, order_ref, first_ref, *outs):
    gradient_rows(order_ref[...], xs, first_ref, outs, cfg["learn"], cfg["width"], cfg["chunk"])


def column_chunk(width):
    return max(c for c in range(128, 1153, 128) if width % c == 0)


def learner(staged, piece_list, aux, head, before, cfg):
    total, width, units, learn = staged.shape[0], cfg["width"], cfg["units"], cfg["learn"]
    padded = head.shape[0]
    cfg = dict(cfg, chunk=column_chunk(width))
    roles = cfg["roles"]
    block = lambda rows: jax.ShapeDtypeStruct((rows, width + units), jnp.bfloat16)
    inputs = 3 + len(piece_list)
    if roles is None:
        lead, rest, later, aliases = [], [block(units)], units, {}
    else:
        rows = units // (len(roles) * CORES)
        wider = jax.ShapeDtypeStruct((rows, width + 2 * units), jnp.bfloat16)
        lead, rest = [wider] * CORES, [block(rows)] * (CORES * (len(roles) - 1))
        later = units - CORES * rows
        aliases = {inputs: 0, inputs + 1: 1}
    weights, _, ghead, own, order, first, *first_outs = pl.pallas_call(
        functools.partial(learner_kernel, cfg),
        out_shape=(
            block(units),
            jax.ShapeDtypeStruct((units, total), jnp.float32),
            jax.ShapeDtypeStruct((padded, units), jnp.float32),
            jax.ShapeDtypeStruct((cfg["heads"] - 1, 1, total - learn), jnp.float32),
            jax.ShapeDtypeStruct((later, 2 * learn), jnp.bfloat16),
            jax.ShapeDtypeStruct((units, learn), jnp.bfloat16),
            *lead,
        ),
        in_specs=[LOCAL] + [ANYWHERE if roles is None else LOCAL] * len(piece_list)
        + [LOCAL] * (2 + len(before)),
        out_specs=(LOCAL,) * (6 + len(lead)),
        input_output_aliases=aliases,
        scratch_shapes=[
            pltpu.VMEM((units, 2 * learn), jnp.bfloat16),
            pltpu.SemaphoreType.DMA((len(piece_list),)),
        ],
        compiler_params=pltpu.CompilerParams(vmem_limit_bytes=32 << 20),
        cost_estimate=pl.CostEstimate(
            flops=4 * units * total * width, bytes_accessed=4 * total * width, transcendentals=0
        ),
        name="learner",
    )(staged, *piece_list, aux, head, *before)
    rest_outs = pl.pallas_call(
        functools.partial(rest_kernel, cfg),
        out_shape=tuple(rest),
        in_specs=[LOCAL] * 3,
        out_specs=(LOCAL,) * len(rest),
        compiler_params=pltpu.CompilerParams(vmem_limit_bytes=32 << 20),
        cost_estimate=pl.CostEstimate(
            flops=2 * later * learn * width, bytes_accessed=2 * learn * width, transcendentals=0
        ),
        name="rest",
    )(staged, order, first)
    return weights, ghead, own, first_outs, list(rest_outs)


def opponent_kernel(cfg, count, *refs):
    frames, (weights, head), refs = refs[:count], refs[count : count + 2], refs[count + 2 :]
    outs, (xs, sems) = refs[:count], refs[count:]
    envs = frames[0].shape[0]
    copies = [
        pltpu.make_async_copy(f, xs.at[pl.ds(i * envs, envs)], sems.at[i])
        for i, f in enumerate(frames)
    ]
    for copy in copies:
        copy.start()
    for copy in copies:
        copy.wait()
    width = cfg["width"]
    pre_one = dot(weights[:, :width], xs[...], NT)
    result = forward(pre_one, weights[...], head[...], width)[0].astype(jnp.bfloat16)
    for i, out in enumerate(outs):
        out[...] = result[:, i * envs : (i + 1) * envs]


def opponents(frames, weights, head, cfg):
    count, (envs, width) = len(frames), frames[0].shape
    return pl.pallas_call(
        functools.partial(opponent_kernel, cfg, count),
        out_shape=(jax.ShapeDtypeStruct((head.shape[0], envs), jnp.bfloat16),) * count,
        in_specs=[ANYWHERE] * count + [LOCAL] * 2,
        out_specs=(LOCAL,) * count,
        scratch_shapes=[
            pltpu.VMEM((count * envs, width), jnp.bfloat16),
            pltpu.SemaphoreType.DMA((count,)),
        ],
        compiler_params=pltpu.CompilerParams(vmem_limit_bytes=24 << 20),
        cost_estimate=pl.CostEstimate(
            flops=2 * cfg["units"] * count * envs * width,
            bytes_accessed=2 * count * envs * width,
            transcendentals=0,
        ),
        name="opponents",
    )(*frames, weights, head)


def other_agent(i, by, agents):
    return i ^ by if agents & (agents - 1) == 0 else (i + by) % agents


def choose_kernel(*refs):
    answers, ids, out = refs[:-2], refs[-2], refs[-1]
    agents, me = len(answers), lax.axis_index("agent")
    result = jnp.zeros(out.shape, jnp.float32)
    for by, answer in enumerate(answers):
        player = other_agent(me, by, agents)
        result = jnp.where(ids[...] == player, answer[: out.shape[0]].astype(jnp.float32), result)
    out[...] = result.astype(out.dtype)


def choose(answers, ids, count):
    return pl.pallas_call(
        choose_kernel,
        out_shape=jax.ShapeDtypeStruct((count, ids.shape[1]), jnp.bfloat16),
        in_specs=[LOCAL] * (len(answers) + 1),
        out_specs=LOCAL,
        compiler_params=pltpu.CompilerParams(vmem_limit_bytes=2 << 20),
        name="choose",
    )(*answers, ids)


def add_with_heads_kernel(count, units, *refs):
    ins, heads, out = refs[:count], refs[count:-1], refs[-1]
    width = out.shape[1] - units
    for columns, parts in ((slice(0, width), ins), (slice(width, width + units), heads)):
        total = sum(x[:, columns].astype(jnp.float32) for x in parts)
        out[:, columns] = total.astype(out.dtype)


def add_with_heads(arrays, heads, units):
    rows, wide = heads[0].shape
    return pl.pallas_call(
        functools.partial(add_with_heads_kernel, len(arrays), units),
        out_shape=jax.ShapeDtypeStruct((rows, wide), jnp.bfloat16),
        in_specs=[LOCAL] * (len(arrays) + len(heads)),
        out_specs=LOCAL,
        compiler_params=pltpu.CompilerParams(vmem_limit_bytes=4 << 20),
        cost_estimate=pl.CostEstimate(
            flops=rows * wide, bytes_accessed=2 * len(arrays) * rows * wide, transcendentals=0
        ),
        name="add",
    )(*arrays, *heads)


def adam_step(master, moment, second, grad, rate):
    moment = beta_first * moment + (1.0 - beta_first) * grad
    second = beta_second * second + (1.0 - beta_second) * grad * grad
    master = master - rate * moment / (jnp.sqrt(second) + adam_eps)
    return (master, moment, second)


def adam_kernel(parts, head_parts, cuts, *refs):
    rate = refs[0][...]
    parts, refs = refs[1 : 1 + parts], refs[1 + parts :]
    head_parts, refs = refs[:head_parts], refs[head_parts:]
    core, head, core_out, head_out = refs[:3], refs[3:6], refs[6:9], refs[9:12]
    stages, head_stages, sems, head_sems = refs[12:15], refs[15:18], refs[18], refs[19]
    count, _, units = head[0].shape
    if len(head_parts) == 1:
        grad = head_parts[0][:count]
    else:
        mine, mid, near, far = (
            x[:count, x.shape[1] - units :].astype(jnp.float32) for x in head_parts
        )
        _, chip = where_am_i()
        end = jnp.logical_or(chip == 0, chip == LINE - 1)
        rounded = lambda x: x.astype(jnp.bfloat16).astype(jnp.float32)
        pair = rounded(mine + jnp.where(end, near, far))
        grad = pair + jnp.where(end, far, rounded(mid + near))
    grad = grad.reshape(head[0].shape)
    copies = []
    for i, value in enumerate(adam_step(*(x[...] for x in head), grad, rate)):
        head_stages[i][...] = value
        copies.append(pltpu.make_async_copy(head_stages[i], head_out[i], head_sems.at[i]))
        copies[-1].start()
    for n, (start, stop) in enumerate(cuts):
        columns = slice(start, stop)
        grad = sum(part[:, columns].astype(jnp.float32) for part in parts)
        for i, value in enumerate(adam_step(*(x[:, columns] for x in core), grad, rate)):
            stages[i][:, columns] = value
            copies.append(
                pltpu.make_async_copy(
                    stages[i].at[:, columns], core_out[i].at[:, columns], sems.at[n, i]
                )
            )
            copies[-1].start()
    for copy in copies:
        copy.wait()


def adam(rates, parts, head_parts, core, head):
    rows, width = core[0].shape
    tiles, pieces = width // 128, 5
    edges = [128 * (tiles * n // pieces) for n in range(pieces)] + [width]
    cuts = list(zip(edges, edges[1:]))
    one = jax.ShapeDtypeStruct((rows, width), jnp.float32)
    small = jax.ShapeDtypeStruct(head[0].shape, jnp.float32)
    return pl.pallas_call(
        functools.partial(adam_kernel, len(parts), len(head_parts), cuts),
        out_shape=(one,) * 3 + (small,) * 3,
        in_specs=[LOCAL] * (len(parts) + len(head_parts) + 7),
        out_specs=(ANYWHERE,) * 6,
        scratch_shapes=[pltpu.VMEM((rows, width), jnp.float32)] * 3
        + [pltpu.VMEM(head[0].shape, jnp.float32)] * 3
        + [pltpu.SemaphoreType.DMA((len(cuts), 3)), pltpu.SemaphoreType.DMA((3,))],
        compiler_params=pltpu.CompilerParams(vmem_limit_bytes=16 << 20),
        cost_estimate=pl.CostEstimate(
            flops=20 * rows * width, bytes_accessed=32 * rows * width, transcendentals=0
        ),
        name="adam",
    )(rates.reshape(1, 1), *parts, *head_parts, *core, *head)


def per_device(
    learn_obs,
    own_obs,
    opp_obs,
    opponent,
    actions,
    done,
    rewards,
    behaviour,
    core_master,
    core_mom,
    core_vel,
    head_master,
    head_mom,
    head_vel,
    rates,
):
    envs, length, width = learn_obs.shape[1:]
    heads, units = head_master.shape[1:]
    action_count = heads - 1
    agents, members = lax.axis_size("agent"), lax.axis_size("dp")
    rows = core_master.shape[1]
    chips = members // CORES
    line = chips == LINE and members == LINE * CORES and units == members * rows and heads <= rows

    def along(x, pairs):
        return lax.ppermute(
            x, "dp", [(a * CORES + c, b * CORES + c) for a, b in pairs for c in range(CORES)]
        )

    def sibling(x):
        return lax.ppermute(x, "dp", [(i, i ^ 1) for i in range(members)])

    def swap(x, by):
        return lax.ppermute(x, "agent", [(i, other_agent(i, by, agents)) for i in range(agents)])

    mine = core_master[0].astype(jnp.bfloat16)
    if line:
        far = along(mine, GATHER_FAR)
        near = along(mine, GATHER_NEAR)
        mid = along(mine, GATHER_MID)
        onward = along(far, GATHER_FORWARD)
        first = (("mine", mine, SELF_FROM, None), ("far", far, FAR_FROM, None),
                 ("near", near, NEAR_FROM, None))
        final = (("mid", mid, LAST_FROM, (1, 2)), ("onward", onward, LAST_FROM, (0, 3)))

        def with_siblings(group):
            arrays = [g[1] for g in group] + [sibling(g[1]) for g in group]
            places = [(rows, g[2], same, g[3]) for same in (True, False) for g in group]
            return arrays, places

        (first_list, first_pieces), (piece_list, pieces) = with_siblings(first), with_siblings(final)
        roles = ROLES
    else:
        piece_list = [lax.all_gather(mine, "dp", axis=0, tiled=True)]
        pieces = [(units, None, True, None)]
        roles = None

    frames = [opp_obs[0]] + [swap(opp_obs[0], by) for by in range(1, agents)]

    by_row = lambda x: jnp.transpose(x, (1, 0, 2))
    cfg = dict(pieces=pieces, heads=heads, width=width, units=units, length=length, roles=roles,
               learn=envs * length)
    staged, aux, head = stage(
        learn_obs[0].reshape(envs * length, width),
        own_obs[0],
        [x[0].T for x in (actions, done, rewards, behaviour)],
        by_row(head_master),
    )
    before = ()
    if line:
        before = early(staged, first_pieces, first_list, units)
    weights, ghead, own, lead, rest = learner(staged, piece_list, aux, head, before, cfg)
    played = opponents(frames, weights, head, cfg)
    own_logits = jnp.transpose(own, (1, 2, 0))

    def undo(by):
        there = other_agent(0, by, agents)
        return next(b for b in range(agents) if other_agent(there, b, agents) == 0)

    answers = [played[0]] + [swap(played[by], undo(by)) for by in range(1, agents)]
    opp_logits = choose(answers, opponent[0].T, action_count)

    if line:
        blocks = lead + rest
        send, keep = blocks[::CORES], blocks[1::CORES]
        came = [sibling(b) for b in send]
        last = add_with_heads((keep[0], came[0]), (keep[0], came[0]), units)
        through = along(last, SCATTER_FORWARD)
        part_mid = along(last, SCATTER_MID)
        toward = add_with_heads((keep[1], came[1]), (last,), units)
        part_near = along(toward, SCATTER_NEAR)
        beyond = add_with_heads((keep[2], came[2], through), (last, through), units)
        part_far = along(beyond, SCATTER_FAR)
        core_parts = (keep[3], came[3], part_near, part_mid, part_far)
        head_parts = (last, part_mid, part_near, part_far)
    else:
        core_parts = (lax.psum_scatter(rest[0], "dp", scatter_dimension=0, tiled=True),)
        head_parts = (lax.psum(ghead, "dp"),)
    new = adam(
        rates,
        core_parts,
        head_parts,
        (core_master[0], core_mom[0], core_vel[0]),
        (by_row(head_master), by_row(head_mom), by_row(head_vel)),
    )
    return (own_logits, opp_logits.T[None], *[x[None] for x in new[:3]], *map(by_row, new[3:]))


def solution(mesh):
    sharded, whole = P("agent", "dp", None), P("agent", None, None)

    return jax.shard_map(
        per_device,
        mesh=mesh,
        in_specs=(P("agent", "dp", None, None),) + (sharded,) * 10 + (whole,) * 3 + (P("agent"),),
        out_specs=(sharded,) * 5 + (whole,) * 3,
        check_vma=False,
    )
```

```python
import functools

import jax
import jax.numpy as jnp
from jax import lax
from jax.experimental import pallas as pl
from jax.experimental.pallas import tpu as pltpu
from jax.sharding import PartitionSpec as P


gamma_rate = 0.99
baseline_cost = 0.5
entropy_cost = 0.05
beta_first = 0.9
beta_second = 0.99
adam_eps = 1e-08

CORES = 2
SUBLANES = 32

LINE = 4
GATHER_FAR = ((0, 2), (3, 1), (1, 0), (2, 3))
GATHER_NEAR = ((0, 1), (3, 2), (1, 3), (2, 0))
GATHER_MID = ((1, 2), (2, 1))
GATHER_FORWARD = ((2, 3), (1, 0))
FAR_FROM = (1, 3, 0, 2)
NEAR_FROM = (2, 0, 3, 1)
LAST_FROM = (3, 2, 1, 0)
SELF_FROM = (0, 1, 2, 3)
ROLES = (LAST_FROM, NEAR_FROM, FAR_FROM, SELF_FROM)
SCATTER_FORWARD = ((3, 2), (0, 1))
SCATTER_NEAR = tuple((b, a) for a, b in GATHER_NEAR)
SCATTER_MID = ((1, 2), (2, 1))
SCATTER_FAR = tuple((b, a) for a, b in GATHER_FAR)


def dot(left, right, dims, precision=None):
    return lax.dot_general(
        left, right, (dims, ((), ())), preferred_element_type=jnp.float32, precision=precision
    )


NN = ((1,), (0,))
NT = ((1,), (1,))


def table(values, index):
    result = jnp.int32(values[0])
    for place, value in enumerate(values[1:], 1):
        result = jnp.where(index == place, jnp.int32(value), result)
    return result


def trace_gradients(out, boot, aux, action_count, length, scale):
    rows, lanes = out.shape
    row = lax.broadcasted_iota(jnp.int32, (rows, lanes), 0)
    step = lax.rem(lax.broadcasted_iota(jnp.int32, (1, lanes), 1), length)
    last = step == length - 1
    policy = row < action_count
    actions, done, rewards, behaviour = (aux[i : i + 1] for i in range(4))
    values = out[action_count : action_count + 1]
    totals = jnp.sum(jnp.where(policy, jnp.exp(out), 0.0), 0, keepdims=True)
    logp = out - jnp.log(totals)
    probs = jnp.where(policy, jnp.exp(logp), 0.0)
    chosen = (row == actions.astype(jnp.int32)).astype(jnp.float32)
    picked = jnp.sum(logp * chosen, 0, keepdims=True)
    ratio = jnp.minimum(1.0, jnp.exp(picked - behaviour))
    discount = gamma_rate * (1.0 - done)
    following = lambda x, end: jnp.where(last, end, pltpu.roll(x, lanes - 1, 1))
    delta = ratio * (rewards + discount * following(values, boot) - values)
    factor = jnp.where(last, 0.0, discount * ratio)
    reach = 1
    while reach < length:
        delta = delta + factor * pltpu.roll(delta, lanes - reach, 1)
        factor = factor * pltpu.roll(factor, lanes - reach, 1)
        reach *= 2
    targets = values + delta
    advantage = ratio * (rewards + discount * following(targets, boot) - values)
    entropy = -jnp.sum(jnp.where(policy, probs * logp, 0.0), 0, keepdims=True)
    grad_logits = scale * (
        -advantage * (chosen - probs) + entropy_cost * probs * (logp + entropy)
    )
    grad_value = scale * (-baseline_cost * (targets - values))
    return jnp.where(policy, grad_logits, jnp.where(row == action_count, grad_value, 0.0))


ANYWHERE = pl.BlockSpec(memory_space=pl.ANY)
LOCAL = pl.BlockSpec(memory_space=pltpu.VMEM)


def in_hbm(arrays):
    return [pltpu.with_memory_space_constraint(x, pltpu.HBM) for x in arrays]


def stage_kernel(learn_ref, own_ref, *refs):
    small, (staged, aux, head_out), local, sems = refs[:5], refs[5:8], refs[8:13], refs[13]
    per_step, head_ref = local[:4], local[4]
    rows = learn_ref.shape[0]
    small_copies = [
        pltpu.make_async_copy(a, b, sems.at[2 + i]) for i, (a, b) in enumerate(zip(small, local))
    ]
    for copy in small_copies:
        copy.start()
    copies = (
        pltpu.make_async_copy(learn_ref, staged.at[pl.ds(0, rows)], sems.at[0]),
        pltpu.make_async_copy(own_ref, staged.at[pl.ds(rows, own_ref.shape[0])], sems.at[1]),
    )
    for copy in copies:
        copy.start()
    length, envs = per_step[0].shape
    lane = lax.broadcasted_iota(jnp.int32, (envs, rows), 1)
    spread = (lane // length == lax.broadcasted_iota(jnp.int32, (envs, rows), 0)).astype(
        jnp.float32
    )
    mask = lax.rem(lax.broadcasted_iota(jnp.int32, (length, rows), 1), length)
    mask = mask == lax.broadcasted_iota(jnp.int32, (length, rows), 0)
    for copy in small_copies:
        copy.wait()
    for i, ref in enumerate(per_step):
        wide = dot(ref[...].astype(jnp.float32), spread, NN, lax.Precision.HIGHEST)
        aux[i : i + 1] = jnp.sum(jnp.where(mask, wide, 0.0), 0, keepdims=True)
    heads, _, units = head_ref.shape
    head_out[...] = jnp.zeros_like(head_out)
    head_out[:heads] = head_ref[...].reshape(heads, units).astype(jnp.bfloat16)
    for copy in copies:
        copy.wait()


def stage(learn_rows, own_rows, per_step, head):
    rows, width = learn_rows.shape
    total = rows + own_rows.shape[0]
    heads, _, units = head.shape
    padded = -(-heads // SUBLANES) * SUBLANES
    return pl.pallas_call(
        stage_kernel,
        out_shape=(
            jax.ShapeDtypeStruct((total, width), jnp.bfloat16),
            jax.ShapeDtypeStruct((len(per_step), rows), jnp.float32),
            jax.ShapeDtypeStruct((padded, units), jnp.bfloat16),
        ),
        in_specs=[ANYWHERE] * 7,
        out_specs=(LOCAL,) * 3,
        scratch_shapes=[pltpu.VMEM(x.shape, x.dtype) for x in (*per_step, head)]
        + [pltpu.SemaphoreType.DMA((7,))],
        compiler_params=pltpu.CompilerParams(vmem_limit_bytes=8 << 20),
        cost_estimate=pl.CostEstimate(
            flops=0, bytes_accessed=4 * total * width, transcendentals=0
        ),
        name="stage",
    )(*in_hbm((learn_rows, own_rows, *per_step, head)))


def where_am_i():
    place = lax.axis_index("dp")
    return lax.rem(place, CORES), lax.div(place, CORES)


def piece_rows(piece):
    rows, source, same = piece
    core, chip = where_am_i()
    owner = core if same else 1 - core
    return pl.ds(pl.multiple_of((table(source, chip) * CORES + owner) * rows, rows), rows)


def each_piece(pieces, w_refs, ws, sems, act):
    for i, piece in enumerate(pieces):
        act(pltpu.make_async_copy(w_refs[i], ws.at[piece_rows(piece)], sems.at[i]))


def multiply_pieces(pieces, w_refs, xs, width, first, first_bf):
    result = dot(jnp.concatenate([ref[:, :width] for ref in w_refs], 0), xs[...], NT)
    result = jnp.maximum(result, 0.0)
    result_bf = result.astype(jnp.bfloat16)
    at = 0
    for piece in pieces:
        rows = piece_rows(piece)
        first[rows, :] = result[at : at + piece[0]]
        first_bf[rows, :] = result_bf[at : at + piece[0]]
        at += piece[0]


def early_kernel(pieces, width, xs, *refs):
    w_refs, (ws, first, first_bf, sems) = refs[: len(pieces)], refs[len(pieces) :]
    each_piece(pieces, w_refs, ws, sems, lambda copy: copy.start())
    multiply_pieces(pieces, w_refs, xs, width, first, first_bf)
    each_piece(pieces, w_refs, ws, sems, lambda copy: copy.wait())


def early(staged, pieces, piece_list, units):
    total, width = staged.shape
    return pl.pallas_call(
        functools.partial(early_kernel, pieces, width),
        out_shape=(
            jax.ShapeDtypeStruct((units, width + units), jnp.bfloat16),
            jax.ShapeDtypeStruct((units, total), jnp.float32),
            jax.ShapeDtypeStruct((units, total), jnp.bfloat16),
        ),
        in_specs=[LOCAL] * (1 + len(pieces)),
        out_specs=(LOCAL,) * 3,
        scratch_shapes=[pltpu.SemaphoreType.DMA((len(pieces),))],
        compiler_params=pltpu.CompilerParams(vmem_limit_bytes=24 << 20),
        cost_estimate=pl.CostEstimate(
            flops=2 * units * total * width, bytes_accessed=4 * units * width, transcendentals=0
        ),
        name="early",
    )(staged, *piece_list)


def forward(first, first_bf, weights, head, width):
    pre_two = dot(weights[:, width:], first_bf, NN)
    second_bf = (jnp.maximum(pre_two, 0.0) + first).astype(jnp.bfloat16)
    return dot(head, second_bf, NN), pre_two, second_bf


def learner_kernel(cfg, *refs):
    pieces, heads, roles = cfg["pieces"], cfg["heads"], cfg["roles"]
    xs, refs = refs[0], refs[1:]
    w_refs, refs = refs[: len(pieces)], refs[len(pieces) :]
    aux_ref, head_ref, refs = refs[0], refs[1], refs[2:]
    if roles is not None:
        refs = refs[3:]
    ws, first, first_bf, ghead_ref, own_ref, gp, refs = *refs[:6], refs[6:]
    lead, sw = refs[:-1], refs[-1]
    learn, width, units, length = cfg["learn"], cfg["width"], cfg["units"], cfg["length"]
    envs = learn // length

    if roles is None:
        pltpu.sync_copy(w_refs[0], ws)
        first[...] = jnp.maximum(dot(ws[:, :width], xs[...], NT), 0.0)
        first_bf[...] = first[...].astype(jnp.bfloat16)
    else:
        each_piece(pieces, w_refs, ws, sw, lambda copy: copy.start())
        multiply_pieces(pieces, w_refs, xs, width, first, first_bf)
        each_piece(pieces, w_refs, ws, sw, lambda copy: copy.wait())
    out, pre_two, second_bf = forward(first[...], first_bf[...], ws[...], head_ref[...], width)
    own_ref[...] = out[: heads - 1, learn:].reshape(heads - 1, 1, envs)
    spread = lax.broadcasted_iota(jnp.int32, (envs, learn), 1) // length
    spread = (spread == lax.broadcasted_iota(jnp.int32, (envs, learn), 0)).astype(jnp.float32)
    boot = dot(out[:, learn:], spread, NN, lax.Precision.HIGHEST)[heads - 1 : heads]
    grad = trace_gradients(
        out[:, :learn], boot, aux_ref[...], heads - 1, length, 1.0 / length
    ).astype(jnp.bfloat16)
    ghead = dot(grad, second_bf[:, :learn], NT)
    ghead_ref[...] = ghead
    grad_second = dot(head_ref[...].T, grad, NN)
    grad_two = jnp.where(pre_two[:, :learn] > 0, grad_second, 0.0).astype(jnp.bfloat16)
    grad_first = grad_second + dot(ws[:, width:].T, grad_two, NN)
    grad_one = jnp.where(first[:, :learn] > 0, grad_first, 0.0).astype(jnp.bfloat16)
    gp[:, :learn] = grad_one
    gp[:, learn:] = grad_two
    if roles is not None:
        for out in lead:
            out[:, width + units :] = ghead[: out.shape[0]].astype(jnp.bfloat16)
        order = role_rows(gp, roles[:1], lead[0].shape[0])
        gradient_rows(order, xs, first_bf, lead, learn, width, cfg["chunk"])


def role_rows(gp, roles, rows):
    parts = [gp[piece_rows((rows, role, same)), :] for role in roles for same in (False, True)]
    return jnp.concatenate(parts, 0)


def gradient_rows(order, xs, first_bf, outs, learn, width, chunk):
    rows = outs[0].shape[0]

    def put(columns, value):
        value = value.astype(jnp.bfloat16)
        for i, out in enumerate(outs):
            out[:, columns] = value[i * rows : (i + 1) * rows]

    for start in range(0, width, chunk):
        columns = slice(start, start + chunk)
        put(columns, dot(order[:, :learn], xs[:learn, columns], NN))
    columns = slice(width, width + first_bf.shape[0])
    put(columns, dot(order[:, learn:], first_bf[:, :learn], NT))


def rest_kernel(cfg, xs, gp, first_bf, *outs):
    roles = cfg["roles"]
    order = gp[...] if roles is None else role_rows(gp, roles[1:], outs[0].shape[0])
    gradient_rows(order, xs, first_bf, outs, cfg["learn"], cfg["width"], cfg["chunk"])


def column_chunk(width):
    return max(c for c in range(128, 1153, 128) if width % c == 0)


def learner(staged, piece_list, aux, head, before, cfg):
    total, width, units, learn = staged.shape[0], cfg["width"], cfg["units"], cfg["learn"]
    padded = head.shape[0]
    cfg = dict(cfg, chunk=column_chunk(width))
    roles = cfg["roles"]
    block = lambda rows: jax.ShapeDtypeStruct((rows, width + units), jnp.bfloat16)
    inputs = 3 + len(piece_list)
    if roles is None:
        lead, rest, aliases = [], [block(units)], {}
    else:
        rows = units // (len(roles) * CORES)
        wider = jax.ShapeDtypeStruct((rows, width + 2 * units), jnp.bfloat16)
        lead, rest = [wider] * CORES, [block(rows)] * (CORES * (len(roles) - 1))
        aliases = {inputs + i: i for i in range(len(before))}
    weights, _, first_bf, ghead, own, gp, *first_outs = pl.pallas_call(
        functools.partial(learner_kernel, cfg),
        out_shape=(
            block(units),
            jax.ShapeDtypeStruct((units, total), jnp.float32),
            jax.ShapeDtypeStruct((units, total), jnp.bfloat16),
            jax.ShapeDtypeStruct((padded, units), jnp.float32),
            jax.ShapeDtypeStruct((cfg["heads"] - 1, 1, total - learn), jnp.float32),
            jax.ShapeDtypeStruct((units, 2 * learn), jnp.bfloat16),
            *lead,
        ),
        in_specs=[LOCAL] + [ANYWHERE if roles is None else LOCAL] * len(piece_list)
        + [LOCAL] * (2 + len(before)),
        out_specs=(LOCAL,) * (6 + len(lead)),
        input_output_aliases=aliases,
        scratch_shapes=[pltpu.SemaphoreType.DMA((len(piece_list),))],
        compiler_params=pltpu.CompilerParams(vmem_limit_bytes=32 << 20),
        cost_estimate=pl.CostEstimate(
            flops=4 * units * total * width, bytes_accessed=4 * total * width, transcendentals=0
        ),
        name="learner",
    )(staged, *piece_list, aux, head, *before)
    rest_outs = pl.pallas_call(
        functools.partial(rest_kernel, cfg),
        out_shape=tuple(rest),
        in_specs=[LOCAL] * 3,
        out_specs=(LOCAL,) * len(rest),
        compiler_params=pltpu.CompilerParams(vmem_limit_bytes=32 << 20),
        cost_estimate=pl.CostEstimate(
            flops=2 * units * learn * width, bytes_accessed=2 * learn * width, transcendentals=0
        ),
        name="rest",
    )(staged, gp, first_bf)
    return weights, ghead, own, first_outs, list(rest_outs)


def opponent_kernel(cfg, count, *refs):
    frames, (weights, head), refs = refs[:count], refs[count : count + 2], refs[count + 2 :]
    outs, (xs, sems) = refs[:count], refs[count:]
    envs = frames[0].shape[0]
    copies = [
        pltpu.make_async_copy(f, xs.at[pl.ds(i * envs, envs)], sems.at[i])
        for i, f in enumerate(frames)
    ]
    for copy in copies:
        copy.start()
    for copy in copies:
        copy.wait()
    width = cfg["width"]
    first = jnp.maximum(dot(weights[:, :width], xs[...], NT), 0.0)
    first_bf = first.astype(jnp.bfloat16)
    result = forward(first, first_bf, weights[...], head[...], width)[0].astype(jnp.bfloat16)
    for i, out in enumerate(outs):
        out[...] = result[:, i * envs : (i + 1) * envs]


def opponents(frames, weights, head, cfg):
    count, (envs, width) = len(frames), frames[0].shape
    return pl.pallas_call(
        functools.partial(opponent_kernel, cfg, count),
        out_shape=(jax.ShapeDtypeStruct((head.shape[0], envs), jnp.bfloat16),) * count,
        in_specs=[ANYWHERE] * count + [LOCAL] * 2,
        out_specs=(LOCAL,) * count,
        scratch_shapes=[
            pltpu.VMEM((count * envs, width), jnp.bfloat16),
            pltpu.SemaphoreType.DMA((count,)),
        ],
        compiler_params=pltpu.CompilerParams(vmem_limit_bytes=24 << 20),
        cost_estimate=pl.CostEstimate(
            flops=2 * cfg["units"] * count * envs * width,
            bytes_accessed=2 * count * envs * width,
            transcendentals=0,
        ),
        name="opponents",
    )(*frames, weights, head)


def other_agent(i, by, agents):
    return i ^ by if agents & (agents - 1) == 0 else (i + by) % agents


def choose_kernel(*refs):
    answers, ids, out = refs[:-2], refs[-2], refs[-1]
    agents, me = len(answers), lax.axis_index("agent")
    result = jnp.zeros(out.shape, jnp.float32)
    for by, answer in enumerate(answers):
        player = other_agent(me, by, agents)
        result = jnp.where(ids[...] == player, answer[: out.shape[0]].astype(jnp.float32), result)
    out[...] = result.astype(out.dtype)


def choose(answers, ids, count):
    return pl.pallas_call(
        choose_kernel,
        out_shape=jax.ShapeDtypeStruct((count, ids.shape[1]), jnp.bfloat16),
        in_specs=[LOCAL] * (len(answers) + 1),
        out_specs=LOCAL,
        compiler_params=pltpu.CompilerParams(vmem_limit_bytes=2 << 20),
        name="choose",
    )(*answers, ids)


def add_kernel(*refs):
    total = sum(x[...].astype(jnp.float32) for x in refs[:-1])
    refs[-1][...] = total.astype(refs[-1].dtype)


def add(*arrays):
    return pl.pallas_call(
        add_kernel,
        out_shape=jax.ShapeDtypeStruct(arrays[0].shape, arrays[0].dtype),
        in_specs=[LOCAL] * len(arrays),
        out_specs=LOCAL,
        compiler_params=pltpu.CompilerParams(vmem_limit_bytes=4 << 20),
        cost_estimate=pl.CostEstimate(
            flops=arrays[0].size, bytes_accessed=6 * arrays[0].size, transcendentals=0
        ),
        name="add",
    )(*arrays)


def add_with_heads_kernel(count, units, *refs):
    ins, heads, out = refs[:count], refs[count:-1], refs[-1]
    width = out.shape[1] - units
    for columns, parts in ((slice(0, width), ins), (slice(width, width + units), heads)):
        total = sum(x[:, columns].astype(jnp.float32) for x in parts)
        out[:, columns] = total.astype(out.dtype)


def add_with_heads(arrays, heads, units):
    rows, wide = heads[0].shape
    return pl.pallas_call(
        functools.partial(add_with_heads_kernel, len(arrays), units),
        out_shape=jax.ShapeDtypeStruct((rows, wide), jnp.bfloat16),
        in_specs=[LOCAL] * (len(arrays) + len(heads)),
        out_specs=LOCAL,
        compiler_params=pltpu.CompilerParams(vmem_limit_bytes=4 << 20),
        cost_estimate=pl.CostEstimate(
            flops=rows * wide, bytes_accessed=2 * len(arrays) * rows * wide, transcendentals=0
        ),
        name="add",
    )(*arrays, *heads)


def adam_step(master, moment, second, grad, rate):
    moment = beta_first * moment + (1.0 - beta_first) * grad
    second = beta_second * second + (1.0 - beta_second) * grad * grad
    master = master - rate * moment / (jnp.sqrt(second) + adam_eps)
    return (master, moment, second)


def adam_kernel(parts, head_parts, cuts, *refs):
    rate = refs[0][...]
    parts, refs = refs[1 : 1 + parts], refs[1 + parts :]
    head_parts, refs = refs[:head_parts], refs[head_parts:]
    core, head, core_out, head_out = refs[:3], refs[3:6], refs[6:9], refs[9:12]
    stages, head_stages, sems, head_sems = refs[12:15], refs[15:18], refs[18], refs[19]
    count, _, units = head[0].shape
    if len(head_parts) == 1:
        grad = head_parts[0][:count]
    else:
        mine, mid, near, far = (
            x[:count, x.shape[1] - units :].astype(jnp.float32) for x in head_parts
        )
        _, chip = where_am_i()
        end = jnp.logical_or(chip == 0, chip == LINE - 1)
        rounded = lambda x: x.astype(jnp.bfloat16).astype(jnp.float32)
        pair = rounded(mine + jnp.where(end, near, far))
        grad = pair + jnp.where(end, far, rounded(mid + near))
    grad = grad.reshape(head[0].shape)
    copies = []
    for i, value in enumerate(adam_step(*(x[...] for x in head), grad, rate)):
        head_stages[i][...] = value
        copies.append(pltpu.make_async_copy(head_stages[i], head_out[i], head_sems.at[i]))
        copies[-1].start()
    for n, (start, stop) in enumerate(cuts):
        columns = slice(start, stop)
        grad = sum(part[:, columns].astype(jnp.float32) for part in parts)
        for i, value in enumerate(adam_step(*(x[:, columns] for x in core), grad, rate)):
            stages[i][:, columns] = value
            copies.append(
                pltpu.make_async_copy(
                    stages[i].at[:, columns], core_out[i].at[:, columns], sems.at[n, i]
                )
            )
            copies[-1].start()
    for copy in copies:
        copy.wait()


def adam(rates, parts, head_parts, core, head):
    rows, width = core[0].shape
    tiles, pieces = width // 128, 5
    edges = [128 * (tiles * n // pieces) for n in range(pieces)] + [width]
    cuts = list(zip(edges, edges[1:]))
    one = jax.ShapeDtypeStruct((rows, width), jnp.float32)
    small = jax.ShapeDtypeStruct(head[0].shape, jnp.float32)
    return pl.pallas_call(
        functools.partial(adam_kernel, len(parts), len(head_parts), cuts),
        out_shape=(one,) * 3 + (small,) * 3,
        in_specs=[LOCAL] * (len(parts) + len(head_parts) + 7),
        out_specs=(ANYWHERE,) * 6,
        scratch_shapes=[pltpu.VMEM((rows, width), jnp.float32)] * 3
        + [pltpu.VMEM(head[0].shape, jnp.float32)] * 3
        + [pltpu.SemaphoreType.DMA((len(cuts), 3)), pltpu.SemaphoreType.DMA((3,))],
        compiler_params=pltpu.CompilerParams(vmem_limit_bytes=16 << 20),
        cost_estimate=pl.CostEstimate(
            flops=20 * rows * width, bytes_accessed=32 * rows * width, transcendentals=0
        ),
        name="adam",
    )(rates.reshape(1, 1), *parts, *head_parts, *core, *head)


def per_device(
    learn_obs,
    own_obs,
    opp_obs,
    opponent,
    actions,
    done,
    rewards,
    behaviour,
    core_master,
    core_mom,
    core_vel,
    head_master,
    head_mom,
    head_vel,
    rates,
):
    envs, length, width = learn_obs.shape[1:]
    heads, units = head_master.shape[1:]
    action_count = heads - 1
    agents, members = lax.axis_size("agent"), lax.axis_size("dp")
    rows = core_master.shape[1]
    chips = members // CORES
    line = chips == LINE and members == LINE * CORES and units == members * rows and heads <= rows

    def along(x, pairs):
        return lax.ppermute(
            x, "dp", [(a * CORES + c, b * CORES + c) for a, b in pairs for c in range(CORES)]
        )

    def sibling(x):
        return lax.ppermute(x, "dp", [(i, i ^ 1) for i in range(members)])

    def swap(x, by):
        return lax.ppermute(x, "agent", [(i, other_agent(i, by, agents)) for i in range(agents)])

    mine = core_master[0].astype(jnp.bfloat16)
    if line:
        far = along(mine, GATHER_FAR)
        near = along(mine, GATHER_NEAR)
        mid = along(mine, GATHER_MID)
        onward = along(far, GATHER_FORWARD)
        joined = add(mid, onward)
        got = [("mine", mine, SELF_FROM), ("far", far, FAR_FROM), ("near", near, NEAR_FROM),
               ("last", joined, LAST_FROM)]

        def with_siblings(group):
            arrays = [g[1] for g in group] + [sibling(g[1]) for g in group]
            return arrays, [(rows, g[2], same) for same in (True, False) for g in group]

        first_list, first_pieces = with_siblings(got[:-1])
        piece_list, pieces = with_siblings(got[-1:])
        roles = ROLES
    else:
        piece_list = [lax.all_gather(mine, "dp", axis=0, tiled=True)]
        pieces = [(units, None, True)]
        roles = None

    frames = [opp_obs[0]] + [swap(opp_obs[0], by) for by in range(1, agents)]

    by_row = lambda x: jnp.transpose(x, (1, 0, 2))
    cfg = dict(pieces=pieces, heads=heads, width=width, units=units, length=length, roles=roles,
               learn=envs * length)
    staged, aux, head = stage(
        learn_obs[0].reshape(envs * length, width),
        own_obs[0],
        [x[0].T for x in (actions, done, rewards, behaviour)],
        by_row(head_master),
    )
    before = ()
    if line:
        before = early(staged, first_pieces, first_list, units)
    weights, ghead, own, lead, rest = learner(staged, piece_list, aux, head, before, cfg)
    played = opponents(frames, weights, head, cfg)
    own_logits = jnp.transpose(own, (1, 2, 0))

    def undo(by):
        there = other_agent(0, by, agents)
        return next(b for b in range(agents) if other_agent(there, b, agents) == 0)

    answers = [played[0]] + [swap(played[by], undo(by)) for by in range(1, agents)]
    opp_logits = choose(answers, opponent[0].T, action_count)

    if line:
        blocks = lead + rest
        send, keep = blocks[::CORES], blocks[1::CORES]
        came = [sibling(b) for b in send]
        last = add_with_heads((keep[0], came[0]), (keep[0], came[0]), units)
        through = along(last, SCATTER_FORWARD)
        part_mid = along(last, SCATTER_MID)
        toward = add_with_heads((keep[1], came[1]), (last,), units)
        part_near = along(toward, SCATTER_NEAR)
        beyond = add_with_heads((keep[2], came[2], through), (last, through), units)
        part_far = along(beyond, SCATTER_FAR)
        core_parts = (keep[3], came[3], part_near, part_mid, part_far)
        head_parts = (last, part_mid, part_near, part_far)
    else:
        core_parts = (lax.psum_scatter(rest[0], "dp", scatter_dimension=0, tiled=True),)
        head_parts = (lax.psum(ghead, "dp"),)
    new = adam(
        rates,
        core_parts,
        head_parts,
        (core_master[0], core_mom[0], core_vel[0]),
        (by_row(head_master), by_row(head_mom), by_row(head_vel)),
    )
    return (own_logits, opp_logits.T[None], *[x[None] for x in new[:3]], *map(by_row, new[3:]))


def solution(mesh):
    sharded, whole = P("agent", "dp", None), P("agent", None, None)

    return jax.shard_map(
        per_device,
        mesh=mesh,
        in_specs=(P("agent", "dp", None, None),) + (sharded,) * 10 + (whole,) * 3 + (P("agent"),),
        out_specs=(sharded,) * 5 + (whole,) * 3,
        check_vma=False,
    )
```

```python
import functools

import jax
import jax.numpy as jnp
from jax import lax
from jax.experimental import pallas as pl
from jax.experimental.pallas import tpu as pltpu
from jax.sharding import PartitionSpec as P


gamma_rate = 0.99
baseline_cost = 0.5
entropy_cost = 0.05
beta_first = 0.9
beta_second = 0.99
adam_eps = 1e-08

CORES = 2
SUBLANES = 32

LINE = 4
GATHER_FAR = ((0, 2), (3, 1), (1, 0), (2, 3))
GATHER_NEAR = ((0, 1), (3, 2), (1, 3), (2, 0))
GATHER_MID = ((1, 2), (2, 1))
GATHER_FORWARD = ((2, 3), (1, 0))
FAR_FROM = (1, 3, 0, 2)
NEAR_FROM = (2, 0, 3, 1)
LAST_FROM = (3, 2, 1, 0)
SELF_FROM = (0, 1, 2, 3)
ROLES = (LAST_FROM, NEAR_FROM, FAR_FROM, SELF_FROM)
SCATTER_FORWARD = ((3, 2), (0, 1))
SCATTER_NEAR = tuple((b, a) for a, b in GATHER_NEAR)
SCATTER_MID = ((1, 2), (2, 1))
SCATTER_FAR = tuple((b, a) for a, b in GATHER_FAR)


def dot(left, right, dims, precision=None):
    return lax.dot_general(
        left, right, (dims, ((), ())), preferred_element_type=jnp.float32, precision=precision
    )


NN = ((1,), (0,))
NT = ((1,), (1,))


def table(values, index):
    result = jnp.int32(values[0])
    for place, value in enumerate(values[1:], 1):
        result = jnp.where(index == place, jnp.int32(value), result)
    return result


def trace_gradients(out, boot, aux, action_count, length, scale):
    rows, lanes = out.shape
    row = lax.broadcasted_iota(jnp.int32, (rows, lanes), 0)
    step = lax.rem(lax.broadcasted_iota(jnp.int32, (1, lanes), 1), length)
    last = step == length - 1
    policy = row < action_count
    actions, done, rewards, behaviour = (aux[i : i + 1] for i in range(4))
    values = out[action_count : action_count + 1]
    totals = jnp.sum(jnp.where(policy, jnp.exp(out), 0.0), 0, keepdims=True)
    logp = out - jnp.log(totals)
    probs = jnp.where(policy, jnp.exp(logp), 0.0)
    chosen = (row == actions.astype(jnp.int32)).astype(jnp.float32)
    picked = jnp.sum(logp * chosen, 0, keepdims=True)
    ratio = jnp.minimum(1.0, jnp.exp(picked - behaviour))
    discount = gamma_rate * (1.0 - done)
    following = lambda x, end: jnp.where(last, end, pltpu.roll(x, lanes - 1, 1))
    delta = ratio * (rewards + discount * following(values, boot) - values)
    factor = jnp.where(last, 0.0, discount * ratio)
    reach = 1
    while reach < length:
        delta = delta + factor * pltpu.roll(delta, lanes - reach, 1)
        factor = factor * pltpu.roll(factor, lanes - reach, 1)
        reach *= 2
    targets = values + delta
    advantage = ratio * (rewards + discount * following(targets, boot) - values)
    entropy = -jnp.sum(jnp.where(policy, probs * logp, 0.0), 0, keepdims=True)
    grad_logits = scale * (
        -advantage * (chosen - probs) + entropy_cost * probs * (logp + entropy)
    )
    grad_value = scale * (-baseline_cost * (targets - values))
    return jnp.where(policy, grad_logits, jnp.where(row == action_count, grad_value, 0.0))


ANYWHERE = pl.BlockSpec(memory_space=pl.ANY)
LOCAL = pl.BlockSpec(memory_space=pltpu.VMEM)


def in_hbm(arrays):
    return [pltpu.with_memory_space_constraint(x, pltpu.HBM) for x in arrays]


def stage_kernel(learn_ref, own_ref, *refs):
    small, (staged, aux, head_out), local, sems = refs[:5], refs[5:8], refs[8:13], refs[13]
    per_step, head_ref = local[:4], local[4]
    rows = learn_ref.shape[0]
    small_copies = [
        pltpu.make_async_copy(a, b, sems.at[2 + i]) for i, (a, b) in enumerate(zip(small, local))
    ]
    for copy in small_copies:
        copy.start()
    copies = (
        pltpu.make_async_copy(learn_ref, staged.at[pl.ds(0, rows)], sems.at[0]),
        pltpu.make_async_copy(own_ref, staged.at[pl.ds(rows, own_ref.shape[0])], sems.at[1]),
    )
    for copy in copies:
        copy.start()
    length, envs = per_step[0].shape
    lane = lax.broadcasted_iota(jnp.int32, (envs, rows), 1)
    spread = (lane // length == lax.broadcasted_iota(jnp.int32, (envs, rows), 0)).astype(
        jnp.float32
    )
    mask = lax.rem(lax.broadcasted_iota(jnp.int32, (length, rows), 1), length)
    mask = mask == lax.broadcasted_iota(jnp.int32, (length, rows), 0)
    for copy in small_copies:
        copy.wait()
    for i, ref in enumerate(per_step):
        wide = dot(ref[...].astype(jnp.float32), spread, NN, lax.Precision.HIGHEST)
        aux[i : i + 1] = jnp.sum(jnp.where(mask, wide, 0.0), 0, keepdims=True)
    heads, _, units = head_ref.shape
    head_out[...] = jnp.zeros_like(head_out)
    head_out[:heads] = head_ref[...].reshape(heads, units).astype(jnp.bfloat16)
    for copy in copies:
        copy.wait()


def stage(learn_rows, own_rows, per_step, head):
    rows, width = learn_rows.shape
    total = rows + own_rows.shape[0]
    heads, _, units = head.shape
    padded = -(-heads // SUBLANES) * SUBLANES
    return pl.pallas_call(
        stage_kernel,
        out_shape=(
            jax.ShapeDtypeStruct((total, width), jnp.bfloat16),
            jax.ShapeDtypeStruct((len(per_step), rows), jnp.float32),
            jax.ShapeDtypeStruct((padded, units), jnp.bfloat16),
        ),
        in_specs=[ANYWHERE] * 7,
        out_specs=(LOCAL,) * 3,
        scratch_shapes=[pltpu.VMEM(x.shape, x.dtype) for x in (*per_step, head)]
        + [pltpu.SemaphoreType.DMA((7,))],
        compiler_params=pltpu.CompilerParams(vmem_limit_bytes=8 << 20),
        cost_estimate=pl.CostEstimate(
            flops=0, bytes_accessed=4 * total * width, transcendentals=0
        ),
        name="stage",
    )(*in_hbm((learn_rows, own_rows, *per_step, head)))


def where_am_i():
    place = lax.axis_index("dp")
    return lax.rem(place, CORES), lax.div(place, CORES)


def piece_rows(piece):
    rows, source, same = piece
    core, chip = where_am_i()
    owner = core if same else 1 - core
    return pl.ds(pl.multiple_of((table(source, chip) * CORES + owner) * rows, rows), rows)


def each_piece(pieces, w_refs, ws, sems, act):
    for i, piece in enumerate(pieces):
        act(pltpu.make_async_copy(w_refs[i], ws.at[piece_rows(piece)], sems.at[i]))


def multiply_pieces(pieces, w_refs, xs, width, first, first_bf):
    result = dot(jnp.concatenate([ref[:, :width] for ref in w_refs], 0), xs[...], NT)
    result = jnp.maximum(result, 0.0)
    result_bf = result.astype(jnp.bfloat16)
    at = 0
    for piece in pieces:
        rows = piece_rows(piece)
        first[rows, :] = result[at : at + piece[0]]
        first_bf[rows, :] = result_bf[at : at + piece[0]]
        at += piece[0]


def early_kernel(pieces, width, xs, *refs):
    w_refs, (ws, first, first_bf, sems) = refs[: len(pieces)], refs[len(pieces) :]
    each_piece(pieces, w_refs, ws, sems, lambda copy: copy.start())
    multiply_pieces(pieces, w_refs, xs, width, first, first_bf)
    each_piece(pieces, w_refs, ws, sems, lambda copy: copy.wait())


def early(staged, pieces, piece_list, units):
    total, width = staged.shape
    return pl.pallas_call(
        functools.partial(early_kernel, pieces, width),
        out_shape=(
            jax.ShapeDtypeStruct((units, width + units), jnp.bfloat16),
            jax.ShapeDtypeStruct((units, total), jnp.float32),
            jax.ShapeDtypeStruct((units, total), jnp.bfloat16),
        ),
        in_specs=[LOCAL] * (1 + len(pieces)),
        out_specs=(LOCAL,) * 3,
        scratch_shapes=[pltpu.SemaphoreType.DMA((len(pieces),))],
        compiler_params=pltpu.CompilerParams(vmem_limit_bytes=24 << 20),
        cost_estimate=pl.CostEstimate(
            flops=2 * units * total * width, bytes_accessed=4 * units * width, transcendentals=0
        ),
        name="early",
    )(staged, *piece_list)


def forward(first, first_bf, weights, head, width):
    pre_two = dot(weights[:, width:], first_bf, NN)
    second_bf = (jnp.maximum(pre_two, 0.0) + first).astype(jnp.bfloat16)
    return dot(head, second_bf, NN), pre_two, second_bf


def learner_kernel(cfg, *refs):
    pieces, heads, roles = cfg["pieces"], cfg["heads"], cfg["roles"]
    xs, refs = refs[0], refs[1:]
    w_refs, refs = refs[: len(pieces)], refs[len(pieces) :]
    aux_ref, head_ref, refs = refs[0], refs[1], refs[2:]
    if roles is not None:
        refs = refs[3:]
    ws, first, first_bf, own_ref, gp, refs = *refs[:5], refs[5:]
    lead, sw = refs[:-1], refs[-1]
    learn, width, units, length = cfg["learn"], cfg["width"], cfg["units"], cfg["length"]
    envs = learn // length

    if roles is None:
        pltpu.sync_copy(w_refs[0], ws)
        first[...] = jnp.maximum(dot(ws[:, :width], xs[...], NT), 0.0)
        first_bf[...] = first[...].astype(jnp.bfloat16)
    else:
        each_piece(pieces, w_refs, ws, sw, lambda copy: copy.start())
        multiply_pieces(pieces, w_refs, xs, width, first, first_bf)
        each_piece(pieces, w_refs, ws, sw, lambda copy: copy.wait())
    out, pre_two, second_bf = forward(first[...], first_bf[...], ws[...], head_ref[...], width)
    own_ref[...] = out[: heads - 1, learn:].reshape(heads - 1, 1, envs)
    spread = lax.broadcasted_iota(jnp.int32, (envs, learn), 1) // length
    spread = (spread == lax.broadcasted_iota(jnp.int32, (envs, learn), 0)).astype(jnp.float32)
    boot = dot(out[:, learn:], spread, NN, lax.Precision.HIGHEST)[heads - 1 : heads]
    grad = trace_gradients(
        out[:, :learn], boot, aux_ref[...], heads - 1, length, 1.0 / length
    ).astype(jnp.bfloat16)
    ghead = dot(grad, second_bf[:, :learn], NT)
    if roles is None:
        lead[0][...] = ghead
    grad_second = dot(head_ref[...].T, grad, NN)
    grad_two = jnp.where(pre_two[:, :learn] > 0, grad_second, 0.0).astype(jnp.bfloat16)
    grad_first = grad_second + dot(ws[:, width:].T, grad_two, NN)
    grad_one = jnp.where(first[:, :learn] > 0, grad_first, 0.0).astype(jnp.bfloat16)
    gp[:, :learn] = grad_one
    gp[:, learn:] = grad_two
    if roles is not None:
        for out in lead:
            out[:, width + units :] = ghead[: out.shape[0]].astype(jnp.bfloat16)
        order = role_rows(gp, roles[:1], lead[0].shape[0])
        gradient_rows(order, xs, first_bf, lead, learn, width, cfg["chunk"])


def role_rows(gp, roles, rows):
    parts = [gp[piece_rows((rows, role, same)), :] for role in roles for same in (False, True)]
    return jnp.concatenate(parts, 0)


def gradient_rows(order, xs, first_bf, outs, learn, width, chunk):
    rows = outs[0].shape[0]

    def put(columns, value):
        value = value.astype(jnp.bfloat16)
        for i, out in enumerate(outs):
            out[:, columns] = value[i * rows : (i + 1) * rows]

    for start in range(0, width, chunk):
        columns = slice(start, start + chunk)
        put(columns, dot(order[:, :learn], xs[:learn, columns], NN))
    columns = slice(width, width + first_bf.shape[0])
    put(columns, dot(order[:, learn:], first_bf[:, :learn], NT))


def rest_kernel(cfg, xs, gp, first_bf, *outs):
    roles = cfg["roles"]
    order = gp[...] if roles is None else role_rows(gp, roles[1:], outs[0].shape[0])
    gradient_rows(order, xs, first_bf, outs, cfg["learn"], cfg["width"], cfg["chunk"])


def column_chunk(width):
    return max(c for c in range(128, 1153, 128) if width % c == 0)


def learner(staged, piece_list, aux, head, before, cfg):
    total, width, units, learn = staged.shape[0], cfg["width"], cfg["units"], cfg["learn"]
    padded = head.shape[0]
    cfg = dict(cfg, chunk=column_chunk(width))
    roles = cfg["roles"]
    block = lambda rows: jax.ShapeDtypeStruct((rows, width + units), jnp.bfloat16)
    inputs = 3 + len(piece_list)
    if roles is None:
        lead, rest, aliases = [jax.ShapeDtypeStruct((padded, units), jnp.float32)], [block(units)], {}
    else:
        rows = units // (len(roles) * CORES)
        wider = jax.ShapeDtypeStruct((rows, width + 2 * units), jnp.bfloat16)
        lead, rest = [wider] * CORES, [block(rows)] * (CORES * (len(roles) - 1))
        aliases = {inputs + i: i for i in range(len(before))}
    weights, _, first_bf, own, gp, *first_outs = pl.pallas_call(
        functools.partial(learner_kernel, cfg),
        out_shape=(
            block(units),
            jax.ShapeDtypeStruct((units, total), jnp.float32),
            jax.ShapeDtypeStruct((units, total), jnp.bfloat16),
            jax.ShapeDtypeStruct((cfg["heads"] - 1, 1, total - learn), jnp.float32),
            jax.ShapeDtypeStruct((units, 2 * learn), jnp.bfloat16),
            *lead,
        ),
        in_specs=[LOCAL] + [ANYWHERE if roles is None else LOCAL] * len(piece_list)
        + [LOCAL] * (2 + len(before)),
        out_specs=(LOCAL,) * (5 + len(lead)),
        input_output_aliases=aliases,
        scratch_shapes=[pltpu.SemaphoreType.DMA((len(piece_list),))],
        compiler_params=pltpu.CompilerParams(vmem_limit_bytes=32 << 20),
        cost_estimate=pl.CostEstimate(
            flops=4 * units * total * width, bytes_accessed=4 * total * width, transcendentals=0
        ),
        name="learner",
    )(staged, *piece_list, aux, head, *before)
    rest_outs = pl.pallas_call(
        functools.partial(rest_kernel, cfg),
        out_shape=tuple(rest),
        in_specs=[LOCAL] * 3,
        out_specs=(LOCAL,) * len(rest),
        compiler_params=pltpu.CompilerParams(vmem_limit_bytes=32 << 20),
        cost_estimate=pl.CostEstimate(
            flops=2 * units * learn * width, bytes_accessed=2 * learn * width, transcendentals=0
        ),
        name="rest",
    )(staged, gp, first_bf)
    return weights, own, first_outs, list(rest_outs)


def opponent_kernel(cfg, count, *refs):
    frames, (weights, head), refs = refs[:count], refs[count : count + 2], refs[count + 2 :]
    outs, (xs, sems) = refs[:count], refs[count:]
    envs = frames[0].shape[0]
    copies = [
        pltpu.make_async_copy(f, xs.at[pl.ds(i * envs, envs)], sems.at[i])
        for i, f in enumerate(frames)
    ]
    for copy in copies:
        copy.start()
    for copy in copies:
        copy.wait()
    width = cfg["width"]
    first = jnp.maximum(dot(weights[:, :width], xs[...], NT), 0.0)
    first_bf = first.astype(jnp.bfloat16)
    result = forward(first, first_bf, weights[...], head[...], width)[0].astype(jnp.bfloat16)
    for i, out in enumerate(outs):
        out[...] = result[:, i * envs : (i + 1) * envs]


def opponents(frames, weights, head, cfg):
    count, (envs, width) = len(frames), frames[0].shape
    return pl.pallas_call(
        functools.partial(opponent_kernel, cfg, count),
        out_shape=(jax.ShapeDtypeStruct((head.shape[0], envs), jnp.bfloat16),) * count,
        in_specs=[ANYWHERE] * count + [LOCAL] * 2,
        out_specs=(LOCAL,) * count,
        scratch_shapes=[
            pltpu.VMEM((count * envs, width), jnp.bfloat16),
            pltpu.SemaphoreType.DMA((count,)),
        ],
        compiler_params=pltpu.CompilerParams(vmem_limit_bytes=24 << 20),
        cost_estimate=pl.CostEstimate(
            flops=2 * cfg["units"] * count * envs * width,
            bytes_accessed=2 * count * envs * width,
            transcendentals=0,
        ),
        name="opponents",
    )(*frames, weights, head)


def other_agent(i, by, agents):
    return i ^ by if agents & (agents - 1) == 0 else (i + by) % agents


def choose_kernel(*refs):
    answers, ids, out = refs[:-2], refs[-2], refs[-1]
    agents, me = len(answers), lax.axis_index("agent")
    result = jnp.zeros(out.shape, jnp.float32)
    for by, answer in enumerate(answers):
        player = other_agent(me, by, agents)
        result = jnp.where(ids[...] == player, answer[: out.shape[0]].astype(jnp.float32), result)
    out[...] = result.astype(out.dtype)


def choose(answers, ids, count):
    return pl.pallas_call(
        choose_kernel,
        out_shape=jax.ShapeDtypeStruct((count, ids.shape[1]), jnp.bfloat16),
        in_specs=[LOCAL] * (len(answers) + 1),
        out_specs=LOCAL,
        compiler_params=pltpu.CompilerParams(vmem_limit_bytes=2 << 20),
        name="choose",
    )(*answers, ids)


def total_of(refs, columns):
    return sum(x[:, columns].astype(jnp.float32) for x in refs)


def small_kernel(body, out_shape, args):
    bytes_accessed = sum(x.size * x.dtype.itemsize for x in args)
    return pl.pallas_call(
        body,
        out_shape=out_shape,
        in_specs=[LOCAL] * len(args),
        out_specs=jax.tree.map(lambda _: LOCAL, out_shape),
        compiler_params=pltpu.CompilerParams(vmem_limit_bytes=4 << 20),
        cost_estimate=pl.CostEstimate(
            flops=bytes_accessed, bytes_accessed=bytes_accessed, transcendentals=0
        ),
    )(*args)


def add(*arrays, dtype=jnp.bfloat16):
    width = min(x.shape[1] for x in arrays)

    def body(*refs):
        refs[-1][...] = total_of(refs[:-1], slice(0, width)).astype(dtype)

    shape = jax.ShapeDtypeStruct((arrays[0].shape[0], width), dtype)
    return small_kernel(body, shape, arrays)


def add_with_heads(arrays, heads, units, cut=None):
    rows, wide = heads[0].shape
    width = wide - units

    def body(*refs):
        ins, tops, outs = refs[: len(arrays)], refs[len(arrays) :][: len(heads)], refs[len(args) :]
        edges = [0, width] if cut is None else [0, cut, width]
        for out, start, stop in zip(outs, edges, edges[1:]):
            out[:, : stop - start] = total_of(ins, slice(start, stop)).astype(out.dtype)
        tail = slice(width, wide)
        outs[-1][:, width - edges[-2] :] = total_of(tops, tail).astype(outs[-1].dtype)

    args = (*arrays, *heads)
    widths = [wide] if cut is None else [cut, wide - cut]
    shape = [jax.ShapeDtypeStruct((rows, w), jnp.bfloat16) for w in widths]
    result = small_kernel(body, tuple(shape), args)
    return result[0] if cut is None else result


def adam_step(master, moment, second, grad, rate):
    moment = beta_first * moment + (1.0 - beta_first) * grad
    second = beta_second * second + (1.0 - beta_second) * grad * grad
    master = master - rate * moment / (jnp.sqrt(second) + adam_eps)
    return (master, moment, second)


def head_gradient(head_parts, count, units):
    if len(head_parts) == 1:
        return head_parts[0][:count]
    mine, mid, near, far = (x[:count, x.shape[1] - units :].astype(jnp.float32) for x in head_parts)
    _, chip = where_am_i()
    end = jnp.logical_or(chip == 0, chip == LINE - 1)
    rounded = lambda x: x.astype(jnp.bfloat16).astype(jnp.float32)
    pair = rounded(mine + jnp.where(end, near, far))
    return pair + jnp.where(end, far, rounded(mid + near))


def adam_kernel(parts, offsets, head_parts, prior, cuts, *refs):
    rate = refs[0][...]
    parts, refs = refs[1 : 1 + parts], refs[1 + parts :]
    head_parts, refs = refs[:head_parts], refs[head_parts:]
    heads = 3 if head_parts else 0
    core, head, refs = refs[:3], refs[3 : 3 + heads], refs[3 + heads + prior :]
    core_out, head_out, refs = refs[:3], refs[3 : 3 + heads], refs[3 + heads :]
    stages, head_stages, refs = refs[:3], refs[3 : 3 + heads], refs[3 + heads :]
    sems, copies = refs[0], []
    if heads:
        count, _, units = head[0].shape
        grad = head_gradient(head_parts, count, units).reshape(head[0].shape)
        for i, value in enumerate(adam_step(*(x[...] for x in head), grad, rate)):
            head_stages[i][...] = value
            copies.append(pltpu.make_async_copy(head_stages[i], head_out[i], refs[1].at[i]))
            copies[-1].start()
    for n, (start, stop) in enumerate(cuts):
        columns = slice(start, stop)
        grad = sum(
            part[:, start - offset : stop - offset].astype(jnp.float32)
            for part, offset in zip(parts, offsets)
        )
        for i, value in enumerate(adam_step(*(x[:, columns] for x in core), grad, rate)):
            stages[i][:, columns] = value
            copies.append(
                pltpu.make_async_copy(
                    stages[i].at[:, columns], core_out[i].at[:, columns], sems.at[n, i]
                )
            )
            copies[-1].start()
    for copy in copies:
        copy.wait()


def adam(rates, parts, head_parts, core, head, span, prior=()):
    rows, width = core[0].shape
    start, stop = span
    tiles = (stop - start) // 128
    pieces = max(1, tiles // 5)
    edges = [start + 128 * (tiles * n // pieces) for n in range(pieces)] + [stop]
    cuts = list(zip(edges, edges[1:]))
    arrays, offsets = [a for a, _ in parts], [o for _, o in parts]
    if not head_parts:
        head = ()
    one = jax.ShapeDtypeStruct((rows, width), jnp.float32)
    inputs = 1 + len(parts) + len(head_parts) + 3 + len(head)
    sems = [pltpu.SemaphoreType.DMA((len(cuts), 3))]
    if head:
        sems.append(pltpu.SemaphoreType.DMA((3,)))
    return pl.pallas_call(
        functools.partial(
            adam_kernel, len(parts), offsets, len(head_parts), len(prior), cuts
        ),
        out_shape=(one,) * 3 + tuple(jax.ShapeDtypeStruct(x.shape, jnp.float32) for x in head),
        in_specs=[LOCAL] * inputs + [ANYWHERE] * len(prior),
        out_specs=(ANYWHERE,) * (3 + len(head)),
        input_output_aliases={inputs + i: i for i in range(len(prior))},
        scratch_shapes=[pltpu.VMEM((rows, width), jnp.float32)] * 3
        + [pltpu.VMEM(x.shape, jnp.float32) for x in head]
        + sems,
        compiler_params=pltpu.CompilerParams(vmem_limit_bytes=12 << 20),
        cost_estimate=pl.CostEstimate(
            flops=20 * rows * (stop - start), bytes_accessed=32 * rows * (stop - start),
            transcendentals=0,
        ),
        name="adam",
    )(rates.reshape(1, 1), *arrays, *head_parts, *core, *head, *prior)


def per_device(
    learn_obs,
    own_obs,
    opp_obs,
    opponent,
    actions,
    done,
    rewards,
    behaviour,
    core_master,
    core_mom,
    core_vel,
    head_master,
    head_mom,
    head_vel,
    rates,
):
    envs, length, width = learn_obs.shape[1:]
    heads, units = head_master.shape[1:]
    action_count = heads - 1
    agents, members = lax.axis_size("agent"), lax.axis_size("dp")
    rows = core_master.shape[1]
    chips = members // CORES
    line = chips == LINE and members == LINE * CORES and units == members * rows and heads <= rows
    wide = jnp.float32

    def along(x, pairs):
        return lax.ppermute(
            x, "dp", [(a * CORES + c, b * CORES + c) for a, b in pairs for c in range(CORES)]
        )

    def sibling(x):
        return lax.ppermute(x, "dp", [(i, i ^ 1) for i in range(members)])

    def swap(x, by):
        return lax.ppermute(x, "agent", [(i, other_agent(i, by, agents)) for i in range(agents)])

    mine = core_master[0].astype(jnp.bfloat16)
    if line:
        far = along(mine, GATHER_FAR)
        near = along(mine, GATHER_NEAR)
        mid = along(mine, GATHER_MID)
        onward = along(far, GATHER_FORWARD)
        joined = add(mid, onward)
        got = [("mine", mine, SELF_FROM), ("far", far, FAR_FROM), ("near", near, NEAR_FROM),
               ("last", joined, LAST_FROM)]

        def with_siblings(group):
            arrays = [g[1] for g in group] + [sibling(g[1]) for g in group]
            return arrays, [(rows, g[2], same) for same in (True, False) for g in group]

        first_list, first_pieces = with_siblings(got[:-1])
        piece_list, pieces = with_siblings(got[-1:])
        roles = ROLES
    else:
        piece_list = [lax.all_gather(mine, "dp", axis=0, tiled=True)]
        pieces = [(units, None, True)]
        roles = None

    frames = [opp_obs[0]] + [swap(opp_obs[0], by) for by in range(1, agents)]

    by_row = lambda x: jnp.transpose(x, (1, 0, 2))
    cfg = dict(pieces=pieces, heads=heads, width=width, units=units, length=length, roles=roles,
               learn=envs * length)
    staged, aux, head = stage(
        learn_obs[0].reshape(envs * length, width),
        own_obs[0],
        [x[0].T for x in (actions, done, rewards, behaviour)],
        by_row(head_master),
    )
    before = ()
    if line:
        before = early(staged, first_pieces, first_list, units)
    weights, own, lead, rest = learner(staged, piece_list, aux, head, before, cfg)
    played = opponents(frames, weights, head, cfg)
    own_logits = jnp.transpose(own, (1, 2, 0))

    def undo(by):
        there = other_agent(0, by, agents)
        return next(b for b in range(agents) if other_agent(there, b, agents) == 0)

    answers = [played[0]] + [swap(played[by], undo(by)) for by in range(1, agents)]
    opp_logits = choose(answers, opponent[0].T, action_count)

    if line:
        blocks = lead + rest
        send, keep = blocks[::CORES], blocks[1::CORES]
        came = [sibling(b) for b in send]
        last = add_with_heads((keep[0], came[0]), (keep[0], came[0]), units)
        through = along(last, SCATTER_FORWARD)
        part_mid = along(last, SCATTER_MID)
        toward = add_with_heads((keep[1], came[1]), (last,), units)
        part_near = along(toward, SCATTER_NEAR)
        cut = 128 * (5 * (width + units) // (8 * 128))
        beyond = add_with_heads((keep[2], came[2], through), (last, through), units, cut)
        part_far = [along(b, SCATTER_FAR) for b in beyond]
        known = add(keep[3], came[3], part_near, part_mid, dtype=wide)
        spans = ((0, cut), (cut, width + units))
        parts = [((known, 0), (far, at)) for far, (at, _) in zip(part_far, spans)]
        head_parts = (last, part_mid, part_near, part_far[1])
    else:
        spans = ((0, width + units),)
        total = lax.psum_scatter(rest[0], "dp", scatter_dimension=0, tiled=True)
        parts, head_parts = [((total, 0),)], (lax.psum(lead[0], "dp"),)
    core = (core_master[0], core_mom[0], core_vel[0])
    head = (by_row(head_master), by_row(head_mom), by_row(head_vel))
    new = ()
    for span, part in zip(spans, parts):
        final = span is spans[-1]
        new = adam(rates, part, head_parts if final else (), core, head, span, new)
    return (own_logits, opp_logits.T[None], *[x[None] for x in new[:3]], *map(by_row, new[3:]))


def solution(mesh):
    sharded, whole = P("agent", "dp", None), P("agent", None, None)

    return jax.shard_map(
        per_device,
        mesh=mesh,
        in_specs=(P("agent", "dp", None, None),) + (sharded,) * 10 + (whole,) * 3 + (P("agent"),),
        out_specs=(sharded,) * 5 + (whole,) * 3,
        check_vma=False,
    )
```

```python
import functools

import jax
import jax.numpy as jnp
from jax import lax
from jax.experimental import pallas as pl
from jax.experimental.pallas import tpu as pltpu
from jax.sharding import PartitionSpec as P


gamma_rate = 0.99
baseline_cost = 0.5
entropy_cost = 0.05
beta_first = 0.9
beta_second = 0.99
adam_eps = 1e-08

CORES = 2
SUBLANES = 32

LINE = 4
GATHER_FAR = ((0, 2), (3, 1), (1, 0), (2, 3))
GATHER_NEAR = ((0, 1), (3, 2), (1, 3), (2, 0))
GATHER_MID = ((1, 2), (2, 1))
GATHER_FORWARD = ((2, 3), (1, 0))
FAR_FROM = (1, 3, 0, 2)
NEAR_FROM = (2, 0, 3, 1)
LAST_FROM = (3, 2, 1, 0)
SELF_FROM = (0, 1, 2, 3)
ROLES = (LAST_FROM, NEAR_FROM, FAR_FROM, SELF_FROM)
SCATTER_FORWARD = ((3, 2), (0, 1))
SCATTER_NEAR = tuple((b, a) for a, b in GATHER_NEAR)
SCATTER_MID = ((1, 2), (2, 1))
SCATTER_FAR = tuple((b, a) for a, b in GATHER_FAR)


def dot(left, right, dims, precision=None):
    return lax.dot_general(
        left, right, (dims, ((), ())), preferred_element_type=jnp.float32, precision=precision
    )


NN = ((1,), (0,))
NT = ((1,), (1,))


def table(values, index):
    result = jnp.int32(values[0])
    for place, value in enumerate(values[1:], 1):
        result = jnp.where(index == place, jnp.int32(value), result)
    return result


def trace_gradients(out, boot, aux, action_count, length, scale):
    rows, lanes = out.shape
    row = lax.broadcasted_iota(jnp.int32, (rows, lanes), 0)
    step = lax.rem(lax.broadcasted_iota(jnp.int32, (1, lanes), 1), length)
    last = step == length - 1
    policy = row < action_count
    actions, done, rewards, behaviour = (aux[i : i + 1] for i in range(4))
    values = out[action_count : action_count + 1]
    totals = jnp.sum(jnp.where(policy, jnp.exp(out), 0.0), 0, keepdims=True)
    logp = out - jnp.log(totals)
    probs = jnp.where(policy, jnp.exp(logp), 0.0)
    chosen = (row == actions.astype(jnp.int32)).astype(jnp.float32)
    picked = jnp.sum(logp * chosen, 0, keepdims=True)
    ratio = jnp.minimum(1.0, jnp.exp(picked - behaviour))
    discount = gamma_rate * (1.0 - done)
    following = lambda x, end: jnp.where(last, end, pltpu.roll(x, lanes - 1, 1))
    delta = ratio * (rewards + discount * following(values, boot) - values)
    factor = jnp.where(last, 0.0, discount * ratio)
    reach = 1
    while reach < length:
        delta = delta + factor * pltpu.roll(delta, lanes - reach, 1)
        factor = factor * pltpu.roll(factor, lanes - reach, 1)
        reach *= 2
    targets = values + delta
    advantage = ratio * (rewards + discount * following(targets, boot) - values)
    entropy = -jnp.sum(jnp.where(policy, probs * logp, 0.0), 0, keepdims=True)
    grad_logits = scale * (
        -advantage * (chosen - probs) + entropy_cost * probs * (logp + entropy)
    )
    grad_value = scale * (-baseline_cost * (targets - values))
    return jnp.where(policy, grad_logits, jnp.where(row == action_count, grad_value, 0.0))


ANYWHERE = pl.BlockSpec(memory_space=pl.ANY)
LOCAL = pl.BlockSpec(memory_space=pltpu.VMEM)


def in_hbm(arrays):
    return [pltpu.with_memory_space_constraint(x, pltpu.HBM) for x in arrays]


def stage_kernel(learn_ref, own_ref, *refs):
    small, (staged, aux, head_out), local, sems = refs[:5], refs[5:8], refs[8:13], refs[13]
    per_step, head_ref = local[:4], local[4]
    rows = learn_ref.shape[0]
    small_copies = [
        pltpu.make_async_copy(a, b, sems.at[2 + i]) for i, (a, b) in enumerate(zip(small, local))
    ]
    for copy in small_copies:
        copy.start()
    copies = (
        pltpu.make_async_copy(learn_ref, staged.at[pl.ds(0, rows)], sems.at[0]),
        pltpu.make_async_copy(own_ref, staged.at[pl.ds(rows, own_ref.shape[0])], sems.at[1]),
    )
    for copy in copies:
        copy.start()
    length, envs = per_step[0].shape
    lane = lax.broadcasted_iota(jnp.int32, (envs, rows), 1)
    spread = (lane // length == lax.broadcasted_iota(jnp.int32, (envs, rows), 0)).astype(
        jnp.float32
    )
    mask = lax.rem(lax.broadcasted_iota(jnp.int32, (length, rows), 1), length)
    mask = mask == lax.broadcasted_iota(jnp.int32, (length, rows), 0)
    for copy in small_copies:
        copy.wait()
    for i, ref in enumerate(per_step):
        wide = dot(ref[...].astype(jnp.float32), spread, NN, lax.Precision.HIGHEST)
        aux[i : i + 1] = jnp.sum(jnp.where(mask, wide, 0.0), 0, keepdims=True)
    heads, _, units = head_ref.shape
    head_out[...] = jnp.zeros_like(head_out)
    head_out[:heads] = head_ref[...].reshape(heads, units).astype(jnp.bfloat16)
    for copy in copies:
        copy.wait()


def stage(learn_rows, own_rows, per_step, head):
    rows, width = learn_rows.shape
    total = rows + own_rows.shape[0]
    heads, _, units = head.shape
    padded = -(-heads // SUBLANES) * SUBLANES
    return pl.pallas_call(
        stage_kernel,
        out_shape=(
            jax.ShapeDtypeStruct((total, width), jnp.bfloat16),
            jax.ShapeDtypeStruct((len(per_step), rows), jnp.float32),
            jax.ShapeDtypeStruct((padded, units), jnp.bfloat16),
        ),
        in_specs=[ANYWHERE] * 7,
        out_specs=(LOCAL,) * 3,
        scratch_shapes=[pltpu.VMEM(x.shape, x.dtype) for x in (*per_step, head)]
        + [pltpu.SemaphoreType.DMA((7,))],
        compiler_params=pltpu.CompilerParams(vmem_limit_bytes=8 << 20),
        cost_estimate=pl.CostEstimate(
            flops=0, bytes_accessed=4 * total * width, transcendentals=0
        ),
        name="stage",
    )(*in_hbm((learn_rows, own_rows, *per_step, head)))


def where_am_i():
    place = lax.axis_index("dp")
    return lax.rem(place, CORES), lax.div(place, CORES)


def piece_rows(piece):
    rows, source, same = piece
    core, chip = where_am_i()
    owner = core if same else 1 - core
    return pl.ds(pl.multiple_of((table(source, chip) * CORES + owner) * rows, rows), rows)


def place_pieces(pieces, w_refs, ws):
    for piece, ref in zip(pieces, w_refs):
        ws[piece_rows(piece), :] = ref[...]


def multiply_pieces(pieces, w_refs, xs, width, first, first_bf):
    result = dot(jnp.concatenate([ref[:, :width] for ref in w_refs], 0), xs[...], NT)
    result = jnp.maximum(result, 0.0)
    result_bf = result.astype(jnp.bfloat16)
    at = 0
    for piece in pieces:
        rows = piece_rows(piece)
        first[rows, :] = result[at : at + piece[0]]
        first_bf[rows, :] = result_bf[at : at + piece[0]]
        at += piece[0]


def early_kernel(pieces, width, xs, *refs):
    w_refs, (ws, first, first_bf) = refs[: len(pieces)], refs[len(pieces) :]
    place_pieces(pieces, w_refs, ws)
    multiply_pieces(pieces, w_refs, xs, width, first, first_bf)


def early(staged, pieces, piece_list, units):
    total, width = staged.shape
    return pl.pallas_call(
        functools.partial(early_kernel, pieces, width),
        out_shape=(
            jax.ShapeDtypeStruct((units, width + units), jnp.bfloat16),
            jax.ShapeDtypeStruct((units, total), jnp.float32),
            jax.ShapeDtypeStruct((units, total), jnp.bfloat16),
        ),
        in_specs=[LOCAL] * (1 + len(pieces)),
        out_specs=(LOCAL,) * 3,
        compiler_params=pltpu.CompilerParams(vmem_limit_bytes=24 << 20),
        cost_estimate=pl.CostEstimate(
            flops=2 * units * total * width, bytes_accessed=4 * units * width, transcendentals=0
        ),
        name="early",
    )(staged, *piece_list)


def forward(first, first_bf, weights, head, width):
    pre_two = dot(weights[:, width:], first_bf, NN)
    second_bf = (jnp.maximum(pre_two, 0.0) + first).astype(jnp.bfloat16)
    return dot(head, second_bf, NN), pre_two, second_bf


def learner_kernel(cfg, *refs):
    pieces, heads, roles = cfg["pieces"], cfg["heads"], cfg["roles"]
    xs, refs = refs[0], refs[1:]
    w_refs, refs = refs[: len(pieces)], refs[len(pieces) :]
    aux_ref, head_ref, refs = refs[0], refs[1], refs[2:]
    if roles is not None:
        refs = refs[3:]
    ws, first, first_bf, own_ref, gp, lead = *refs[:5], refs[5:]
    learn, width, units, length = cfg["learn"], cfg["width"], cfg["units"], cfg["length"]
    envs = learn // length

    if roles is None:
        pltpu.sync_copy(w_refs[0], ws)
        first[...] = jnp.maximum(dot(ws[:, :width], xs[...], NT), 0.0)
        first_bf[...] = first[...].astype(jnp.bfloat16)
    else:
        place_pieces(pieces, w_refs, ws)
        multiply_pieces(pieces, w_refs, xs, width, first, first_bf)
    out, pre_two, second_bf = forward(first[...], first_bf[...], ws[...], head_ref[...], width)
    own_ref[...] = out[: heads - 1, learn:].reshape(heads - 1, 1, envs)
    spread = lax.broadcasted_iota(jnp.int32, (envs, learn), 1) // length
    spread = (spread == lax.broadcasted_iota(jnp.int32, (envs, learn), 0)).astype(jnp.float32)
    boot = dot(out[:, learn:], spread, NN, lax.Precision.HIGHEST)[heads - 1 : heads]
    grad = trace_gradients(
        out[:, :learn], boot, aux_ref[...], heads - 1, length, 1.0 / length
    ).astype(jnp.bfloat16)
    ghead = dot(grad, second_bf[:, :learn], NT)
    if roles is None:
        lead[0][...] = ghead
    grad_second = dot(head_ref[...].T, grad, NN)
    grad_two = jnp.where(pre_two[:, :learn] > 0, grad_second, 0.0).astype(jnp.bfloat16)
    grad_first = grad_second + dot(ws[:, width:].T, grad_two, NN)
    grad_one = jnp.where(first[:, :learn] > 0, grad_first, 0.0).astype(jnp.bfloat16)
    gp[:, :learn] = grad_one
    gp[:, learn:] = grad_two
    if roles is not None:
        for out in lead:
            out[:, width + units :] = ghead[: out.shape[0]].astype(jnp.bfloat16)
        order = role_rows(gp, roles[:1], lead[0].shape[0])
        gradient_rows(order, xs, first_bf, lead, learn, width, cfg["chunk"])


def role_rows(gp, roles, rows):
    parts = [gp[piece_rows((rows, role, same)), :] for role in roles for same in (False, True)]
    return jnp.concatenate(parts, 0)


def gradient_rows(order, xs, first_bf, outs, learn, width, chunk):
    rows = outs[0].shape[0]

    def put(columns, value):
        value = value.astype(jnp.bfloat16)
        for i, out in enumerate(outs):
            out[:, columns] = value[i * rows : (i + 1) * rows]

    for start in range(0, width, chunk):
        columns = slice(start, start + chunk)
        put(columns, dot(order[:, :learn], xs[:learn, columns], NN))
    columns = slice(width, width + first_bf.shape[0])
    put(columns, dot(order[:, learn:], first_bf[:, :learn], NT))


def rest_kernel(cfg, xs, gp, first_bf, *outs):
    roles = cfg["roles"]
    order = gp[...] if roles is None else role_rows(gp, roles[1:], outs[0].shape[0])
    gradient_rows(order, xs, first_bf, outs, cfg["learn"], cfg["width"], cfg["chunk"])


def column_chunk(width):
    return max(c for c in range(128, 1153, 128) if width % c == 0)


def learner(staged, piece_list, aux, head, before, cfg):
    total, width, units, learn = staged.shape[0], cfg["width"], cfg["units"], cfg["learn"]
    padded = head.shape[0]
    cfg = dict(cfg, chunk=column_chunk(width))
    roles = cfg["roles"]
    block = lambda rows: jax.ShapeDtypeStruct((rows, width + units), jnp.bfloat16)
    inputs = 3 + len(piece_list)
    if roles is None:
        lead, rest, aliases = [jax.ShapeDtypeStruct((padded, units), jnp.float32)], [block(units)], {}
    else:
        rows = units // (len(roles) * CORES)
        wider = jax.ShapeDtypeStruct((rows, width + 2 * units), jnp.bfloat16)
        lead, rest = [wider] * CORES, [block(rows)] * (CORES * (len(roles) - 1))
        aliases = {inputs + i: i for i in range(len(before))}
    weights, _, first_bf, own, gp, *first_outs = pl.pallas_call(
        functools.partial(learner_kernel, cfg),
        out_shape=(
            block(units),
            jax.ShapeDtypeStruct((units, total), jnp.float32),
            jax.ShapeDtypeStruct((units, total), jnp.bfloat16),
            jax.ShapeDtypeStruct((cfg["heads"] - 1, 1, total - learn), jnp.float32),
            jax.ShapeDtypeStruct((units, 2 * learn), jnp.bfloat16),
            *lead,
        ),
        in_specs=[LOCAL] + [ANYWHERE if roles is None else LOCAL] * len(piece_list)
        + [LOCAL] * (2 + len(before)),
        out_specs=(LOCAL,) * (5 + len(lead)),
        input_output_aliases=aliases,
        compiler_params=pltpu.CompilerParams(vmem_limit_bytes=32 << 20),
        cost_estimate=pl.CostEstimate(
            flops=4 * units * total * width, bytes_accessed=4 * total * width, transcendentals=0
        ),
        name="learner",
    )(staged, *piece_list, aux, head, *before)
    rest_outs = pl.pallas_call(
        functools.partial(rest_kernel, cfg),
        out_shape=tuple(rest),
        in_specs=[LOCAL] * 3,
        out_specs=(LOCAL,) * len(rest),
        compiler_params=pltpu.CompilerParams(vmem_limit_bytes=32 << 20),
        cost_estimate=pl.CostEstimate(
            flops=2 * units * learn * width, bytes_accessed=2 * learn * width, transcendentals=0
        ),
        name="rest",
    )(staged, gp, first_bf)
    return weights, own, first_outs, list(rest_outs)


def opponent_kernel(count, *refs):
    frames, (weights, head), outs = refs[:count], refs[count : count + 2], refs[count + 2 :]
    envs, width = frames[0].shape
    rows = jnp.concatenate([f[...] for f in frames], 0)
    first = jnp.maximum(dot(weights[:, :width], rows, NT), 0.0)
    first_bf = first.astype(jnp.bfloat16)
    result = forward(first, first_bf, weights[...], head[...], width)[0].astype(jnp.bfloat16)
    for i, out in enumerate(outs):
        out[...] = result[:, i * envs : (i + 1) * envs]


def opponents(frames, weights, head, cfg):
    count, (envs, width) = len(frames), frames[0].shape
    return pl.pallas_call(
        functools.partial(opponent_kernel, count),
        out_shape=(jax.ShapeDtypeStruct((head.shape[0], envs), jnp.bfloat16),) * count,
        in_specs=[LOCAL] * (count + 2),
        out_specs=(LOCAL,) * count,
        compiler_params=pltpu.CompilerParams(vmem_limit_bytes=24 << 20),
        cost_estimate=pl.CostEstimate(
            flops=2 * cfg["units"] * count * envs * width,
            bytes_accessed=2 * count * envs * width,
            transcendentals=0,
        ),
        name="opponents",
    )(*frames, weights, head)


def other_agent(i, by, agents):
    return i ^ by if agents & (agents - 1) == 0 else (i + by) % agents


def choose_kernel(*refs):
    answers, ids, out = refs[:-2], refs[-2], refs[-1]
    agents, me = len(answers), lax.axis_index("agent")
    result = jnp.zeros(out.shape, jnp.float32)
    for by, answer in enumerate(answers):
        player = other_agent(me, by, agents)
        result = jnp.where(ids[...] == player, answer[: out.shape[0]].astype(jnp.float32), result)
    out[...] = result.astype(out.dtype)


def choose(answers, ids, count):
    return pl.pallas_call(
        choose_kernel,
        out_shape=jax.ShapeDtypeStruct((count, ids.shape[1]), jnp.bfloat16),
        in_specs=[LOCAL] * (len(answers) + 1),
        out_specs=LOCAL,
        compiler_params=pltpu.CompilerParams(vmem_limit_bytes=2 << 20),
        name="choose",
    )(*answers, ids)


def total_of(refs, columns):
    return sum(x[:, columns].astype(jnp.float32) for x in refs)


def small_kernel(body, out_shape, args):
    bytes_accessed = sum(x.size * x.dtype.itemsize for x in args)
    return pl.pallas_call(
        body,
        out_shape=out_shape,
        in_specs=[LOCAL] * len(args),
        out_specs=jax.tree.map(lambda _: LOCAL, out_shape),
        compiler_params=pltpu.CompilerParams(vmem_limit_bytes=4 << 20),
        cost_estimate=pl.CostEstimate(
            flops=bytes_accessed, bytes_accessed=bytes_accessed, transcendentals=0
        ),
    )(*args)


def add(*arrays, dtype=jnp.bfloat16):
    width = min(x.shape[1] for x in arrays)

    def body(*refs):
        refs[-1][...] = total_of(refs[:-1], slice(0, width)).astype(dtype)

    shape = jax.ShapeDtypeStruct((arrays[0].shape[0], width), dtype)
    return small_kernel(body, shape, arrays)


def add_with_heads(arrays, heads, units, cut=None):
    rows, wide = heads[0].shape
    width = wide - units

    def body(*refs):
        ins, tops, outs = refs[: len(arrays)], refs[len(arrays) :][: len(heads)], refs[len(args) :]
        edges = [0, width] if cut is None else [0, cut, width]
        for out, start, stop in zip(outs, edges, edges[1:]):
            out[:, : stop - start] = total_of(ins, slice(start, stop)).astype(out.dtype)
        tail = slice(width, wide)
        outs[0][:, edges[1] :] = total_of(tops, tail).astype(outs[0].dtype)

    args = (*arrays, *heads)
    widths = [wide] if cut is None else [cut + units, width - cut]
    shape = [jax.ShapeDtypeStruct((rows, w), jnp.bfloat16) for w in widths]
    result = small_kernel(body, tuple(shape), args)
    return result[0] if cut is None else result


def adam_step(master, moment, second, grad, rate):
    moment = beta_first * moment + (1.0 - beta_first) * grad
    second = beta_second * second + (1.0 - beta_second) * grad * grad
    master = master - rate * moment / (jnp.sqrt(second) + adam_eps)
    return (master, moment, second)


def head_gradient(head_parts, count, units):
    if len(head_parts) == 1:
        return head_parts[0][:count]
    mine, mid, near, far = (x[:count, x.shape[1] - units :].astype(jnp.float32) for x in head_parts)
    _, chip = where_am_i()
    end = jnp.logical_or(chip == 0, chip == LINE - 1)
    rounded = lambda x: x.astype(jnp.bfloat16).astype(jnp.float32)
    pair = rounded(mine + jnp.where(end, near, far))
    return pair + jnp.where(end, far, rounded(mid + near))


def adam_kernel(parts, offsets, head_parts, prior, cuts, *refs):
    rate = refs[0][...]
    parts, refs = refs[1 : 1 + parts], refs[1 + parts :]
    head_parts, refs = refs[:head_parts], refs[head_parts:]
    heads = 3 if head_parts else 0
    core, head, refs = refs[:3], refs[3 : 3 + heads], refs[3 + heads + prior :]
    core_out, head_out, refs = refs[:3], refs[3 : 3 + heads], refs[3 + heads :]
    stages, head_stages, refs = refs[:3], refs[3 : 3 + heads], refs[3 + heads :]
    sems, copies = refs[0], []
    if heads:
        count, _, units = head[0].shape
        grad = head_gradient(head_parts, count, units).reshape(head[0].shape)
        for i, value in enumerate(adam_step(*(x[...] for x in head), grad, rate)):
            head_stages[i][...] = value
            copies.append(pltpu.make_async_copy(head_stages[i], head_out[i], refs[1].at[i]))
            copies[-1].start()
    for n, (start, stop) in enumerate(cuts):
        columns = slice(start, stop)
        grad = sum(
            part[:, start - offset : stop - offset].astype(jnp.float32)
            for part, offset in zip(parts, offsets)
        )
        for i, value in enumerate(adam_step(*(x[:, columns] for x in core), grad, rate)):
            stages[i][:, columns] = value
            copies.append(
                pltpu.make_async_copy(
                    stages[i].at[:, columns], core_out[i].at[:, columns], sems.at[n, i]
                )
            )
            copies[-1].start()
    for copy in copies:
        copy.wait()


def adam(rates, parts, head_parts, core, head, span, prior=()):
    rows, width = core[0].shape
    start, stop = span
    tiles = (stop - start) // 128
    pieces = max(1, tiles // 5)
    edges = [start + 128 * (tiles * n // pieces) for n in range(pieces)] + [stop]
    cuts = list(zip(edges, edges[1:]))
    arrays, offsets = [a for a, _ in parts], [o for _, o in parts]
    if not head_parts:
        head = ()
    one = jax.ShapeDtypeStruct((rows, width), jnp.float32)
    inputs = 1 + len(parts) + len(head_parts) + 3 + len(head)
    sems = [pltpu.SemaphoreType.DMA((len(cuts), 3))]
    if head:
        sems.append(pltpu.SemaphoreType.DMA((3,)))
    return pl.pallas_call(
        functools.partial(
            adam_kernel, len(parts), offsets, len(head_parts), len(prior), cuts
        ),
        out_shape=(one,) * 3 + tuple(jax.ShapeDtypeStruct(x.shape, jnp.float32) for x in head),
        in_specs=[LOCAL] * inputs + [ANYWHERE] * len(prior),
        out_specs=(ANYWHERE,) * (3 + len(head)),
        input_output_aliases={inputs + i: i for i in range(len(prior))},
        scratch_shapes=[pltpu.VMEM((rows, width), jnp.float32)] * 3
        + [pltpu.VMEM(x.shape, jnp.float32) for x in head]
        + sems,
        compiler_params=pltpu.CompilerParams(vmem_limit_bytes=12 << 20),
        cost_estimate=pl.CostEstimate(
            flops=20 * rows * (stop - start), bytes_accessed=32 * rows * (stop - start),
            transcendentals=0,
        ),
        name="adam",
    )(rates.reshape(1, 1), *arrays, *head_parts, *core, *head, *prior)


def per_device(
    learn_obs,
    own_obs,
    opp_obs,
    opponent,
    actions,
    done,
    rewards,
    behaviour,
    core_master,
    core_mom,
    core_vel,
    head_master,
    head_mom,
    head_vel,
    rates,
):
    envs, length, width = learn_obs.shape[1:]
    heads, units = head_master.shape[1:]
    action_count = heads - 1
    agents, members = lax.axis_size("agent"), lax.axis_size("dp")
    rows = core_master.shape[1]
    chips = members // CORES
    line = chips == LINE and members == LINE * CORES and units == members * rows and heads <= rows
    wide = jnp.float32

    def along(x, pairs):
        return lax.ppermute(
            x, "dp", [(a * CORES + c, b * CORES + c) for a, b in pairs for c in range(CORES)]
        )

    def sibling(x):
        return lax.ppermute(x, "dp", [(i, i ^ 1) for i in range(members)])

    def swap(x, by):
        return lax.ppermute(x, "agent", [(i, other_agent(i, by, agents)) for i in range(agents)])

    mine = core_master[0].astype(jnp.bfloat16)
    if line:
        far = along(mine, GATHER_FAR)
        near = along(mine, GATHER_NEAR)
        mid = along(mine, GATHER_MID)
        onward = along(far, GATHER_FORWARD)
        joined = add(mid, onward)
        got = [("mine", mine, SELF_FROM), ("far", far, FAR_FROM), ("near", near, NEAR_FROM),
               ("last", joined, LAST_FROM)]

        def with_siblings(group):
            arrays = [g[1] for g in group] + [sibling(g[1]) for g in group]
            return arrays, [(rows, g[2], same) for same in (True, False) for g in group]

        first_list, first_pieces = with_siblings(got[:-1])
        piece_list, pieces = with_siblings(got[-1:])
        roles = ROLES
    else:
        piece_list = [lax.all_gather(mine, "dp", axis=0, tiled=True)]
        pieces = [(units, None, True)]
        roles = None

    frames = [opp_obs[0]] + [swap(opp_obs[0], by) for by in range(1, agents)]

    by_row = lambda x: jnp.transpose(x, (1, 0, 2))
    cfg = dict(pieces=pieces, heads=heads, width=width, units=units, length=length, roles=roles,
               learn=envs * length)
    staged, aux, head = stage(
        learn_obs[0].reshape(envs * length, width),
        own_obs[0],
        [x[0].T for x in (actions, done, rewards, behaviour)],
        by_row(head_master),
    )
    before = ()
    if line:
        before = early(staged, first_pieces, first_list, units)
    weights, own, lead, rest = learner(staged, piece_list, aux, head, before, cfg)
    played = opponents(frames, weights, head, cfg)
    own_logits = jnp.transpose(own, (1, 2, 0))

    def undo(by):
        there = other_agent(0, by, agents)
        return next(b for b in range(agents) if other_agent(there, b, agents) == 0)

    answers = [played[0]] + [swap(played[by], undo(by)) for by in range(1, agents)]
    opp_logits = choose(answers, opponent[0].T, action_count)

    if line:
        blocks = lead + rest
        send, keep = blocks[::CORES], blocks[1::CORES]
        came = [sibling(b) for b in send]
        last = add_with_heads((keep[0], came[0]), (keep[0], came[0]), units)
        through = along(last, SCATTER_FORWARD)
        part_mid = along(last, SCATTER_MID)
        toward = add_with_heads((keep[1], came[1]), (last,), units)
        part_near = along(toward, SCATTER_NEAR)
        cut = 128 * (5 * (width + units) // (8 * 128))
        beyond = add_with_heads((keep[2], came[2], through), (last, through), units, cut)
        part_far = [along(b, SCATTER_FAR) for b in beyond]
        known = add(keep[3], came[3], part_near, part_mid, dtype=wide)
        spans = ((0, cut), (cut, width + units))
        parts = [((known, 0), (far, at)) for far, (at, _) in zip(part_far, spans)]
        head_parts = (last, part_mid, part_near, part_far[0])
    else:
        spans = ((0, width + units),)
        total = lax.psum_scatter(rest[0], "dp", scatter_dimension=0, tiled=True)
        parts, head_parts = [((total, 0),)], (lax.psum(lead[0], "dp"),)
    core = (core_master[0], core_mom[0], core_vel[0])
    head = (by_row(head_master), by_row(head_mom), by_row(head_vel))
    new = ()
    for n, (span, part) in enumerate(zip(spans, parts)):
        done = adam(rates, part, () if n else head_parts, core, head, span, new[:3])
        new = (*done[:3], *(new[3:] or done[3:]))
    return (own_logits, opp_logits.T[None], *[x[None] for x in new[:3]], *map(by_row, new[3:]))


def solution(mesh):
    sharded, whole = P("agent", "dp", None), P("agent", None, None)

    return jax.shard_map(
        per_device,
        mesh=mesh,
        in_specs=(P("agent", "dp", None, None),) + (sharded,) * 10 + (whole,) * 3 + (P("agent"),),
        out_specs=(sharded,) * 5 + (whole,) * 3,
        check_vma=False,
    )
```

```python
import functools

import jax
import jax.numpy as jnp
from jax import lax
from jax.experimental import pallas as pl
from jax.experimental.pallas import tpu as pltpu
from jax.sharding import PartitionSpec as P


gamma_rate = 0.99
baseline_cost = 0.5
entropy_cost = 0.05
beta_first = 0.9
beta_second = 0.99
adam_eps = 1e-08

CORES = 2
SUBLANES = 32

LINE = 4
GATHER_FAR = ((0, 2), (3, 1), (1, 0), (2, 3))
GATHER_NEAR = ((0, 1), (3, 2), (1, 3), (2, 0))
GATHER_MID = ((1, 2), (2, 1))
GATHER_FORWARD = ((2, 3), (1, 0), (0, 1), (3, 2))
FAR_FROM = (1, 3, 0, 2)
NEAR_FROM = (2, 0, 3, 1)
LAST_FROM = (3, 2, 1, 0)
SELF_FROM = (0, 1, 2, 3)
ROLES = (LAST_FROM, NEAR_FROM, FAR_FROM, SELF_FROM)
SCATTER_FORWARD = ((3, 2), (0, 1), (1, 0), (2, 3))
SCATTER_NEAR = tuple((b, a) for a, b in GATHER_NEAR)
SCATTER_MID = ((1, 2), (2, 1))
SCATTER_FAR = tuple((b, a) for a, b in GATHER_FAR)


def dot(left, right, dims, precision=None):
    return lax.dot_general(
        left, right, (dims, ((), ())), preferred_element_type=jnp.float32, precision=precision
    )


NN = ((1,), (0,))
NT = ((1,), (1,))


def table(values, index):
    result = jnp.int32(values[0])
    for place, value in enumerate(values[1:], 1):
        result = jnp.where(index == place, jnp.int32(value), result)
    return result


def trace_gradients(out, boot, aux, action_count, length, scale):
    rows, lanes = out.shape
    row = lax.broadcasted_iota(jnp.int32, (rows, lanes), 0)
    step = lax.rem(lax.broadcasted_iota(jnp.int32, (1, lanes), 1), length)
    last = step == length - 1
    policy = row < action_count
    actions, done, rewards, behaviour = (aux[i : i + 1] for i in range(4))
    values = out[action_count : action_count + 1]
    totals = jnp.sum(jnp.where(policy, jnp.exp(out), 0.0), 0, keepdims=True)
    logp = out - jnp.log(totals)
    probs = jnp.where(policy, jnp.exp(logp), 0.0)
    chosen = (row == actions.astype(jnp.int32)).astype(jnp.float32)
    picked = jnp.sum(logp * chosen, 0, keepdims=True)
    ratio = jnp.minimum(1.0, jnp.exp(picked - behaviour))
    discount = gamma_rate * (1.0 - done)
    following = lambda x, end: jnp.where(last, end, pltpu.roll(x, lanes - 1, 1))
    delta = ratio * (rewards + discount * following(values, boot) - values)
    factor = jnp.where(last, 0.0, discount * ratio)
    reach = 1
    while reach < length:
        delta = delta + factor * pltpu.roll(delta, lanes - reach, 1)
        factor = factor * pltpu.roll(factor, lanes - reach, 1)
        reach *= 2
    targets = values + delta
    advantage = ratio * (rewards + discount * following(targets, boot) - values)
    entropy = -jnp.sum(jnp.where(policy, probs * logp, 0.0), 0, keepdims=True)
    grad_logits = scale * (
        -advantage * (chosen - probs) + entropy_cost * probs * (logp + entropy)
    )
    grad_value = scale * (-baseline_cost * (targets - values))
    return jnp.where(policy, grad_logits, jnp.where(row == action_count, grad_value, 0.0))


ANYWHERE = pl.BlockSpec(memory_space=pl.ANY)
LOCAL = pl.BlockSpec(memory_space=pltpu.VMEM)


def in_hbm(arrays):
    return [pltpu.with_memory_space_constraint(x, pltpu.HBM) for x in arrays]


def stage_kernel(learn_ref, own_ref, *refs):
    small, (staged, aux, head_out), local, sems = refs[:5], refs[5:8], refs[8:13], refs[13]
    per_step, head_ref = local[:4], local[4]
    rows = learn_ref.shape[0]
    small_copies = [
        pltpu.make_async_copy(a, b, sems.at[2 + i]) for i, (a, b) in enumerate(zip(small, local))
    ]
    for copy in small_copies:
        copy.start()
    copies = (
        pltpu.make_async_copy(learn_ref, staged.at[pl.ds(0, rows)], sems.at[0]),
        pltpu.make_async_copy(own_ref, staged.at[pl.ds(rows, own_ref.shape[0])], sems.at[1]),
    )
    for copy in copies:
        copy.start()
    length, envs = per_step[0].shape
    lane = lax.broadcasted_iota(jnp.int32, (envs, rows), 1)
    spread = (lane // length == lax.broadcasted_iota(jnp.int32, (envs, rows), 0)).astype(
        jnp.float32
    )
    mask = lax.rem(lax.broadcasted_iota(jnp.int32, (length, rows), 1), length)
    mask = mask == lax.broadcasted_iota(jnp.int32, (length, rows), 0)
    for copy in small_copies:
        copy.wait()
    for i, ref in enumerate(per_step):
        wide = dot(ref[...].astype(jnp.float32), spread, NN, lax.Precision.HIGHEST)
        aux[i : i + 1] = jnp.sum(jnp.where(mask, wide, 0.0), 0, keepdims=True)
    heads, _, units = head_ref.shape
    head_out[...] = jnp.zeros_like(head_out)
    head_out[:heads] = head_ref[...].reshape(heads, units).astype(jnp.bfloat16)
    for copy in copies:
        copy.wait()


def stage(learn_rows, own_rows, per_step, head):
    rows, width = learn_rows.shape
    total = rows + own_rows.shape[0]
    heads, _, units = head.shape
    padded = -(-heads // SUBLANES) * SUBLANES
    return pl.pallas_call(
        stage_kernel,
        out_shape=(
            jax.ShapeDtypeStruct((total, width), jnp.bfloat16),
            jax.ShapeDtypeStruct((len(per_step), rows), jnp.float32),
            jax.ShapeDtypeStruct((padded, units), jnp.bfloat16),
        ),
        in_specs=[ANYWHERE] * 7,
        out_specs=(LOCAL,) * 3,
        scratch_shapes=[pltpu.VMEM(x.shape, x.dtype) for x in (*per_step, head)]
        + [pltpu.SemaphoreType.DMA((7,))],
        compiler_params=pltpu.CompilerParams(vmem_limit_bytes=8 << 20),
        cost_estimate=pl.CostEstimate(
            flops=0, bytes_accessed=4 * total * width, transcendentals=0
        ),
        name="stage",
    )(*in_hbm((learn_rows, own_rows, *per_step, head)))


def where_am_i():
    place = lax.axis_index("dp")
    return lax.rem(place, CORES), lax.div(place, CORES)


def piece_rows(piece):
    rows, source, same = piece
    core, chip = where_am_i()
    owner = core if same else 1 - core
    return pl.ds(pl.multiple_of((table(source, chip) * CORES + owner) * rows, rows), rows)


def place_pieces(pieces, w_refs, ws):
    for piece, ref in zip(pieces, w_refs):
        ws[piece_rows(piece), :] = ref[...]


def multiply_pieces(pieces, w_refs, xs, width, first, first_bf):
    result = dot(jnp.concatenate([ref[:, :width] for ref in w_refs], 0), xs[...], NT)
    result = jnp.maximum(result, 0.0)
    result_bf = result.astype(jnp.bfloat16)
    at = 0
    for piece in pieces:
        rows = piece_rows(piece)
        first[rows, :] = result[at : at + piece[0]]
        first_bf[rows, :] = result_bf[at : at + piece[0]]
        at += piece[0]


def early_kernel(pieces, width, xs, *refs):
    w_refs, (ws, first, first_bf) = refs[: len(pieces)], refs[len(pieces) :]
    place_pieces(pieces, w_refs, ws)
    multiply_pieces(pieces, w_refs, xs, width, first, first_bf)


def early(staged, pieces, piece_list, units):
    total, width = staged.shape
    return pl.pallas_call(
        functools.partial(early_kernel, pieces, width),
        out_shape=(
            jax.ShapeDtypeStruct((units, width + units), jnp.bfloat16),
            jax.ShapeDtypeStruct((units, total), jnp.float32),
            jax.ShapeDtypeStruct((units, total), jnp.bfloat16),
        ),
        in_specs=[LOCAL] * (1 + len(pieces)),
        out_specs=(LOCAL,) * 3,
        compiler_params=pltpu.CompilerParams(vmem_limit_bytes=24 << 20),
        cost_estimate=pl.CostEstimate(
            flops=2 * units * total * width, bytes_accessed=4 * units * width, transcendentals=0
        ),
        name="early",
    )(staged, *piece_list)


def forward(first, first_bf, weights, head, width):
    pre_two = dot(weights[:, width:], first_bf, NN)
    second_bf = (jnp.maximum(pre_two, 0.0) + first).astype(jnp.bfloat16)
    return dot(head, second_bf, NN), pre_two, second_bf


def learner_kernel(cfg, *refs):
    pieces, heads, roles = cfg["pieces"], cfg["heads"], cfg["roles"]
    xs, refs = refs[0], refs[1:]
    w_refs, refs = refs[: len(pieces)], refs[len(pieces) :]
    aux_ref, head_ref, refs = refs[0], refs[1], refs[2:]
    if roles is not None:
        refs = refs[3:]
    ws, first, first_bf, own_ref, gp, lead = *refs[:5], refs[5:]
    learn, width, units, length = cfg["learn"], cfg["width"], cfg["units"], cfg["length"]
    envs = learn // length

    if roles is None:
        pltpu.sync_copy(w_refs[0], ws)
        first[...] = jnp.maximum(dot(ws[:, :width], xs[...], NT), 0.0)
        first_bf[...] = first[...].astype(jnp.bfloat16)
    else:
        place_pieces(pieces, w_refs, ws)
        multiply_pieces(pieces, w_refs, xs, width, first, first_bf)
    out, pre_two, second_bf = forward(first[...], first_bf[...], ws[...], head_ref[...], width)
    own_ref[...] = out[: heads - 1, learn:].reshape(heads - 1, 1, envs)
    spread = lax.broadcasted_iota(jnp.int32, (envs, learn), 1) // length
    spread = (spread == lax.broadcasted_iota(jnp.int32, (envs, learn), 0)).astype(jnp.float32)
    boot = dot(out[:, learn:], spread, NN, lax.Precision.HIGHEST)[heads - 1 : heads]
    grad = trace_gradients(
        out[:, :learn], boot, aux_ref[...], heads - 1, length, 1.0 / length
    ).astype(jnp.bfloat16)
    ghead = dot(grad, second_bf[:, :learn], NT)
    if roles is None:
        lead[0][...] = ghead
    grad_second = dot(head_ref[...].T, grad, NN)
    grad_two = jnp.where(pre_two[:, :learn] > 0, grad_second, 0.0).astype(jnp.bfloat16)
    grad_first = grad_second + dot(ws[:, width:].T, grad_two, NN)
    grad_one = jnp.where(first[:, :learn] > 0, grad_first, 0.0).astype(jnp.bfloat16)
    gp[:, :learn] = grad_one
    gp[:, learn:] = grad_two
    if roles is not None:
        for out in lead:
            out[:, width + units :] = ghead[: out.shape[0]].astype(jnp.bfloat16)
        order = role_rows(gp, roles[:1], lead[0].shape[0])
        gradient_rows(order, xs, first_bf, lead, learn, width, cfg["chunk"])


def role_rows(gp, roles, rows):
    parts = [gp[piece_rows((rows, role, same)), :] for role in roles for same in (False, True)]
    return jnp.concatenate(parts, 0)


def gradient_rows(order, xs, first_bf, outs, learn, width, chunk):
    rows = outs[0].shape[0]

    def put(columns, value):
        value = value.astype(jnp.bfloat16)
        for i, out in enumerate(outs):
            out[:, columns] = value[i * rows : (i + 1) * rows]

    for start in range(0, width, chunk):
        columns = slice(start, start + chunk)
        put(columns, dot(order[:, :learn], xs[:learn, columns], NN))
    columns = slice(width, width + first_bf.shape[0])
    put(columns, dot(order[:, learn:], first_bf[:, :learn], NT))


def rest_kernel(cfg, xs, gp, first_bf, *outs):
    roles = cfg["roles"]
    order = gp[...] if roles is None else role_rows(gp, roles[1:], outs[0].shape[0])
    gradient_rows(order, xs, first_bf, outs, cfg["learn"], cfg["width"], cfg["chunk"])


def column_chunk(width):
    return max(c for c in range(128, 1153, 128) if width % c == 0)


def learner(staged, piece_list, aux, head, before, cfg):
    total, width, units, learn = staged.shape[0], cfg["width"], cfg["units"], cfg["learn"]
    padded = head.shape[0]
    cfg = dict(cfg, chunk=column_chunk(width))
    roles = cfg["roles"]
    block = lambda rows: jax.ShapeDtypeStruct((rows, width + units), jnp.bfloat16)
    inputs = 3 + len(piece_list)
    if roles is None:
        lead, rest, aliases = [jax.ShapeDtypeStruct((padded, units), jnp.float32)], [block(units)], {}
    else:
        rows = units // (len(roles) * CORES)
        wider = jax.ShapeDtypeStruct((rows, width + 2 * units), jnp.bfloat16)
        lead, rest = [wider] * CORES, [block(rows)] * (CORES * (len(roles) - 1))
        aliases = {inputs + i: i for i in range(len(before))}
    weights, _, first_bf, own, gp, *first_outs = pl.pallas_call(
        functools.partial(learner_kernel, cfg),
        out_shape=(
            block(units),
            jax.ShapeDtypeStruct((units, total), jnp.float32),
            jax.ShapeDtypeStruct((units, total), jnp.bfloat16),
            jax.ShapeDtypeStruct((cfg["heads"] - 1, 1, total - learn), jnp.float32),
            jax.ShapeDtypeStruct((units, 2 * learn), jnp.bfloat16),
            *lead,
        ),
        in_specs=[LOCAL] + [ANYWHERE if roles is None else LOCAL] * len(piece_list)
        + [LOCAL] * (2 + len(before)),
        out_specs=(LOCAL,) * (5 + len(lead)),
        input_output_aliases=aliases,
        compiler_params=pltpu.CompilerParams(vmem_limit_bytes=32 << 20),
        cost_estimate=pl.CostEstimate(
            flops=4 * units * total * width, bytes_accessed=4 * total * width, transcendentals=0
        ),
        name="learner",
    )(staged, *piece_list, aux, head, *before)
    rest_outs = pl.pallas_call(
        functools.partial(rest_kernel, cfg),
        out_shape=tuple(rest),
        in_specs=[LOCAL] * 3,
        out_specs=(LOCAL,) * len(rest),
        compiler_params=pltpu.CompilerParams(vmem_limit_bytes=32 << 20),
        cost_estimate=pl.CostEstimate(
            flops=2 * units * learn * width, bytes_accessed=2 * learn * width, transcendentals=0
        ),
        name="rest",
    )(staged, gp, first_bf)
    return weights, own, first_outs, list(rest_outs)


def opponent_kernel(count, *refs):
    frames, (weights, head), outs = refs[:count], refs[count : count + 2], refs[count + 2 :]
    envs, width = frames[0].shape
    rows = jnp.concatenate([f[...] for f in frames], 0)
    first = jnp.maximum(dot(weights[:, :width], rows, NT), 0.0)
    first_bf = first.astype(jnp.bfloat16)
    result = forward(first, first_bf, weights[...], head[...], width)[0].astype(jnp.bfloat16)
    for i, out in enumerate(outs):
        out[...] = result[:, i * envs : (i + 1) * envs]


def opponents(frames, weights, head, cfg):
    count, (envs, width) = len(frames), frames[0].shape
    return pl.pallas_call(
        functools.partial(opponent_kernel, count),
        out_shape=(jax.ShapeDtypeStruct((head.shape[0], envs), jnp.bfloat16),) * count,
        in_specs=[LOCAL] * (count + 2),
        out_specs=(LOCAL,) * count,
        compiler_params=pltpu.CompilerParams(vmem_limit_bytes=24 << 20),
        cost_estimate=pl.CostEstimate(
            flops=2 * cfg["units"] * count * envs * width,
            bytes_accessed=2 * count * envs * width,
            transcendentals=0,
        ),
        name="opponents",
    )(*frames, weights, head)


def other_agent(i, by, agents):
    return i ^ by if agents & (agents - 1) == 0 else (i + by) % agents


def choose_kernel(*refs):
    answers, ids, out = refs[:-2], refs[-2], refs[-1]
    agents, me = len(answers), lax.axis_index("agent")
    result = jnp.zeros(out.shape, jnp.float32)
    for by, answer in enumerate(answers):
        player = other_agent(me, by, agents)
        result = jnp.where(ids[...] == player, answer[: out.shape[0]].astype(jnp.float32), result)
    out[...] = result.astype(out.dtype)


def choose(answers, ids, count):
    return pl.pallas_call(
        choose_kernel,
        out_shape=jax.ShapeDtypeStruct((count, ids.shape[1]), jnp.bfloat16),
        in_specs=[LOCAL] * (len(answers) + 1),
        out_specs=LOCAL,
        compiler_params=pltpu.CompilerParams(vmem_limit_bytes=2 << 20),
        name="choose",
    )(*answers, ids)


def total_of(refs, columns, through=0):
    values = [x[:, columns].astype(jnp.float32) for x in refs]
    for i in range(len(values) - through, len(values)):
        values[i] = jnp.where(inner_chip(), values[i], 0.0)
    return sum(values)


def inner_chip():
    _, chip = where_am_i()
    return jnp.logical_and(chip > 0, chip < LINE - 1)


def small_kernel(body, out_shape, args):
    bytes_accessed = sum(x.size * x.dtype.itemsize for x in args)
    return pl.pallas_call(
        body,
        out_shape=out_shape,
        in_specs=[LOCAL] * len(args),
        out_specs=jax.tree.map(lambda _: LOCAL, out_shape),
        compiler_params=pltpu.CompilerParams(vmem_limit_bytes=4 << 20),
        cost_estimate=pl.CostEstimate(
            flops=bytes_accessed, bytes_accessed=bytes_accessed, transcendentals=0
        ),
    )(*args)


def add(*arrays, dtype=jnp.bfloat16):
    width = min(x.shape[1] for x in arrays)

    def body(*refs):
        refs[-1][...] = total_of(refs[:-1], slice(0, width)).astype(dtype)

    shape = jax.ShapeDtypeStruct((arrays[0].shape[0], width), dtype)
    return small_kernel(body, shape, arrays)


def join(mid, onward):
    def body(mid_ref, onward_ref, out):
        out[...] = jnp.where(inner_chip(), mid_ref[...], onward_ref[...])

    return small_kernel(body, jax.ShapeDtypeStruct(mid.shape, mid.dtype), (mid, onward))


def add_with_heads(arrays, heads, units, cut=None, through=()):
    arrays, heads = (*arrays, *through), (*heads, *through)
    rows, wide = heads[0].shape
    width = wide - units

    def body(*refs):
        ins, tops, outs = refs[: len(arrays)], refs[len(arrays) :][: len(heads)], refs[len(args) :]
        edges = [0, width] if cut is None else [0, cut, width]
        for out, start, stop in zip(outs, edges, edges[1:]):
            value = total_of(ins, slice(start, stop), len(through))
            out[:, : stop - start] = value.astype(out.dtype)
        tail = slice(width, wide)
        outs[0][:, edges[1] :] = total_of(tops, tail, len(through)).astype(outs[0].dtype)

    args = (*arrays, *heads)
    widths = [wide] if cut is None else [cut + units, width - cut]
    shape = [jax.ShapeDtypeStruct((rows, w), jnp.bfloat16) for w in widths]
    result = small_kernel(body, tuple(shape), args)
    return result[0] if cut is None else result


def adam_step(master, moment, second, grad, rate):
    moment = beta_first * moment + (1.0 - beta_first) * grad
    second = beta_second * second + (1.0 - beta_second) * grad * grad
    master = master - rate * moment / (jnp.sqrt(second) + adam_eps)
    return (master, moment, second)


def head_gradient(head_parts, count, units):
    if len(head_parts) == 1:
        return head_parts[0][:count]
    mine, mid, near, far = (x[:count, x.shape[1] - units :].astype(jnp.float32) for x in head_parts)
    _, chip = where_am_i()
    end = jnp.logical_or(chip == 0, chip == LINE - 1)
    rounded = lambda x: x.astype(jnp.bfloat16).astype(jnp.float32)
    pair = rounded(mine + jnp.where(end, near, far))
    return pair + jnp.where(end, far, rounded(mid + near))


def adam_kernel(parts, offsets, head_parts, prior, cuts, *refs):
    rate = refs[0][...]
    parts, refs = refs[1 : 1 + parts], refs[1 + parts :]
    head_parts, refs = refs[:head_parts], refs[head_parts:]
    heads = 3 if head_parts else 0
    core, head, refs = refs[:3], refs[3 : 3 + heads], refs[3 + heads + prior :]
    core_out, head_out, refs = refs[:3], refs[3 : 3 + heads], refs[3 + heads :]
    stages, head_stages, refs = refs[:3], refs[3 : 3 + heads], refs[3 + heads :]
    sems, copies = refs[0], []
    if heads:
        count, _, units = head[0].shape
        grad = head_gradient(head_parts, count, units).reshape(head[0].shape)
        for i, value in enumerate(adam_step(*(x[...] for x in head), grad, rate)):
            head_stages[i][...] = value
            copies.append(pltpu.make_async_copy(head_stages[i], head_out[i], refs[1].at[i]))
            copies[-1].start()
    for n, (start, stop) in enumerate(cuts):
        columns = slice(start, stop)
        grad = sum(
            part[:, start - offset : stop - offset].astype(jnp.float32)
            for part, offset in zip(parts, offsets)
        )
        for i, value in enumerate(adam_step(*(x[:, columns] for x in core), grad, rate)):
            stages[i][:, columns] = value
            copies.append(
                pltpu.make_async_copy(
                    stages[i].at[:, columns], core_out[i].at[:, columns], sems.at[n, i]
                )
            )
            copies[-1].start()
    for copy in copies:
        copy.wait()


def adam(rates, parts, head_parts, core, head, span, prior=()):
    rows, width = core[0].shape
    start, stop = span
    tiles = (stop - start) // 128
    pieces = max(1, tiles // 5)
    edges = [start + 128 * (tiles * n // pieces) for n in range(pieces)] + [stop]
    cuts = list(zip(edges, edges[1:]))
    arrays, offsets = [a for a, _ in parts], [o for _, o in parts]
    if not head_parts:
        head = ()
    one = jax.ShapeDtypeStruct((rows, width), jnp.float32)
    inputs = 1 + len(parts) + len(head_parts) + 3 + len(head)
    sems = [pltpu.SemaphoreType.DMA((len(cuts), 3))]
    if head:
        sems.append(pltpu.SemaphoreType.DMA((3,)))
    return pl.pallas_call(
        functools.partial(
            adam_kernel, len(parts), offsets, len(head_parts), len(prior), cuts
        ),
        out_shape=(one,) * 3 + tuple(jax.ShapeDtypeStruct(x.shape, jnp.float32) for x in head),
        in_specs=[LOCAL] * inputs + [ANYWHERE] * len(prior),
        out_specs=(ANYWHERE,) * (3 + len(head)),
        input_output_aliases={inputs + i: i for i in range(len(prior))},
        scratch_shapes=[pltpu.VMEM((rows, width), jnp.float32)] * 3
        + [pltpu.VMEM(x.shape, jnp.float32) for x in head]
        + sems,
        compiler_params=pltpu.CompilerParams(vmem_limit_bytes=12 << 20),
        cost_estimate=pl.CostEstimate(
            flops=20 * rows * (stop - start), bytes_accessed=32 * rows * (stop - start),
            transcendentals=0,
        ),
        name="adam",
    )(rates.reshape(1, 1), *arrays, *head_parts, *core, *head, *prior)


def per_device(
    learn_obs,
    own_obs,
    opp_obs,
    opponent,
    actions,
    done,
    rewards,
    behaviour,
    core_master,
    core_mom,
    core_vel,
    head_master,
    head_mom,
    head_vel,
    rates,
):
    envs, length, width = learn_obs.shape[1:]
    heads, units = head_master.shape[1:]
    action_count = heads - 1
    agents, members = lax.axis_size("agent"), lax.axis_size("dp")
    rows = core_master.shape[1]
    chips = members // CORES
    line = chips == LINE and members == LINE * CORES and units == members * rows and heads <= rows
    wide = jnp.float32

    def along(x, pairs):
        return lax.ppermute(
            x, "dp", [(a * CORES + c, b * CORES + c) for a, b in pairs for c in range(CORES)]
        )

    def sibling(x):
        return lax.ppermute(x, "dp", [(i, i ^ 1) for i in range(members)])

    def swap(x, by):
        return lax.ppermute(x, "agent", [(i, other_agent(i, by, agents)) for i in range(agents)])

    mine = core_master[0].astype(jnp.bfloat16)
    if line:
        far = along(mine, GATHER_FAR)
        near = along(mine, GATHER_NEAR)
        mid = along(mine, GATHER_MID)
        onward = along(far, GATHER_FORWARD)
        joined = join(mid, onward)
        got = [("mine", mine, SELF_FROM), ("far", far, FAR_FROM), ("near", near, NEAR_FROM),
               ("last", joined, LAST_FROM)]

        def with_siblings(group):
            arrays = [g[1] for g in group] + [sibling(g[1]) for g in group]
            return arrays, [(rows, g[2], same) for same in (True, False) for g in group]

        first_list, first_pieces = with_siblings(got[:-1])
        piece_list, pieces = with_siblings(got[-1:])
        roles = ROLES
    else:
        piece_list = [lax.all_gather(mine, "dp", axis=0, tiled=True)]
        pieces = [(units, None, True)]
        roles = None

    frames = [opp_obs[0]] + [swap(opp_obs[0], by) for by in range(1, agents)]

    by_row = lambda x: jnp.transpose(x, (1, 0, 2))
    cfg = dict(pieces=pieces, heads=heads, width=width, units=units, length=length, roles=roles,
               learn=envs * length)
    staged, aux, head = stage(
        learn_obs[0].reshape(envs * length, width),
        own_obs[0],
        [x[0].T for x in (actions, done, rewards, behaviour)],
        by_row(head_master),
    )
    before = ()
    if line:
        before = early(staged, first_pieces, first_list, units)
    weights, own, lead, rest = learner(staged, piece_list, aux, head, before, cfg)
    played = opponents(frames, weights, head, cfg)
    own_logits = jnp.transpose(own, (1, 2, 0))

    def undo(by):
        there = other_agent(0, by, agents)
        return next(b for b in range(agents) if other_agent(there, b, agents) == 0)

    answers = [played[0]] + [swap(played[by], undo(by)) for by in range(1, agents)]
    opp_logits = choose(answers, opponent[0].T, action_count)

    if line:
        blocks = lead + rest
        send, keep = blocks[::CORES], blocks[1::CORES]
        came = [sibling(b) for b in send]
        last = add_with_heads((keep[0], came[0]), (keep[0], came[0]), units)
        through = along(last, SCATTER_FORWARD)
        part_mid = along(last, SCATTER_MID)
        toward = add_with_heads((keep[1], came[1]), (last,), units)
        part_near = along(toward, SCATTER_NEAR)
        cut = 128 * ((width + units) // 256 + 1)
        beyond = add_with_heads((keep[2], came[2]), (last,), units, cut, (through,))
        part_far = [along(b, SCATTER_FAR) for b in beyond]
        known = add(keep[3], came[3], part_near, part_mid, dtype=wide)
        spans = ((0, cut), (cut, width + units))
        parts = [((known, 0), (far, at)) for far, (at, _) in zip(part_far, spans)]
        head_parts = (last, part_mid, part_near, part_far[0])
    else:
        spans = ((0, width + units),)
        total = lax.psum_scatter(rest[0], "dp", scatter_dimension=0, tiled=True)
        parts, head_parts = [((total, 0),)], (lax.psum(lead[0], "dp"),)
    core = (core_master[0], core_mom[0], core_vel[0])
    head = (by_row(head_master), by_row(head_mom), by_row(head_vel))
    new = ()
    for n, (span, part) in enumerate(zip(spans, parts)):
        done = adam(rates, part, () if n else head_parts, core, head, span, new[:3])
        new = (*done[:3], *(new[3:] or done[3:]))
    return (own_logits, opp_logits.T[None], *[x[None] for x in new[:3]], *map(by_row, new[3:]))


def solution(mesh):
    sharded, whole = P("agent", "dp", None), P("agent", None, None)

    return jax.shard_map(
        per_device,
        mesh=mesh,
        in_specs=(P("agent", "dp", None, None),) + (sharded,) * 10 + (whole,) * 3 + (P("agent"),),
        out_specs=(sharded,) * 5 + (whole,) * 3,
        check_vma=False,
    )
```

```python
import functools

import jax
import jax.numpy as jnp
from jax import lax
from jax.experimental import pallas as pl
from jax.experimental.pallas import tpu as pltpu
from jax.sharding import PartitionSpec as P


gamma_rate = 0.99
baseline_cost = 0.5
entropy_cost = 0.05
beta_first = 0.9
beta_second = 0.99
adam_eps = 1e-08

CORES = 2
SUBLANES = 32

LINE = 4
GATHER_FAR = ((0, 2), (3, 1), (1, 0), (2, 3))
GATHER_NEAR = ((0, 1), (3, 2), (1, 3), (2, 0))
GATHER_MID = ((1, 2), (2, 1))
GATHER_FORWARD = ((2, 3), (1, 0), (0, 1), (3, 2))
FAR_FROM = (1, 3, 0, 2)
NEAR_FROM = (2, 0, 3, 1)
LAST_FROM = (3, 2, 1, 0)
SELF_FROM = (0, 1, 2, 3)
ROLES = (LAST_FROM, NEAR_FROM, FAR_FROM, SELF_FROM)
SCATTER_FORWARD = ((3, 2), (0, 1), (1, 0), (2, 3))
SCATTER_NEAR = tuple((b, a) for a, b in GATHER_NEAR)
SCATTER_MID = ((1, 2), (2, 1))
SCATTER_FAR = tuple((b, a) for a, b in GATHER_FAR)


def dot(left, right, dims, precision=None):
    return lax.dot_general(
        left, right, (dims, ((), ())), preferred_element_type=jnp.float32, precision=precision
    )


NN = ((1,), (0,))
NT = ((1,), (1,))


def table(values, index):
    result = jnp.int32(values[0])
    for place, value in enumerate(values[1:], 1):
        result = jnp.where(index == place, jnp.int32(value), result)
    return result


def trace_gradients(out, boot, aux, action_count, length, scale):
    rows, lanes = out.shape
    row = lax.broadcasted_iota(jnp.int32, (rows, lanes), 0)
    step = lax.rem(lax.broadcasted_iota(jnp.int32, (1, lanes), 1), length)
    last = step == length - 1
    policy = row < action_count
    actions, done, rewards, behaviour = (aux[i : i + 1] for i in range(4))
    values = out[action_count : action_count + 1]
    totals = jnp.sum(jnp.where(policy, jnp.exp(out), 0.0), 0, keepdims=True)
    logp = out - jnp.log(totals)
    probs = jnp.where(policy, jnp.exp(logp), 0.0)
    chosen = (row == actions.astype(jnp.int32)).astype(jnp.float32)
    picked = jnp.sum(logp * chosen, 0, keepdims=True)
    ratio = jnp.minimum(1.0, jnp.exp(picked - behaviour))
    discount = gamma_rate * (1.0 - done)
    following = lambda x, end: jnp.where(last, end, pltpu.roll(x, lanes - 1, 1))
    delta = ratio * (rewards + discount * following(values, boot) - values)
    factor = jnp.where(last, 0.0, discount * ratio)
    reach = 1
    while reach < length:
        delta = delta + factor * pltpu.roll(delta, lanes - reach, 1)
        factor = factor * pltpu.roll(factor, lanes - reach, 1)
        reach *= 2
    targets = values + delta
    advantage = ratio * (rewards + discount * following(targets, boot) - values)
    entropy = -jnp.sum(jnp.where(policy, probs * logp, 0.0), 0, keepdims=True)
    grad_logits = scale * (
        -advantage * (chosen - probs) + entropy_cost * probs * (logp + entropy)
    )
    grad_value = scale * (-baseline_cost * (targets - values))
    return jnp.where(policy, grad_logits, jnp.where(row == action_count, grad_value, 0.0))


ANYWHERE = pl.BlockSpec(memory_space=pl.ANY)
LOCAL = pl.BlockSpec(memory_space=pltpu.VMEM)


def in_hbm(arrays):
    return [pltpu.with_memory_space_constraint(x, pltpu.HBM) for x in arrays]


def stage_kernel(learn_ref, own_ref, *refs):
    small, (staged, aux, head_out), local, sems = refs[:5], refs[5:8], refs[8:13], refs[13]
    per_step, head_ref = local[:4], local[4]
    rows = learn_ref.shape[0]
    small_copies = [
        pltpu.make_async_copy(a, b, sems.at[2 + i]) for i, (a, b) in enumerate(zip(small, local))
    ]
    for copy in small_copies:
        copy.start()
    copies = (
        pltpu.make_async_copy(learn_ref, staged.at[pl.ds(0, rows)], sems.at[0]),
        pltpu.make_async_copy(own_ref, staged.at[pl.ds(rows, own_ref.shape[0])], sems.at[1]),
    )
    for copy in copies:
        copy.start()
    length, envs = per_step[0].shape
    lane = lax.broadcasted_iota(jnp.int32, (envs, rows), 1)
    spread = (lane // length == lax.broadcasted_iota(jnp.int32, (envs, rows), 0)).astype(
        jnp.float32
    )
    mask = lax.rem(lax.broadcasted_iota(jnp.int32, (length, rows), 1), length)
    mask = mask == lax.broadcasted_iota(jnp.int32, (length, rows), 0)
    for copy in small_copies:
        copy.wait()
    for i, ref in enumerate(per_step):
        wide = dot(ref[...].astype(jnp.float32), spread, NN, lax.Precision.HIGHEST)
        aux[i : i + 1] = jnp.sum(jnp.where(mask, wide, 0.0), 0, keepdims=True)
    heads, _, units = head_ref.shape
    head_out[...] = jnp.zeros_like(head_out)
    head_out[:heads] = head_ref[...].reshape(heads, units).astype(jnp.bfloat16)
    for copy in copies:
        copy.wait()


def stage(learn_rows, own_rows, per_step, head):
    rows, width = learn_rows.shape
    total = rows + own_rows.shape[0]
    heads, _, units = head.shape
    padded = -(-heads // SUBLANES) * SUBLANES
    return pl.pallas_call(
        stage_kernel,
        out_shape=(
            jax.ShapeDtypeStruct((total, width), jnp.bfloat16),
            jax.ShapeDtypeStruct((len(per_step), rows), jnp.float32),
            jax.ShapeDtypeStruct((padded, units), jnp.bfloat16),
        ),
        in_specs=[ANYWHERE] * 7,
        out_specs=(LOCAL,) * 3,
        scratch_shapes=[pltpu.VMEM(x.shape, x.dtype) for x in (*per_step, head)]
        + [pltpu.SemaphoreType.DMA((7,))],
        compiler_params=pltpu.CompilerParams(vmem_limit_bytes=8 << 20),
        cost_estimate=pl.CostEstimate(
            flops=0, bytes_accessed=4 * total * width, transcendentals=0
        ),
        name="stage",
    )(*in_hbm((learn_rows, own_rows, *per_step, head)))


def where_am_i():
    place = lax.axis_index("dp")
    return lax.rem(place, CORES), lax.div(place, CORES)


def piece_rows(piece):
    rows, source, same = piece
    core, chip = where_am_i()
    owner = core if same else 1 - core
    return pl.ds(pl.multiple_of((table(source, chip) * CORES + owner) * rows, rows), rows)


def place_pieces(pieces, w_refs, ws):
    for piece, ref in zip(pieces, w_refs):
        ws[piece_rows(piece), :] = ref[...]


def multiply_pieces(pieces, w_refs, xs, width, first, first_bf):
    result = dot(jnp.concatenate([ref[:, :width] for ref in w_refs], 0), xs[...], NT)
    result = jnp.maximum(result, 0.0)
    result_bf = result.astype(jnp.bfloat16)
    at = 0
    for piece in pieces:
        rows = piece_rows(piece)
        first[rows, :] = result[at : at + piece[0]]
        first_bf[rows, :] = result_bf[at : at + piece[0]]
        at += piece[0]


def early_kernel(pieces, width, xs, *refs):
    w_refs, (ws, first, first_bf) = refs[: len(pieces)], refs[len(pieces) :]
    place_pieces(pieces, w_refs, ws)
    multiply_pieces(pieces, w_refs, xs, width, first, first_bf)


def early(staged, pieces, piece_list, units):
    total, width = staged.shape
    return pl.pallas_call(
        functools.partial(early_kernel, pieces, width),
        out_shape=(
            jax.ShapeDtypeStruct((units, width + units), jnp.bfloat16),
            jax.ShapeDtypeStruct((units, total), jnp.float32),
            jax.ShapeDtypeStruct((units, total), jnp.bfloat16),
        ),
        in_specs=[LOCAL] * (1 + len(pieces)),
        out_specs=(LOCAL,) * 3,
        compiler_params=pltpu.CompilerParams(vmem_limit_bytes=24 << 20),
        cost_estimate=pl.CostEstimate(
            flops=2 * units * total * width, bytes_accessed=4 * units * width, transcendentals=0
        ),
        name="early",
    )(staged, *piece_list)


def forward(first, first_bf, weights, head, width):
    pre_two = dot(weights[:, width:], first_bf, NN)
    second_bf = (jnp.maximum(pre_two, 0.0) + first).astype(jnp.bfloat16)
    return dot(head, second_bf, NN), pre_two, second_bf


def learner_kernel(cfg, *refs):
    pieces, heads, roles = cfg["pieces"], cfg["heads"], cfg["roles"]
    xs, refs = refs[0], refs[1:]
    w_refs, refs = refs[: len(pieces)], refs[len(pieces) :]
    aux_ref, head_ref, refs = refs[0], refs[1], refs[2:]
    if roles is not None:
        refs = refs[3:]
    ws, first, first_bf, own_ref, gp, lead = *refs[:5], refs[5:]
    learn, width, units, length = cfg["learn"], cfg["width"], cfg["units"], cfg["length"]
    envs = learn // length

    if roles is None:
        pltpu.sync_copy(w_refs[0], ws)
        first[...] = jnp.maximum(dot(ws[:, :width], xs[...], NT), 0.0)
        first_bf[...] = first[...].astype(jnp.bfloat16)
    else:
        place_pieces(pieces, w_refs, ws)
        multiply_pieces(pieces, w_refs, xs, width, first, first_bf)
    out, pre_two, second_bf = forward(first[...], first_bf[...], ws[...], head_ref[...], width)
    own_ref[...] = out[: heads - 1, learn:].reshape(heads - 1, 1, envs)
    spread = lax.broadcasted_iota(jnp.int32, (envs, learn), 1) // length
    spread = (spread == lax.broadcasted_iota(jnp.int32, (envs, learn), 0)).astype(jnp.float32)
    boot = dot(out[:, learn:], spread, NN, lax.Precision.HIGHEST)[heads - 1 : heads]
    grad = trace_gradients(
        out[:, :learn], boot, aux_ref[...], heads - 1, length, 1.0 / length
    ).astype(jnp.bfloat16)
    ghead = dot(grad, second_bf[:, :learn], NT)
    if roles is None:
        lead[0][...] = ghead
    grad_second = dot(head_ref[...].T, grad, NN)
    grad_two = jnp.where(pre_two[:, :learn] > 0, grad_second, 0.0).astype(jnp.bfloat16)
    grad_first = grad_second + dot(ws[:, width:].T, grad_two, NN)
    grad_one = jnp.where(first[:, :learn] > 0, grad_first, 0.0).astype(jnp.bfloat16)
    gp[:, :learn] = grad_one
    gp[:, learn:] = grad_two
    if roles is not None:
        for out in lead:
            out[:, width + units :] = ghead[: out.shape[0]].astype(jnp.bfloat16)
        order = role_rows(gp, roles[:1], lead[0].shape[0])
        gradient_rows(order, xs, first_bf, lead, learn, width)


def role_rows(gp, roles, rows):
    parts = [gp[piece_rows((rows, role, same)), :] for role in roles for same in (False, True)]
    return jnp.concatenate(parts, 0)


def gradient_rows(order, xs, first_bf, outs, learn, width):
    rows = outs[0].shape[0]

    def put(columns, value):
        value = value.astype(jnp.bfloat16)
        for i, out in enumerate(outs):
            out[:, columns] = value[i * rows : (i + 1) * rows]

    put(slice(0, width), dot(order[:, :learn], xs[:learn], NN))
    columns = slice(width, width + first_bf.shape[0])
    put(columns, dot(order[:, learn:], first_bf[:, :learn], NT))


def rest_kernel(cfg, xs, gp, first_bf, *outs):
    roles = cfg["roles"]
    order = gp[...] if roles is None else role_rows(gp, roles[1:], outs[0].shape[0])
    gradient_rows(order, xs, first_bf, outs, cfg["learn"], cfg["width"])


def learner(staged, piece_list, aux, head, before, cfg):
    total, width, units, learn = staged.shape[0], cfg["width"], cfg["units"], cfg["learn"]
    padded = head.shape[0]
    roles = cfg["roles"]
    block = lambda rows: jax.ShapeDtypeStruct((rows, width + units), jnp.bfloat16)
    inputs = 3 + len(piece_list)
    if roles is None:
        lead, rest, aliases = [jax.ShapeDtypeStruct((padded, units), jnp.float32)], [block(units)], {}
    else:
        rows = units // (len(roles) * CORES)
        wider = jax.ShapeDtypeStruct((rows, width + 2 * units), jnp.bfloat16)
        lead, rest = [wider] * CORES, [block(rows)] * (CORES * (len(roles) - 1))
        aliases = {inputs + i: i for i in range(len(before))}
    weights, _, first_bf, own, gp, *first_outs = pl.pallas_call(
        functools.partial(learner_kernel, cfg),
        out_shape=(
            block(units),
            jax.ShapeDtypeStruct((units, total), jnp.float32),
            jax.ShapeDtypeStruct((units, total), jnp.bfloat16),
            jax.ShapeDtypeStruct((cfg["heads"] - 1, 1, total - learn), jnp.float32),
            jax.ShapeDtypeStruct((units, 2 * learn), jnp.bfloat16),
            *lead,
        ),
        in_specs=[LOCAL] + [ANYWHERE if roles is None else LOCAL] * len(piece_list)
        + [LOCAL] * (2 + len(before)),
        out_specs=(LOCAL,) * (5 + len(lead)),
        input_output_aliases=aliases,
        compiler_params=pltpu.CompilerParams(vmem_limit_bytes=32 << 20),
        cost_estimate=pl.CostEstimate(
            flops=4 * units * total * width, bytes_accessed=4 * total * width, transcendentals=0
        ),
        name="learner",
    )(staged, *piece_list, aux, head, *before)
    rest_outs = pl.pallas_call(
        functools.partial(rest_kernel, cfg),
        out_shape=tuple(rest),
        in_specs=[LOCAL] * 3,
        out_specs=(LOCAL,) * len(rest),
        compiler_params=pltpu.CompilerParams(vmem_limit_bytes=32 << 20),
        cost_estimate=pl.CostEstimate(
            flops=2 * units * learn * width, bytes_accessed=2 * learn * width, transcendentals=0
        ),
        name="rest",
    )(staged, gp, first_bf)
    return weights, own, first_outs, list(rest_outs)


def opponent_kernel(count, *refs):
    frames, (weights, head), outs = refs[:count], refs[count : count + 2], refs[count + 2 :]
    envs, width = frames[0].shape
    rows = jnp.concatenate([f[...] for f in frames], 0)
    first = jnp.maximum(dot(weights[:, :width], rows, NT), 0.0)
    first_bf = first.astype(jnp.bfloat16)
    result = forward(first, first_bf, weights[...], head[...], width)[0].astype(jnp.bfloat16)
    for i, out in enumerate(outs):
        out[...] = result[:, i * envs : (i + 1) * envs]


def opponents(frames, weights, head, cfg):
    count, (envs, width) = len(frames), frames[0].shape
    return pl.pallas_call(
        functools.partial(opponent_kernel, count),
        out_shape=(jax.ShapeDtypeStruct((head.shape[0], envs), jnp.bfloat16),) * count,
        in_specs=[LOCAL] * (count + 2),
        out_specs=(LOCAL,) * count,
        compiler_params=pltpu.CompilerParams(vmem_limit_bytes=24 << 20),
        cost_estimate=pl.CostEstimate(
            flops=2 * cfg["units"] * count * envs * width,
            bytes_accessed=2 * count * envs * width,
            transcendentals=0,
        ),
        name="opponents",
    )(*frames, weights, head)


def other_agent(i, by, agents):
    return i ^ by if agents & (agents - 1) == 0 else (i + by) % agents


def choose_kernel(*refs):
    answers, ids, out = refs[:-2], refs[-2], refs[-1]
    agents, me = len(answers), lax.axis_index("agent")
    result = jnp.zeros(out.shape, jnp.float32)
    for by, answer in enumerate(answers):
        player = other_agent(me, by, agents)
        result = jnp.where(ids[...] == player, answer[: out.shape[0]].astype(jnp.float32), result)
    out[...] = result.astype(out.dtype)


def choose(answers, ids, count):
    return pl.pallas_call(
        choose_kernel,
        out_shape=jax.ShapeDtypeStruct((count, ids.shape[1]), jnp.bfloat16),
        in_specs=[LOCAL] * (len(answers) + 1),
        out_specs=LOCAL,
        compiler_params=pltpu.CompilerParams(vmem_limit_bytes=2 << 20),
        name="choose",
    )(*answers, ids)


def total_of(refs, columns, through=0):
    values = [x[:, columns].astype(jnp.float32) for x in refs]
    for i in range(len(values) - through, len(values)):
        values[i] = jnp.where(inner_chip(), values[i], 0.0)
    return sum(values)


def inner_chip():
    _, chip = where_am_i()
    return jnp.logical_and(chip > 0, chip < LINE - 1)


def small_kernel(body, out_shape, args):
    bytes_accessed = sum(x.size * x.dtype.itemsize for x in args)
    return pl.pallas_call(
        body,
        out_shape=out_shape,
        in_specs=[LOCAL] * len(args),
        out_specs=jax.tree.map(lambda _: LOCAL, out_shape),
        compiler_params=pltpu.CompilerParams(vmem_limit_bytes=4 << 20),
        cost_estimate=pl.CostEstimate(
            flops=bytes_accessed, bytes_accessed=bytes_accessed, transcendentals=0
        ),
    )(*args)


def add(*arrays, dtype=jnp.bfloat16):
    width = min(x.shape[1] for x in arrays)

    def body(*refs):
        refs[-1][...] = total_of(refs[:-1], slice(0, width)).astype(dtype)

    shape = jax.ShapeDtypeStruct((arrays[0].shape[0], width), dtype)
    return small_kernel(body, shape, arrays)


def join(mid, onward):
    def body(mid_ref, onward_ref, out):
        out[...] = jnp.where(inner_chip(), mid_ref[...], onward_ref[...])

    return small_kernel(body, jax.ShapeDtypeStruct(mid.shape, mid.dtype), (mid, onward))


def add_with_heads(arrays, heads, units, cut=None, through=()):
    arrays, heads = (*arrays, *through), (*heads, *through)
    rows, wide = heads[0].shape
    width = wide - units

    def body(*refs):
        ins, tops, outs = refs[: len(arrays)], refs[len(arrays) :][: len(heads)], refs[len(args) :]
        edges = [0, width] if cut is None else [0, cut, width]
        for out, start, stop in zip(outs, edges, edges[1:]):
            value = total_of(ins, slice(start, stop), len(through))
            out[:, : stop - start] = value.astype(out.dtype)
        tail = slice(width, wide)
        outs[0][:, edges[1] :] = total_of(tops, tail, len(through)).astype(outs[0].dtype)

    args = (*arrays, *heads)
    widths = [wide] if cut is None else [cut + units, width - cut]
    shape = [jax.ShapeDtypeStruct((rows, w), jnp.bfloat16) for w in widths]
    result = small_kernel(body, tuple(shape), args)
    return result[0] if cut is None else result


def adam_step(master, moment, second, grad, rate):
    moment = beta_first * moment + (1.0 - beta_first) * grad
    second = beta_second * second + (1.0 - beta_second) * grad * grad
    master = master - rate * moment / (jnp.sqrt(second) + adam_eps)
    return (master, moment, second)


def head_gradient(head_parts, count, units):
    if len(head_parts) == 1:
        return head_parts[0][:count]
    mine, mid, near, far = (x[:count, x.shape[1] - units :].astype(jnp.float32) for x in head_parts)
    _, chip = where_am_i()
    end = jnp.logical_or(chip == 0, chip == LINE - 1)
    rounded = lambda x: x.astype(jnp.bfloat16).astype(jnp.float32)
    pair = rounded(mine + jnp.where(end, near, far))
    return pair + jnp.where(end, far, rounded(mid + near))


def adam_kernel(parts, offsets, head_parts, prior, cuts, *refs):
    rate = refs[0][...]
    parts, refs = refs[1 : 1 + parts], refs[1 + parts :]
    head_parts, refs = refs[:head_parts], refs[head_parts:]
    heads = 3 if head_parts else 0
    core, head, refs = refs[:3], refs[3 : 3 + heads], refs[3 + heads + prior :]
    core_out, head_out, refs = refs[:3], refs[3 : 3 + heads], refs[3 + heads :]
    stages, head_stages, refs = refs[:3], refs[3 : 3 + heads], refs[3 + heads :]
    sems, copies = refs[0], []
    if heads:
        count, _, units = head[0].shape
        grad = head_gradient(head_parts, count, units).reshape(head[0].shape)
        for i, value in enumerate(adam_step(*(x[...] for x in head), grad, rate)):
            head_stages[i][...] = value
            copies.append(pltpu.make_async_copy(head_stages[i], head_out[i], refs[1].at[i]))
            copies[-1].start()
    for n, (start, stop) in enumerate(cuts):
        columns = slice(start, stop)
        grad = sum(
            part[:, start - offset : stop - offset].astype(jnp.float32)
            for part, offset in zip(parts, offsets)
        )
        for i, value in enumerate(adam_step(*(x[:, columns] for x in core), grad, rate)):
            stages[i][:, columns] = value
            copies.append(
                pltpu.make_async_copy(
                    stages[i].at[:, columns], core_out[i].at[:, columns], sems.at[n, i]
                )
            )
            copies[-1].start()
    for copy in copies:
        copy.wait()


def adam(rates, parts, head_parts, core, head, span, prior=()):
    rows, width = core[0].shape
    start, stop = span
    tiles = (stop - start) // 128
    pieces = max(1, tiles // 5)
    edges = [start + 128 * (tiles * n // pieces) for n in range(pieces)] + [stop]
    cuts = list(zip(edges, edges[1:]))
    arrays, offsets = [a for a, _ in parts], [o for _, o in parts]
    if not head_parts:
        head = ()
    one = jax.ShapeDtypeStruct((rows, width), jnp.float32)
    inputs = 1 + len(parts) + len(head_parts) + 3 + len(head)
    sems = [pltpu.SemaphoreType.DMA((len(cuts), 3))]
    if head:
        sems.append(pltpu.SemaphoreType.DMA((3,)))
    return pl.pallas_call(
        functools.partial(
            adam_kernel, len(parts), offsets, len(head_parts), len(prior), cuts
        ),
        out_shape=(one,) * 3 + tuple(jax.ShapeDtypeStruct(x.shape, jnp.float32) for x in head),
        in_specs=[LOCAL] * inputs + [ANYWHERE] * len(prior),
        out_specs=(ANYWHERE,) * (3 + len(head)),
        input_output_aliases={inputs + i: i for i in range(len(prior))},
        scratch_shapes=[pltpu.VMEM((rows, width), jnp.float32)] * 3
        + [pltpu.VMEM(x.shape, jnp.float32) for x in head]
        + sems,
        compiler_params=pltpu.CompilerParams(vmem_limit_bytes=12 << 20),
        cost_estimate=pl.CostEstimate(
            flops=20 * rows * (stop - start), bytes_accessed=32 * rows * (stop - start),
            transcendentals=0,
        ),
        name="adam",
    )(rates.reshape(1, 1), *arrays, *head_parts, *core, *head, *prior)


def per_device(
    learn_obs,
    own_obs,
    opp_obs,
    opponent,
    actions,
    done,
    rewards,
    behaviour,
    core_master,
    core_mom,
    core_vel,
    head_master,
    head_mom,
    head_vel,
    rates,
):
    envs, length, width = learn_obs.shape[1:]
    heads, units = head_master.shape[1:]
    action_count = heads - 1
    agents, members = lax.axis_size("agent"), lax.axis_size("dp")
    rows = core_master.shape[1]
    chips = members // CORES
    line = chips == LINE and members == LINE * CORES and units == members * rows and heads <= rows
    wide = jnp.float32

    def along(x, pairs):
        return lax.ppermute(
            x, "dp", [(a * CORES + c, b * CORES + c) for a, b in pairs for c in range(CORES)]
        )

    def sibling(x):
        return lax.ppermute(x, "dp", [(i, i ^ 1) for i in range(members)])

    def swap(x, by):
        return lax.ppermute(x, "agent", [(i, other_agent(i, by, agents)) for i in range(agents)])

    mine = core_master[0].astype(jnp.bfloat16)
    if line:
        far = along(mine, GATHER_FAR)
        near = along(mine, GATHER_NEAR)
        mid = along(mine, GATHER_MID)
        onward = along(far, GATHER_FORWARD)
        joined = join(mid, onward)
        got = [("mine", mine, SELF_FROM), ("far", far, FAR_FROM), ("near", near, NEAR_FROM),
               ("last", joined, LAST_FROM)]

        def with_siblings(group):
            arrays = [g[1] for g in group] + [sibling(g[1]) for g in group]
            return arrays, [(rows, g[2], same) for same in (True, False) for g in group]

        first_list, first_pieces = with_siblings(got[:-1])
        piece_list, pieces = with_siblings(got[-1:])
        roles = ROLES
    else:
        piece_list = [lax.all_gather(mine, "dp", axis=0, tiled=True)]
        pieces = [(units, None, True)]
        roles = None

    frames = [opp_obs[0]] + [swap(opp_obs[0], by) for by in range(1, agents)]

    by_row = lambda x: jnp.transpose(x, (1, 0, 2))
    cfg = dict(pieces=pieces, heads=heads, width=width, units=units, length=length, roles=roles,
               learn=envs * length)
    staged, aux, head = stage(
        learn_obs[0].reshape(envs * length, width),
        own_obs[0],
        [x[0].T for x in (actions, done, rewards, behaviour)],
        by_row(head_master),
    )
    before = ()
    if line:
        before = early(staged, first_pieces, first_list, units)
    weights, own, lead, rest = learner(staged, piece_list, aux, head, before, cfg)
    played = opponents(frames, weights, head, cfg)
    own_logits = jnp.transpose(own, (1, 2, 0))

    def undo(by):
        there = other_agent(0, by, agents)
        return next(b for b in range(agents) if other_agent(there, b, agents) == 0)

    answers = [played[0]] + [swap(played[by], undo(by)) for by in range(1, agents)]
    opp_logits = choose(answers, opponent[0].T, action_count)

    if line:
        blocks = lead + rest
        send, keep = blocks[::CORES], blocks[1::CORES]
        came = [sibling(b) for b in send]
        last = add_with_heads((keep[0], came[0]), (keep[0], came[0]), units)
        through = along(last, SCATTER_FORWARD)
        part_mid = along(last, SCATTER_MID)
        toward = add_with_heads((keep[1], came[1]), (last,), units)
        part_near = along(toward, SCATTER_NEAR)
        cut = 128 * (5 * (width + units) // (8 * 128))
        beyond = add_with_heads((keep[2], came[2]), (last,), units, cut, (through,))
        part_far = [along(b, SCATTER_FAR) for b in beyond]
        known = add(keep[3], came[3], part_near, part_mid, dtype=wide)
        spans = ((0, cut), (cut, width + units))
        parts = [((known, 0), (far, at)) for far, (at, _) in zip(part_far, spans)]
        head_parts = (last, part_mid, part_near, part_far[0])
    else:
        spans = ((0, width + units),)
        total = lax.psum_scatter(rest[0], "dp", scatter_dimension=0, tiled=True)
        parts, head_parts = [((total, 0),)], (lax.psum(lead[0], "dp"),)
    core = (core_master[0], core_mom[0], core_vel[0])
    head = (by_row(head_master), by_row(head_mom), by_row(head_vel))
    new = ()
    for n, (span, part) in enumerate(zip(spans, parts)):
        done = adam(rates, part, () if n else head_parts, core, head, span, new[:3])
        new = (*done[:3], *(new[3:] or done[3:]))
    return (own_logits, opp_logits.T[None], *[x[None] for x in new[:3]], *map(by_row, new[3:]))


def solution(mesh):
    sharded, whole = P("agent", "dp", None), P("agent", None, None)

    return jax.shard_map(
        per_device,
        mesh=mesh,
        in_specs=(P("agent", "dp", None, None),) + (sharded,) * 10 + (whole,) * 3 + (P("agent"),),
        out_specs=(sharded,) * 5 + (whole,) * 3,
        check_vma=False,
    )
```
